32 devices in a mesh: seq: 16 (over z, y, x), feat: 2 (over core).
Axes of the slice: x: 2, y: 2, z: 4, core: 2. Of those that a mesh axis runs over, the one named last changes fastest.
Arguments:
- tokens: bfloat16 [131072, 1280], P(('seq', 'feat')), may hold values from -12 to 12
- shot_starts: int32 [32], replicated, may hold values from 0 to 128512, as said below
- seed_offsets: int32 [32, 64], replicated, may hold values from 0 to 1023, as said below
- norm_gain: float32 [1280], replicated, may hold values from 0.5 to 1.5
- proj_weight: bfloat16 [1280, 8192], P(None, 'feat'), may hold values from -0.15625 to 0.15625
Outputs:
- projected: bfloat16 [2048, 8192], P('seq', 'feat')
The draws below stay inside these ranges and needn't reach their ends.
Inputs may be any that keep to these rules, and one draw needn't show every extreme that they name: shot_starts[0] = 0, the starts rise, and shot s starts within 1536 tokens of s * 4096, so a shot has 1024 to 7168 tokens. `seed_offsets`: each row holds 64 different offsets, all below 1024.
All inputs are finite; a program needn't handle non-finite values.
Results may differ from the reference program's by a relative error of at most 0.0055.
Values may be sent and summed in bfloat16 or wider, within the bound.
No kernel may reach another device: no remote copies, remote signals or barrier semaphores. Data moves between devices by JAX's collectives and lax.ppermute only.
A program may use at most 128 MiB of HBM per device.

```python
import math
import jax
import jax.numpy as jnp
from jax import lax

D = 1280
P_SIZE = 8192
K = 64
ITERS = 3
TOK_DEV = 4096
HALF = 1536
MINLEN = 1024
LMAX = 7168
SHOTS = 32
TOKENS = 131072


def shot_layout(key):
    folded = jax.random.fold_in(key, 17)
    key_offset, key_pick, key_seed = jax.random.split(folded, 3)
    offsets = jax.random.randint(key_offset, (SHOTS,), -HALF, HALF + 1)
    chosen = jax.random.randint(key_pick, (), 1, SHOTS - 2)
    shot_index = jnp.arange(SHOTS)
    offsets = jnp.where(shot_index == chosen, HALF, offsets)
    offsets = jnp.where(shot_index == chosen + 1, -HALF, offsets)
    offsets = jnp.where(shot_index == chosen + 2, HALF, offsets)
    offsets = jnp.where(shot_index == 0, 0, offsets)
    shot_starts = (shot_index * TOK_DEV + offsets).astype(jnp.int32)
    seed_keys = jax.random.split(key_seed, SHOTS)
    seed_offsets = jax.vmap(lambda subkey: jax.random.permutation(subkey, MINLEN)[:K])(seed_keys)
    return (shot_starts, seed_offsets.astype(jnp.int32))


def draw_shot_starts(key, part):
    return shot_layout(key)[0]


def draw_seed_offsets(key, part):
    return shot_layout(key)[1]


def draw_tokens(key, part):
    shot_starts, seed_offsets = shot_layout(key)
    key_center, key_count, key_member, key_value = jax.random.split(jax.random.fold_in(key, 29), 4)
    position = jnp.arange(TOKENS, dtype=jnp.int32)
    shot_of = (jnp.searchsorted(shot_starts, position, side='right') - 1).astype(jnp.int32)
    cluster_counts = jax.random.randint(key_count, (SHOTS,), K // 2, 2 * K + 1)
    member_raw = jax.random.randint(key_member, (TOKENS,), 0, 1 << 20)
    member = member_raw % jnp.take(cluster_counts, shot_of)
    cluster_id = (shot_of * (2 * K) + member).astype(jnp.int32)
    centres = 0.6 * jnp.clip(jax.random.normal(key_center, (SHOTS * 2 * K, D), jnp.float32), -4.0, 4.0)
    noise = 0.5 * jnp.clip(jax.random.normal(key_value, (TOKENS, D), jnp.float32), -4.0, 4.0)
    values = jnp.take(centres, cluster_id, axis=0) + noise
    return jnp.clip(values, -12.0, 12.0).astype(jnp.bfloat16)


def level_of(stream_key, dims, cuts, smallest, high):
    loudness = 1.0
    for axis_at, shards_of in cuts:
        draws = jax.random.uniform(jax.random.fold_in(jax.random.fold_in(stream_key, 6), axis_at), (shards_of,), jnp.float32, smallest / len(cuts), high / len(cuts))
        loudness = loudness * jnp.repeat(jnp.exp(draws), dims[axis_at] // shards_of).reshape((-1,) + (1,) * (len(dims) - 1 - axis_at))
    return loudness


def bell_draw(stream_key, dims, width, limit, pieces=(), held_as=jnp.bfloat16):
    loudness = level_of(stream_key, dims, pieces, -0.22, 0.18) if pieces else 1.0
    array = jax.random.normal(stream_key, dims, jnp.float32) * width * loudness
    return jnp.minimum(jnp.maximum(array, -limit), limit).astype(held_as)


def setup_inputs(seed: int = 0) -> dict:
    keys = jax.random.split(jax.random.key(seed), 6)
    tokens = draw_tokens(jax.random.fold_in(keys[5], 71), 0)
    shot_starts = draw_shot_starts(jax.random.fold_in(keys[5], 71), 0)
    seed_offsets = draw_seed_offsets(jax.random.fold_in(keys[5], 71), 0)
    norm_gain = jnp.clip(1.0 + 0.1 * jax.random.normal(keys[3], (D,), jnp.float32), 0.5, 1.5)
    proj_weight = bell_draw(keys[4], (D, P_SIZE), D ** -0.5, 0.15625, ((1, 2),))
    return dict(tokens=tokens, shot_starts=shot_starts, seed_offsets=seed_offsets, norm_gain=norm_gain, proj_weight=proj_weight)


def shot_centroids(tokens, norm_gain, shot_begin, shot_finish, seed_row):
    token_total = tokens.shape[0]
    window_start = jnp.minimum(shot_begin, token_total - LMAX).astype(jnp.int32)
    window = lax.dynamic_slice_in_dim(tokens, window_start, LMAX, 0)
    position = window_start + jnp.arange(LMAX, dtype=jnp.int32)
    inside = (position >= shot_begin) & (position < shot_finish)
    seed_rows = (shot_begin + seed_row).astype(jnp.int32)
    centroid = jnp.take(tokens, seed_rows, axis=0).astype(jnp.float32)
    factor = 1.0 / math.sqrt(D)
    for iteration in range(ITERS):
        scores = jnp.dot(window, centroid.astype(jnp.bfloat16).T, preferred_element_type=jnp.float32) * factor
        weights = jax.nn.softmax(scores, axis=-1)
        weights = jnp.where(inside[:, None], weights, jnp.zeros_like(weights))
        shot_mass = lax.optimization_barrier(jnp.sum(weights, axis=0))
        shot_sums = lax.dot_general(weights.astype(jnp.bfloat16), window, (((0,), (0,)), ((), ())), preferred_element_type=jnp.float32)
        centroid = shot_sums / shot_mass[:, None]
    spread = jnp.sqrt(lax.optimization_barrier(jnp.mean(centroid * centroid, axis=-1, keepdims=True)) + 1e-06)
    return (centroid / spread * norm_gain).astype(jnp.bfloat16)

def reference(tokens, shot_starts, seed_offsets, norm_gain, proj_weight):
    token_total = tokens.shape[0]
    shot_ends = jnp.concatenate([shot_starts[1:], jnp.full((1,), token_total, jnp.int32)])
    normed = lax.map(lambda shot_item: shot_centroids(tokens, norm_gain, shot_item[0], shot_item[1], shot_item[2]), (shot_starts, shot_ends, seed_offsets))
    flat_rows = normed.reshape(SHOTS * K, D)
    return jnp.dot(flat_rows, proj_weight, preferred_element_type=jnp.float32).astype(jnp.bfloat16)
```

```python
import functools
import math

import jax
import jax.numpy as jnp
from jax import lax
from jax.experimental import pallas as pl
from jax.experimental.pallas import tpu as pltpu
from jax.sharding import PartitionSpec as P

ITERS = 3
AXES = ("seq", "feat")
LANES = 128
TILE = 512
F32 = jnp.float32
BF16 = jnp.bfloat16
VMEM_SPEC = pl.BlockSpec(memory_space=pltpu.VMEM)
HBM_SPEC = pl.BlockSpec(memory_space=pltpu.HBM)
SMEM_SPEC = pl.BlockSpec(memory_space=pltpu.SMEM)


def start_of(starts_ref, shot, shots, total):
    first = starts_ref[jnp.minimum(shot, shots - 1)]
    return jnp.where(shot >= shots, total, first)


def placement(place_ref, starts_ref, rows):
    shots = starts_ref.shape[0]
    total = shots * rows
    index = place_ref[0]
    second = index % 2 == 1
    here = start_of(starts_ref, index, shots, total)
    after = start_of(starts_ref, index + 1, shots, total)
    base = index * rows
    low = jnp.where(second, here, base)
    high = jnp.where(second, base + rows, after)
    cut = jnp.where(second, after, here)
    split = jnp.where(second, after < base + rows, here > base)
    x_low = jnp.where(split & second, cut, low)
    x_high = jnp.where(split & ~second, cut, high)
    y_low = jnp.where(split, jnp.where(second, low, cut), high)
    y_high = jnp.where(split, jnp.where(second, cut, high), high)
    return index, second, base, split, (x_low, x_high), (y_low, y_high)


def column_of(row):
    n = row.shape[1]
    diagonal = lax.broadcasted_iota(jnp.int32, (n, n), 0) == lax.broadcasted_iota(
        jnp.int32, (n, n), 1
    )
    spread = jnp.where(diagonal, jnp.broadcast_to(row, (n, n)), 0)
    return jnp.sum(spread, axis=1, keepdims=True)


def seed_kernel(
    reach,
    place_ref,
    starts_ref,
    seeds_ref,
    seed_rows_ref,
    tokens_ref,
    first_ref,
    own_ref,
    give_ref,
    edge_ref,
    picked,
    strip,
    pick_sem,
    in_sems,
    out_sem,
):
    rows = tokens_ref.shape[0]
    shots, count = seeds_ref.shape
    total = shots * rows
    index = place_ref[0]
    second = index % 2 == 1
    base = index * rows
    pieces = in_sems.shape[0]
    piece = reach // pieces
    strip_low = jnp.where(second, 0, rows - reach)
    following = jnp.minimum(index + 1, shots - 1)
    here = start_of(starts_ref, index, shots, total)
    after = start_of(starts_ref, index + 1, shots, total)
    later = start_of(starts_ref, index + 2, shots, total)

    def fetch(k, carry):
        for which, (shot, begin) in enumerate(((index, here), (following, after))):
            place = jnp.clip(begin + seeds_ref[shot, k] - base, 0, rows - 1)
            group = pl.multiple_of((place // 8) * 8, 8)
            slot = pl.multiple_of((which * count + k) * 8, 8)
            pltpu.make_async_copy(
                tokens_ref.at[pl.ds(group, 8), :], picked.at[pl.ds(slot, 8), :], pick_sem
            ).start()
        return carry

    lax.fori_loop(0, count, fetch, 0, unroll=4)
    loads = []
    for i in range(pieces):
        source = pl.multiple_of(strip_low + i * piece, 8)
        loads.append(
            pltpu.make_async_copy(
                tokens_ref.at[pl.ds(source, piece), :],
                strip.at[pl.ds(i * piece, piece), :],
                in_sems.at[i],
            )
        )
        loads[-1].start()
    pltpu.make_async_copy(tokens_ref.at[pl.ds(0, 16 * count), :], picked, pick_sem).wait()

    found = []
    for which, (shot, begin) in enumerate(((index, here), (following, after))):
        offsets = seed_rows_ref[pl.ds(shot, 1), :]
        place = column_of(offsets) + (begin - base)
        valid = (place >= 0) & (place < rows)
        target = lax.broadcasted_iota(jnp.int32, (count, 1), 0) * 8 + place % 8
        lane = lax.broadcasted_iota(jnp.int32, (count, 8 * count), 1)
        choose = jnp.where(valid & (lane == target), 1.0, 0.0).astype(BF16)
        block = picked[pl.ds(which * 8 * count, 8 * count), :]
        found.append(jnp.dot(choose, block, preferred_element_type=F32))
    own, tail = found
    ahead = jnp.where(second, after < base + rows, here > base)
    first = jnp.where(ahead, jnp.where(second, tail, 0.0), own)
    first_ref[...] = first.astype(BF16)
    own_ref[...] = own.astype(BF16)
    shared = later >= base + 2 * rows
    give_ref[pl.ds(0, count), :] = jnp.where(shared, tail, 0.0).astype(BF16)
    give_ref[pl.ds(count, count), :] = tail.astype(BF16)

    for i in range(pieces):
        loads[i].wait()
        pltpu.make_async_copy(
            strip.at[pl.ds(i * piece, piece), :],
            edge_ref.at[pl.ds(i * piece, piece), :],
            out_sem,
        ).start()
    pltpu.make_async_copy(strip, edge_ref, out_sem).wait()


def total_mass(block):
    return jnp.sum(block.astype(F32), axis=1, keepdims=True)


def pool_kernel(
    first,
    reach,
    place_ref,
    starts_ref,
    tokens_ref,
    edge_ref,
    x_ref,
    recv_ref,
    mass_ref,
    y_ref,
    send_out,
    x_out,
    mass_out,
    y_out,
    centroids,
    sums,
    masses,
):
    rows, width = tokens_ref.shape
    count = y_ref.shape[0]
    index, second, base, _, x_range, y_range = placement(place_ref, starts_ref, rows)
    edge_base = jnp.where(second, base - reach, base + rows)
    scale = math.log2(math.e) / math.sqrt(width)

    if first:
        centroids[pl.ds(0, count), :] = x_ref[...] + recv_ref[...]
        centroids[pl.ds(count, count), :] = y_ref[...]
    else:
        mass = mass_ref[:, :1] + total_mass(recv_ref[:, width:])
        joined = x_ref[...] + recv_ref[:, :width].astype(F32)
        centroids[pl.ds(0, count), :] = (joined / mass).astype(BF16)
        centroids[pl.ds(count, count), :] = y_ref[...].astype(BF16)
    sums[...] = jnp.zeros_like(sums)
    masses[...] = jnp.zeros_like(masses)

    tiles = [(tokens_ref, i * TILE, base + i * TILE) for i in range(rows // TILE)]
    tiles += [(edge_ref, i * TILE, edge_base + i * TILE) for i in range(reach // TILE)]

    def scores_of(tile):
        ref, row, _ = tile
        return lax.dot_general(
            centroids[...],
            ref[pl.ds(row, TILE), :],
            (((1,), (1,)), ((), ())),
            preferred_element_type=F32,
        )

    def weights_of(tile, scores):
        place = tile[2] + lax.broadcasted_iota(jnp.int32, (1, TILE), 1)
        in_x = (place >= x_range[0]) & (place < x_range[1])
        in_y = (place >= y_range[0]) & (place < y_range[1])
        mine = jnp.where(in_y, scores[count:], scores[:count])
        top = jnp.max(mine, axis=0, keepdims=True)
        powers = jnp.exp2((mine - top) * scale)
        inverse = 1.0 / jnp.sum(powers, axis=0, keepdims=True)
        weights = jnp.concatenate(
            [powers * jnp.where(in_x, inverse, 0.0), powers * jnp.where(in_y, inverse, 0.0)], axis=0
        )
        part = weights[:, :LANES]
        for i in range(1, TILE // LANES):
            part = part + weights[:, i * LANES : (i + 1) * LANES]
        masses[...] += part
        return weights.astype(BF16)

    scores = scores_of(tiles[0])
    for at, tile in enumerate(tiles):
        upcoming = scores_of(tiles[at + 1]) if at + 1 < len(tiles) else None
        weights = weights_of(tile, scores)
        sums[...] += jnp.dot(
            weights, tile[0][pl.ds(tile[1], TILE), :], preferred_element_type=F32
        )
        scores = upcoming

    mass = jnp.sum(masses[...], axis=1, keepdims=True)
    x_mass = mass[:count]
    x_sums = sums[pl.ds(0, count), :]
    x_out[...] = x_sums
    mass_out[...] = jnp.broadcast_to(x_mass, mass_out.shape)
    y_out[...] = sums[pl.ds(count, count), :] / mass[count:]
    send_out[:, :width] = x_sums.astype(BF16)
    high = x_mass.astype(BF16).astype(F32)
    middle = (x_mass - high).astype(BF16).astype(F32)
    low = x_mass - high - middle
    lane = lax.broadcasted_iota(jnp.int32, (count, LANES), 1)
    block = jnp.where(
        lane == 0, high, jnp.where(lane == 1, middle, jnp.where(lane == 2, low, 0.0))
    )
    send_out[:, width:] = block.astype(BF16)


def norm_kernel(
    rows, place_ref, starts_ref, x_ref, recv_ref, mass_ref, y_ref, gain_ref, out_ref
):
    width = x_ref.shape[1]
    split = placement(place_ref, starts_ref, rows)[3]
    mass = mass_ref[:, :1] + total_mass(recv_ref[:, width:])
    joined = (x_ref[...] + recv_ref[:, :width].astype(F32)) / mass
    centroid = jnp.where(split, y_ref[...], joined)
    spread = jnp.sqrt(jnp.mean(centroid * centroid, axis=-1, keepdims=True) + 1e-06)
    out_ref[...] = (centroid / spread * gain_ref[...]).astype(BF16)


def on_device(tokens, shot_starts, seed_offsets, norm_gain, proj_weight):
    rows, width = tokens.shape
    count = seed_offsets.shape[1]
    reach = 3 * rows // 8
    devices = lax.axis_size(AXES)
    place = lax.axis_index(AXES).astype(jnp.int32).reshape(1)
    across = [(i, i + 1) for i in range(1, devices - 1, 2)]
    across += [(target, source) for source, target in across]

    def shape(*dims, dtype=BF16):
        return jax.ShapeDtypeStruct(dims, dtype)

    first, own, give, edge = pl.pallas_call(
        functools.partial(seed_kernel, reach),
        out_shape=(
            shape(count, width),
            shape(count, width),
            shape(2 * count, width),
            shape(reach, width),
        ),
        in_specs=[SMEM_SPEC, SMEM_SPEC, SMEM_SPEC, VMEM_SPEC, HBM_SPEC],
        out_specs=[VMEM_SPEC, VMEM_SPEC, VMEM_SPEC, HBM_SPEC],
        scratch_shapes=[
            pltpu.VMEM((16 * count, width), BF16),
            pltpu.VMEM((reach, width), BF16),
            pltpu.SemaphoreType.DMA(()),
            pltpu.SemaphoreType.DMA((3,)),
            pltpu.SemaphoreType.DMA(()),
        ],
        compiler_params=pltpu.CompilerParams(vmem_limit_bytes=16 << 20),
        name="seeds",
    )(place, shot_starts, seed_offsets, seed_offsets, pltpu.with_memory_space_constraint(tokens, pltpu.HBM))
    given = lax.ppermute(give, "feat", [(0, 1)])
    edge = lax.ppermute(edge, "feat", [(0, 1), (1, 0)])
    x = first + given[:count]
    y = own + given[count:]
    received = lax.ppermute(x, AXES, across)
    mass = jnp.zeros((count, LANES), F32)
    for iteration in range(ITERS):
        send, x, mass, y = pl.pallas_call(
            functools.partial(pool_kernel, iteration == 0, reach),
            out_shape=(
                shape(count, width + LANES),
                shape(count, width, dtype=F32),
                shape(count, LANES, dtype=F32),
                shape(count, width, dtype=F32),
            ),
            in_specs=[SMEM_SPEC] * 2 + [VMEM_SPEC] * 6,
            out_specs=[VMEM_SPEC] * 4,
            scratch_shapes=[
                pltpu.VMEM((2 * count, width), BF16),
                pltpu.VMEM((2 * count, width), F32),
                pltpu.VMEM((2 * count, LANES), F32),
            ],
            compiler_params=pltpu.CompilerParams(vmem_limit_bytes=16 << 20),
            name="pool",
        )(place, shot_starts, tokens, edge, x, received, mass, y)
        received = lax.ppermute(send, AXES, across)
    normed = pl.pallas_call(
        functools.partial(norm_kernel, rows),
        out_shape=shape(count, width),
        in_specs=[SMEM_SPEC] * 2 + [VMEM_SPEC] * 5,
        out_specs=VMEM_SPEC,
        compiler_params=pltpu.CompilerParams(vmem_limit_bytes=8 << 20),
        name="norm",
    )(place, shot_starts, x, received, mass, y, norm_gain[None, :])
    projected = jnp.dot(
        lax.all_gather(normed, "feat", axis=0, tiled=True),
        proj_weight,
        preferred_element_type=F32,
    )
    return projected.astype(BF16)


def solution(mesh):
    in_specs = (P(AXES, None), P(), P(), P(), P(None, "feat"))
    out_specs = P("seq", "feat")
    return jax.shard_map(
        on_device, mesh=mesh, in_specs=in_specs, out_specs=out_specs, check_vma=False
    )
```

```python
import functools
import math

import jax
import jax.numpy as jnp
from jax import lax
from jax.experimental import pallas as pl
from jax.experimental.pallas import tpu as pltpu
from jax.sharding import PartitionSpec as P

ITERS = 3
AXES = ("seq", "feat")
LANES = 128
TILE = 512
F32 = jnp.float32
BF16 = jnp.bfloat16
VMEM_SPEC = pl.BlockSpec(memory_space=pltpu.VMEM)
HBM_SPEC = pl.BlockSpec(memory_space=pltpu.HBM)
SMEM_SPEC = pl.BlockSpec(memory_space=pltpu.SMEM)


def start_of(starts_ref, shot, shots, total):
    first = starts_ref[jnp.minimum(shot, shots - 1)]
    return jnp.where(shot >= shots, total, first)


def placement(index, starts_ref, rows):
    shots = starts_ref.shape[0]
    total = shots * rows
    second = index % 2 == 1
    here = start_of(starts_ref, index, shots, total)
    after = start_of(starts_ref, index + 1, shots, total)
    base = index * rows
    low = jnp.where(second, here, base)
    high = jnp.where(second, base + rows, after)
    cut = jnp.where(second, after, here)
    split = jnp.where(second, after < base + rows, here > base)
    x_low = jnp.where(split & second, cut, low)
    x_high = jnp.where(split & ~second, cut, high)
    y_low = jnp.where(split, jnp.where(second, low, cut), high)
    y_high = jnp.where(split, jnp.where(second, cut, high), high)
    return split, x_low, x_high, y_low, y_high


def column_of(row):
    n = row.shape[1]
    diagonal = lax.broadcasted_iota(jnp.int32, (n, n), 0) == lax.broadcasted_iota(
        jnp.int32, (n, n), 1
    )
    spread = jnp.where(diagonal, jnp.broadcast_to(row, (n, n)), 0)
    return jnp.sum(spread, axis=1, keepdims=True)


def seed_kernel(
    place_ref,
    starts_hbm,
    seeds_hbm,
    tokens_ref,
    first_ref,
    own_ref,
    give_ref,
    edge_ref,
    meta_ref,
    starts_ref,
    seeds_ref,
    seed_rows_ref,
    picked,
    index_sems,
    pick_sem,
    edge_sem,
):
    rows = tokens_ref.shape[0]
    reach = edge_ref.shape[0]
    shots, count = seeds_ref.shape
    total = shots * rows
    index = place_ref[0]
    second = index % 2 == 1
    base = index * rows
    indices = [
        pltpu.make_async_copy(starts_hbm, starts_ref, index_sems.at[0]),
        pltpu.make_async_copy(seeds_hbm, seeds_ref, index_sems.at[1]),
        pltpu.make_async_copy(seeds_hbm, seed_rows_ref, index_sems.at[2]),
    ]
    for copy in indices:
        copy.start()
    strip_low = pl.multiple_of(jnp.where(second, 0, rows - reach), 8)
    strip = pltpu.make_async_copy(tokens_ref.at[pl.ds(strip_low, reach), :], edge_ref, edge_sem)
    strip.start()
    for copy in indices:
        copy.wait()
    following = jnp.minimum(index + 1, shots - 1)
    here = start_of(starts_ref, index, shots, total)
    after = start_of(starts_ref, index + 1, shots, total)
    later = start_of(starts_ref, index + 2, shots, total)

    def fetch(k, carry):
        for which, (shot, begin) in enumerate(((index, here), (following, after))):
            place = jnp.clip(begin + seeds_ref[shot, k] - base, 0, rows - 1)
            group = pl.multiple_of((place // 8) * 8, 8)
            slot = pl.multiple_of((which * count + k) * 8, 8)
            pltpu.make_async_copy(
                tokens_ref.at[pl.ds(group, 8), :], picked.at[pl.ds(slot, 8), :], pick_sem
            ).start()
        return carry

    lax.fori_loop(0, count, fetch, 0, unroll=8)
    for at, value in enumerate(placement(index, starts_ref, rows)):
        meta_ref[at] = value.astype(jnp.int32)
    choices = []
    for shot, begin in ((index, here), (following, after)):
        place = column_of(seed_rows_ref[pl.ds(shot, 1), :]) + (begin - base)
        valid = (place >= 0) & (place < rows)
        target = lax.broadcasted_iota(jnp.int32, (count, 1), 0) * 8 + place % 8
        lane = lax.broadcasted_iota(jnp.int32, (count, 8 * count), 1)
        choices.append(jnp.where(valid & (lane == target), 1.0, 0.0).astype(BF16))
    pltpu.make_async_copy(tokens_ref.at[pl.ds(0, 16 * count), :], picked, pick_sem).wait()
    own, tail = (
        jnp.dot(
            choose,
            picked[pl.ds(which * 8 * count, 8 * count), :],
            preferred_element_type=F32,
        )
        for which, choose in enumerate(choices)
    )
    ahead = jnp.where(second, after < base + rows, here > base)
    first = jnp.where(ahead, jnp.where(second, tail, 0.0), own)
    first_ref[...] = first.astype(BF16)
    own_ref[...] = own.astype(BF16)
    shared = later >= base + 2 * rows
    give_ref[pl.ds(0, count), :] = jnp.where(shared, tail, 0.0).astype(BF16)
    give_ref[pl.ds(count, count), :] = tail.astype(BF16)
    strip.wait()


def load_kernel(tokens_ref, after_ref, out_ref, sems):
    pieces = sems.shape[0]
    piece = tokens_ref.shape[0] // pieces
    copies = [
        pltpu.make_async_copy(
            tokens_ref.at[pl.ds(i * piece, piece), :],
            out_ref.at[pl.ds(i * piece, piece), :],
            sems.at[i],
        )
        for i in range(pieces)
    ]
    for copy in copies:
        copy.start()
    for copy in copies:
        copy.wait()


def total_mass(block):
    return jnp.sum(block.astype(F32), axis=1, keepdims=True)


def pool_kernel(
    first,
    place_ref,
    meta_ref,
    tokens_ref,
    edge_ref,
    x_ref,
    recv_ref,
    mass_ref,
    y_ref,
    send_out,
    x_out,
    mass_out,
    y_out,
    centroids,
    sums,
    masses,
):
    rows, width = tokens_ref.shape
    count = y_ref.shape[0]
    reach = edge_ref.shape[0]
    index = place_ref[0]
    base = index * rows
    edge_base = jnp.where(index % 2 == 1, base - reach, base + rows)
    x_range = (meta_ref[1], meta_ref[2])
    y_range = (meta_ref[3], meta_ref[4])
    scale = math.log2(math.e) / math.sqrt(width)

    if first:
        centroids[pl.ds(0, count), :] = x_ref[...] + recv_ref[...]
        centroids[pl.ds(count, count), :] = y_ref[...]
    else:
        mass = mass_ref[:, :1] + total_mass(recv_ref[:, width:])
        joined = x_ref[...] + recv_ref[:, :width].astype(F32)
        centroids[pl.ds(0, count), :] = (joined / mass).astype(BF16)
        centroids[pl.ds(count, count), :] = y_ref[...].astype(BF16)
    sums[...] = jnp.zeros_like(sums)
    masses[...] = jnp.zeros_like(masses)

    tiles = [(tokens_ref, i * TILE, base + i * TILE) for i in range(rows // TILE)]
    tiles += [(edge_ref, i * TILE, edge_base + i * TILE) for i in range(reach // TILE)]

    def scores_of(tile):
        ref, row, _ = tile
        return lax.dot_general(
            centroids[...],
            ref[pl.ds(row, TILE), :],
            (((1,), (1,)), ((), ())),
            preferred_element_type=F32,
        )

    def weights_of(tile, scores):
        place = tile[2] + lax.broadcasted_iota(jnp.int32, (1, TILE), 1)
        in_x = (place >= x_range[0]) & (place < x_range[1])
        in_y = (place >= y_range[0]) & (place < y_range[1])
        mine = jnp.where(in_y, scores[count:], scores[:count])
        top = jnp.max(mine, axis=0, keepdims=True)
        powers = jnp.exp2((mine - top) * scale)
        inverse = 1.0 / jnp.sum(powers, axis=0, keepdims=True)
        weights = jnp.concatenate(
            [powers * jnp.where(in_x, inverse, 0.0), powers * jnp.where(in_y, inverse, 0.0)], axis=0
        )
        part = weights[:, :LANES]
        for i in range(1, TILE // LANES):
            part = part + weights[:, i * LANES : (i + 1) * LANES]
        masses[...] += part
        return weights.astype(BF16)

    scores = scores_of(tiles[0])
    for at, tile in enumerate(tiles):
        upcoming = scores_of(tiles[at + 1]) if at + 1 < len(tiles) else None
        weights = weights_of(tile, scores)
        sums[...] += jnp.dot(
            weights, tile[0][pl.ds(tile[1], TILE), :], preferred_element_type=F32
        )
        scores = upcoming

    mass = jnp.sum(masses[...], axis=1, keepdims=True)
    x_mass = mass[:count]
    x_sums = sums[pl.ds(0, count), :]
    x_out[...] = x_sums
    mass_out[...] = jnp.broadcast_to(x_mass, mass_out.shape)
    y_out[...] = sums[pl.ds(count, count), :] / mass[count:]
    send_out[:, :width] = x_sums.astype(BF16)
    high = x_mass.astype(BF16).astype(F32)
    middle = (x_mass - high).astype(BF16).astype(F32)
    low = x_mass - high - middle
    lane = lax.broadcasted_iota(jnp.int32, (count, LANES), 1)
    block = jnp.where(
        lane == 0, high, jnp.where(lane == 1, middle, jnp.where(lane == 2, low, 0.0))
    )
    send_out[:, width:] = block.astype(BF16)


def norm_kernel(meta_ref, x_ref, recv_ref, mass_ref, y_ref, gain_ref, out_ref):
    width = x_ref.shape[1]
    split = meta_ref[0] != 0
    mass = mass_ref[:, :1] + total_mass(recv_ref[:, width:])
    joined = (x_ref[...] + recv_ref[:, :width].astype(F32)) / mass
    centroid = jnp.where(split, y_ref[...], joined)
    spread = jnp.sqrt(jnp.mean(centroid * centroid, axis=-1, keepdims=True) + 1e-06)
    out_ref[...] = (centroid / spread * gain_ref[...]).astype(BF16)


def on_device(tokens, shot_starts, seed_offsets, norm_gain, proj_weight):
    rows, width = tokens.shape
    count = seed_offsets.shape[1]
    reach = 3 * rows // 8
    devices = lax.axis_size(AXES)
    place = lax.axis_index(AXES).astype(jnp.int32).reshape(1)
    across = [(i, i + 1) for i in range(1, devices - 1, 2)]
    across += [(target, source) for source, target in across]

    def shape(*dims, dtype=BF16):
        return jax.ShapeDtypeStruct(dims, dtype)

    far_tokens = pltpu.with_memory_space_constraint(tokens, pltpu.HBM)
    first, own, give, edge, meta = pl.pallas_call(
        seed_kernel,
        out_shape=(
            shape(count, width),
            shape(count, width),
            shape(2 * count, width),
            shape(reach, width),
            shape(8, dtype=jnp.int32),
        ),
        in_specs=[SMEM_SPEC, HBM_SPEC, HBM_SPEC, HBM_SPEC],
        out_specs=[VMEM_SPEC, VMEM_SPEC, VMEM_SPEC, VMEM_SPEC, SMEM_SPEC],
        scratch_shapes=[
            pltpu.SMEM(shot_starts.shape, jnp.int32),
            pltpu.SMEM(seed_offsets.shape, jnp.int32),
            pltpu.VMEM(seed_offsets.shape, jnp.int32),
            pltpu.VMEM((16 * count, width), BF16),
            pltpu.SemaphoreType.DMA((3,)),
            pltpu.SemaphoreType.DMA(()),
            pltpu.SemaphoreType.DMA(()),
        ],
        compiler_params=pltpu.CompilerParams(vmem_limit_bytes=16 << 20),
        name="seeds",
    )(
        place,
        pltpu.with_memory_space_constraint(shot_starts, pltpu.HBM),
        pltpu.with_memory_space_constraint(seed_offsets, pltpu.HBM),
        far_tokens,
    )
    given = lax.ppermute(give, "feat", [(0, 1)])
    edge, given = lax.optimization_barrier((edge, given))
    edge = lax.ppermute(edge, "feat", [(0, 1), (1, 0)])
    x = first + given[:count]
    y = own + given[count:]
    received = lax.ppermute(x, AXES, across)
    near_tokens = pl.pallas_call(
        load_kernel,
        out_shape=shape(rows, width),
        in_specs=[HBM_SPEC, VMEM_SPEC],
        out_specs=VMEM_SPEC,
        scratch_shapes=[pltpu.SemaphoreType.DMA((4,))],
        compiler_params=pltpu.CompilerParams(vmem_limit_bytes=16 << 20),
        name="load",
    )(far_tokens, x)
    mass = jnp.zeros((count, LANES), F32)
    for iteration in range(ITERS):
        send, x, mass, y = pl.pallas_call(
            functools.partial(pool_kernel, iteration == 0),
            out_shape=(
                shape(count, width + LANES),
                shape(count, width, dtype=F32),
                shape(count, LANES, dtype=F32),
                shape(count, width, dtype=F32),
            ),
            in_specs=[SMEM_SPEC] * 2 + [VMEM_SPEC] * 6,
            out_specs=[VMEM_SPEC] * 4,
            scratch_shapes=[
                pltpu.VMEM((2 * count, width), BF16),
                pltpu.VMEM((2 * count, width), F32),
                pltpu.VMEM((2 * count, LANES), F32),
            ],
            compiler_params=pltpu.CompilerParams(vmem_limit_bytes=16 << 20),
            name="pool",
        )(place, meta, near_tokens, edge, x, received, mass, y)
        received = lax.ppermute(send, AXES, across)
    normed = pl.pallas_call(
        norm_kernel,
        out_shape=shape(count, width),
        in_specs=[SMEM_SPEC] + [VMEM_SPEC] * 5,
        out_specs=VMEM_SPEC,
        compiler_params=pltpu.CompilerParams(vmem_limit_bytes=8 << 20),
        name="norm",
    )(meta, x, received, mass, y, norm_gain[None, :])
    projected = jnp.dot(
        lax.all_gather(normed, "feat", axis=0, tiled=True),
        proj_weight,
        preferred_element_type=F32,
    )
    return projected.astype(BF16)


def solution(mesh):
    in_specs = (P(AXES, None), P(), P(), P(), P(None, "feat"))
    out_specs = P("seq", "feat")
    return jax.shard_map(
        on_device, mesh=mesh, in_specs=in_specs, out_specs=out_specs, check_vma=False
    )
```

```python
import functools
import math

import jax
import jax.numpy as jnp
from jax import lax
from jax.experimental import pallas as pl
from jax.experimental.pallas import tpu as pltpu
from jax.sharding import PartitionSpec as P

ITERS = 3
AXES = ("seq", "feat")
LANES = 128
TILE = 512
F32 = jnp.float32
BF16 = jnp.bfloat16
VMEM_SPEC = pl.BlockSpec(memory_space=pltpu.VMEM)
HBM_SPEC = pl.BlockSpec(memory_space=pltpu.HBM)
SMEM_SPEC = pl.BlockSpec(memory_space=pltpu.SMEM)


def start_of(starts_ref, shot, shots, total):
    first = starts_ref[jnp.minimum(shot, shots - 1)]
    return jnp.where(shot >= shots, total, first)


def placement(index, starts_ref, rows):
    shots = starts_ref.shape[0]
    total = shots * rows
    second = index % 2 == 1
    here = start_of(starts_ref, index, shots, total)
    after = start_of(starts_ref, index + 1, shots, total)
    base = index * rows
    low = jnp.where(second, here, base)
    high = jnp.where(second, base + rows, after)
    cut = jnp.where(second, after, here)
    split = jnp.where(second, after < base + rows, here > base)
    x_low = jnp.where(split & second, cut, low)
    x_high = jnp.where(split & ~second, cut, high)
    y_low = jnp.where(split, jnp.where(second, low, cut), high)
    y_high = jnp.where(split, jnp.where(second, cut, high), high)
    return split, x_low, x_high, y_low, y_high


def column_of(row):
    n = row.shape[1]
    diagonal = lax.broadcasted_iota(jnp.int32, (n, n), 0) == lax.broadcasted_iota(
        jnp.int32, (n, n), 1
    )
    spread = jnp.where(diagonal, jnp.broadcast_to(row, (n, n)), 0)
    return jnp.sum(spread, axis=1, keepdims=True)


def seed_kernel(
    place_ref,
    starts_hbm,
    seeds_hbm,
    tokens_ref,
    first_ref,
    own_ref,
    give_ref,
    edge_ref,
    meta_ref,
    starts_ref,
    seeds_ref,
    seed_rows_ref,
    picked,
    index_sems,
    pick_sem,
    edge_sem,
):
    rows = tokens_ref.shape[0]
    reach = edge_ref.shape[0]
    shots, count = seeds_ref.shape
    total = shots * rows
    index = place_ref[0]
    second = index % 2 == 1
    base = index * rows
    indices = [
        pltpu.make_async_copy(starts_hbm, starts_ref, index_sems.at[0]),
        pltpu.make_async_copy(seeds_hbm, seeds_ref, index_sems.at[1]),
        pltpu.make_async_copy(seeds_hbm, seed_rows_ref, index_sems.at[2]),
    ]
    for copy in indices:
        copy.start()
    strip_low = pl.multiple_of(jnp.where(second, 0, rows - reach), 8)
    strip = pltpu.make_async_copy(tokens_ref.at[pl.ds(strip_low, reach), :], edge_ref, edge_sem)
    strip.start()
    for copy in indices:
        copy.wait()
    following = jnp.minimum(index + 1, shots - 1)
    here = start_of(starts_ref, index, shots, total)
    after = start_of(starts_ref, index + 1, shots, total)
    later = start_of(starts_ref, index + 2, shots, total)

    def fetch(k, carry):
        for which, (shot, begin) in enumerate(((index, here), (following, after))):
            place = begin + seeds_ref[shot, k] - base
            slot = pl.multiple_of((which * count + k) * 8, 8)
            here_too = (place >= 0) & (place < rows)
            group = pl.multiple_of(jnp.where(here_too, (place // 8) * 8, slot), 8)
            pltpu.make_async_copy(
                tokens_ref.at[pl.ds(group, 8), :], picked.at[pl.ds(slot, 8), :], pick_sem
            ).start()
        return carry

    lax.fori_loop(0, count, fetch, 0, unroll=8)
    for at, value in enumerate(placement(index, starts_ref, rows)):
        meta_ref[at] = value.astype(jnp.int32)
    choices = []
    for shot, begin in ((index, here), (following, after)):
        place = column_of(seed_rows_ref[pl.ds(shot, 1), :]) + (begin - base)
        valid = (place >= 0) & (place < rows)
        target = lax.broadcasted_iota(jnp.int32, (count, 1), 0) * 8 + place % 8
        lane = lax.broadcasted_iota(jnp.int32, (count, 8 * count), 1)
        choices.append(jnp.where(valid & (lane == target), 1.0, 0.0).astype(BF16))
    pltpu.make_async_copy(tokens_ref.at[pl.ds(0, 16 * count), :], picked, pick_sem).wait()
    own, tail = (
        jnp.dot(
            choose,
            picked[pl.ds(which * 8 * count, 8 * count), :],
            preferred_element_type=F32,
        )
        for which, choose in enumerate(choices)
    )
    ahead = jnp.where(second, after < base + rows, here > base)
    first = jnp.where(ahead, jnp.where(second, tail, 0.0), own)
    first_ref[...] = first.astype(BF16)
    own_ref[...] = own.astype(BF16)
    shared = later >= base + 2 * rows
    give_ref[pl.ds(0, count), :] = jnp.where(shared, tail, 0.0).astype(BF16)
    give_ref[pl.ds(count, count), :] = tail.astype(BF16)
    strip.wait()


def load_kernel(tokens_ref, after_ref, out_ref, sems):
    pieces = sems.shape[0]
    piece = tokens_ref.shape[0] // pieces
    copies = [
        pltpu.make_async_copy(
            tokens_ref.at[pl.ds(i * piece, piece), :],
            out_ref.at[pl.ds(i * piece, piece), :],
            sems.at[i],
        )
        for i in range(pieces)
    ]
    for copy in copies:
        copy.start()
    for copy in copies:
        copy.wait()


def total_mass(block):
    return jnp.sum(block.astype(F32), axis=1, keepdims=True)


def pool_kernel(first, role, place_ref, meta_ref, *refs):
    @pl.when(place_ref[0] % 2 == role)
    def _():
        pool_body(first, place_ref, meta_ref, *refs)


def pool_body(
    first,
    place_ref,
    meta_ref,
    tokens_ref,
    edge_ref,
    x_ref,
    recv_ref,
    mass_ref,
    y_ref,
    order_ref,
    send_out,
    x_out,
    mass_out,
    y_out,
    centroids,
    sums,
    masses,
):
    rows, width = tokens_ref.shape
    count = y_ref.shape[0]
    reach = edge_ref.shape[0]
    index = place_ref[0]
    base = index * rows
    edge_base = jnp.where(index % 2 == 1, base - reach, base + rows)
    x_range = (meta_ref[1], meta_ref[2])
    y_range = (meta_ref[3], meta_ref[4])
    scale = math.log2(math.e) / math.sqrt(width)

    if first:
        centroids[pl.ds(0, count), :] = x_ref[...] + recv_ref[...]
        centroids[pl.ds(count, count), :] = y_ref[...]
    else:
        mass = mass_ref[:, :1] + total_mass(recv_ref[:, width:])
        joined = x_ref[...] + recv_ref[:, :width].astype(F32)
        centroids[pl.ds(0, count), :] = (joined * (1.0 / mass)).astype(BF16)
        centroids[pl.ds(count, count), :] = y_ref[...].astype(BF16)
    sums[...] = jnp.zeros_like(sums)
    masses[...] = jnp.zeros_like(masses)

    tiles = [(tokens_ref, i * TILE, base + i * TILE) for i in range(rows // TILE)]
    tiles += [(edge_ref, i * TILE, edge_base + i * TILE) for i in range(reach // TILE)]

    def scores_of(tile):
        ref, row, _ = tile
        return lax.dot_general(
            centroids[...],
            ref[pl.ds(row, TILE), :],
            (((1,), (1,)), ((), ())),
            preferred_element_type=F32,
        )

    def weights_of(tile, scores):
        place = tile[2] + lax.broadcasted_iota(jnp.int32, (1, TILE), 1)
        in_x = (place >= x_range[0]) & (place < x_range[1])
        in_y = (place >= y_range[0]) & (place < y_range[1])
        mine = jnp.where(in_y, scores[count:], scores[:count])
        top = jnp.max(mine, axis=0, keepdims=True)
        powers = jnp.exp2((mine - top) * scale)
        inverse = 1.0 / jnp.sum(powers, axis=0, keepdims=True)
        weights = jnp.concatenate(
            [powers * jnp.where(in_x, inverse, 0.0), powers * jnp.where(in_y, inverse, 0.0)], axis=0
        )
        part = weights[:, :LANES]
        for i in range(1, TILE // LANES):
            part = part + weights[:, i * LANES : (i + 1) * LANES]
        masses[...] += part
        return weights.astype(BF16)

    scores = scores_of(tiles[0])
    for at, tile in enumerate(tiles):
        upcoming = scores_of(tiles[at + 1]) if at + 1 < len(tiles) else None
        weights = weights_of(tile, scores)
        sums[...] += jnp.dot(
            weights, tile[0][pl.ds(tile[1], TILE), :], preferred_element_type=F32
        )
        scores = upcoming

    mass = jnp.sum(masses[...], axis=1, keepdims=True)
    x_mass = mass[:count]
    x_sums = sums[pl.ds(0, count), :]
    x_out[...] = x_sums
    mass_out[...] = jnp.broadcast_to(x_mass, mass_out.shape)
    y_out[...] = sums[pl.ds(count, count), :] * (1.0 / mass[count:])
    send_out[:, :width] = x_sums.astype(BF16)
    high = x_mass.astype(BF16).astype(F32)
    middle = (x_mass - high).astype(BF16).astype(F32)
    low = x_mass - high - middle
    lane = lax.broadcasted_iota(jnp.int32, (count, LANES), 1)
    block = jnp.where(
        lane == 0, high, jnp.where(lane == 1, middle, jnp.where(lane == 2, low, 0.0))
    )
    send_out[:, width:] = block.astype(BF16)


def norm_kernel(place_ref, meta_ref, gain_ref, *refs):
    out_ref = refs[-1]
    width = out_ref.shape[1]
    split = meta_ref[0] != 0

    def finish(x_ref, recv_ref, mass_ref, y_ref):
        mass = mass_ref[:, :1] + total_mass(recv_ref[:, width:])
        joined = (x_ref[...] + recv_ref[:, :width].astype(F32)) * (1.0 / mass)
        centroid = jnp.where(split, y_ref[...], joined)
        spread = jnp.sqrt(jnp.mean(centroid * centroid, axis=-1, keepdims=True) + 1e-06)
        out_ref[...] = (centroid * (1.0 / spread) * gain_ref[...]).astype(BF16)

    for role in range(2):

        @pl.when(place_ref[0] % 2 == role)
        def _():
            finish(*refs[4 * role : 4 * role + 4])


def on_device(tokens, shot_starts, seed_offsets, norm_gain, proj_weight):
    rows, width = tokens.shape
    count = seed_offsets.shape[1]
    reach = 3 * rows // 8
    devices = lax.axis_size(AXES)
    place = lax.axis_index(AXES).astype(jnp.int32).reshape(1)
    ahead = [(i, i + 1) for i in range(1, devices - 1, 2)]
    across = ahead + [(target, source) for source, target in ahead]

    def shape(*dims, dtype=BF16):
        return jax.ShapeDtypeStruct(dims, dtype)

    far_tokens = pltpu.with_memory_space_constraint(tokens, pltpu.HBM)
    first, own, give, edge, meta = pl.pallas_call(
        seed_kernel,
        out_shape=(
            shape(count, width),
            shape(count, width),
            shape(2 * count, width),
            shape(reach, width),
            shape(8, dtype=jnp.int32),
        ),
        in_specs=[SMEM_SPEC, HBM_SPEC, HBM_SPEC, HBM_SPEC],
        out_specs=[VMEM_SPEC, VMEM_SPEC, VMEM_SPEC, VMEM_SPEC, SMEM_SPEC],
        scratch_shapes=[
            pltpu.SMEM(shot_starts.shape, jnp.int32),
            pltpu.SMEM(seed_offsets.shape, jnp.int32),
            pltpu.VMEM(seed_offsets.shape, jnp.int32),
            pltpu.VMEM((16 * count, width), BF16),
            pltpu.SemaphoreType.DMA((3,)),
            pltpu.SemaphoreType.DMA(()),
            pltpu.SemaphoreType.DMA(()),
        ],
        compiler_params=pltpu.CompilerParams(vmem_limit_bytes=16 << 20),
        name="seeds",
    )(
        place,
        pltpu.with_memory_space_constraint(shot_starts, pltpu.HBM),
        pltpu.with_memory_space_constraint(seed_offsets, pltpu.HBM),
        far_tokens,
    )
    given = lax.ppermute(give, "feat", [(0, 1)])
    edge, given = lax.optimization_barrier((edge, given))
    edge = lax.ppermute(edge, "feat", [(0, 1), (1, 0)])
    x = first + given[:count]
    y = own + given[count:]
    received = lax.ppermute(x, AXES, across)
    near_tokens = pl.pallas_call(
        load_kernel,
        out_shape=shape(rows, width),
        in_specs=[HBM_SPEC, VMEM_SPEC],
        out_specs=VMEM_SPEC,
        scratch_shapes=[pltpu.SemaphoreType.DMA((4,))],
        compiler_params=pltpu.CompilerParams(vmem_limit_bytes=16 << 20),
        name="load",
    )(far_tokens, x)
    mass = jnp.zeros((count, LANES), F32)
    ways = [(target, source) for source, target in ahead], ahead
    states = [(x, received, mass, y), (x, received, mass, y)]
    order = mass
    for iteration in range(ITERS):
        sends = [None, None]
        for role in (1, 0) if iteration % 2 == 0 else (0, 1):
            send, x, mass, y = pl.pallas_call(
                functools.partial(pool_kernel, iteration == 0, role),
                out_shape=(
                    shape(count, width + LANES),
                    shape(count, width, dtype=F32),
                    shape(count, LANES, dtype=F32),
                    shape(count, width, dtype=F32),
                ),
                in_specs=[SMEM_SPEC] * 2 + [VMEM_SPEC] * 7,
                out_specs=[VMEM_SPEC] * 4,
                scratch_shapes=[
                    pltpu.VMEM((2 * count, width), BF16),
                    pltpu.VMEM((2 * count, width), F32),
                    pltpu.VMEM((2 * count, LANES), F32),
                ],
                compiler_params=pltpu.CompilerParams(vmem_limit_bytes=16 << 20),
                name="pool",
            )(place, meta, near_tokens, edge, *states[role], order)
            order = mass
            sends[role] = lax.ppermute(send, AXES, ways[role])
            states[role] = (x, None, mass, y)
        states = [
            (x, sends[1 - role], mass, y) for role, (x, _, mass, y) in enumerate(states)
        ]
    normed = pl.pallas_call(
        norm_kernel,
        out_shape=shape(count, width),
        in_specs=[SMEM_SPEC] * 2 + [VMEM_SPEC] * 9,
        out_specs=VMEM_SPEC,
        compiler_params=pltpu.CompilerParams(vmem_limit_bytes=8 << 20),
        name="norm",
    )(place, meta, norm_gain[None, :], *states[0], *states[1])
    projected = jnp.dot(
        lax.all_gather(normed, "feat", axis=0, tiled=True),
        proj_weight,
        preferred_element_type=F32,
    )
    return projected.astype(BF16)


def solution(mesh):
    in_specs = (P(AXES, None), P(), P(), P(), P(None, "feat"))
    out_specs = P("seq", "feat")
    return jax.shard_map(
        on_device, mesh=mesh, in_specs=in_specs, out_specs=out_specs, check_vma=False
    )
```

```python
import functools
import math

import jax
import jax.numpy as jnp
from jax import lax
from jax.experimental import pallas as pl
from jax.experimental.pallas import tpu as pltpu
from jax.sharding import PartitionSpec as P

ITERS = 3
AXES = ("seq", "feat")
LANES = 128
TILE = 512
F32 = jnp.float32
BF16 = jnp.bfloat16
VMEM_SPEC = pl.BlockSpec(memory_space=pltpu.VMEM)
HBM_SPEC = pl.BlockSpec(memory_space=pltpu.HBM)
SMEM_SPEC = pl.BlockSpec(memory_space=pltpu.SMEM)


def start_of(starts_ref, shot, shots, total):
    first = starts_ref[jnp.minimum(shot, shots - 1)]
    return jnp.where(shot >= shots, total, first)


def placement(index, starts_ref, rows):
    shots = starts_ref.shape[0]
    total = shots * rows
    second = index % 2 == 1
    here = start_of(starts_ref, index, shots, total)
    after = start_of(starts_ref, index + 1, shots, total)
    base = index * rows
    low = jnp.where(second, here, base)
    high = jnp.where(second, base + rows, after)
    cut = jnp.where(second, after, here)
    split = jnp.where(second, after <= base + rows, here > base) | (index == 0)
    x_low = jnp.where(split & second, cut, low)
    x_high = jnp.where(split & ~second, cut, high)
    y_low = jnp.where(split, jnp.where(second, low, cut), high)
    y_high = jnp.where(split, jnp.where(second, cut, high), high)
    return split, x_low, x_high, y_low, y_high


def column_of(row):
    n = row.shape[1]
    diagonal = lax.broadcasted_iota(jnp.int32, (n, n), 0) == lax.broadcasted_iota(
        jnp.int32, (n, n), 1
    )
    spread = jnp.where(diagonal, jnp.broadcast_to(row, (n, n)), 0)
    return jnp.sum(spread, axis=1, keepdims=True)


def seed_kernel(
    place_ref,
    starts_hbm,
    seeds_hbm,
    tokens_ref,
    first_ref,
    own_ref,
    give_ref,
    edge_ref,
    meta_ref,
    starts_ref,
    seeds_ref,
    seed_rows_ref,
    picked,
    index_sems,
    pick_sem,
    edge_sem,
):
    rows = tokens_ref.shape[0]
    reach = edge_ref.shape[0]
    shots, count = seeds_ref.shape
    total = shots * rows
    index = place_ref[0]
    second = index % 2 == 1
    base = index * rows
    indices = [
        pltpu.make_async_copy(starts_hbm, starts_ref, index_sems.at[0]),
        pltpu.make_async_copy(seeds_hbm, seeds_ref, index_sems.at[1]),
        pltpu.make_async_copy(seeds_hbm, seed_rows_ref, index_sems.at[2]),
    ]
    for copy in indices:
        copy.start()
    strip_low = pl.multiple_of(jnp.where(second, 0, rows - reach), 8)
    strip = pltpu.make_async_copy(tokens_ref.at[pl.ds(strip_low, reach), :], edge_ref, edge_sem)
    strip.start()
    for copy in indices:
        copy.wait()
    following = jnp.minimum(index + 1, shots - 1)
    here = start_of(starts_ref, index, shots, total)
    after = start_of(starts_ref, index + 1, shots, total)
    later = start_of(starts_ref, index + 2, shots, total)

    def fetch(k, carry):
        for which, (shot, begin) in enumerate(((index, here), (following, after))):
            place = begin + seeds_ref[shot, k] - base
            slot = pl.multiple_of((which * count + k) * 8, 8)
            here_too = (place >= 0) & (place < rows)
            group = pl.multiple_of(jnp.where(here_too, (place // 8) * 8, slot), 8)
            pltpu.make_async_copy(
                tokens_ref.at[pl.ds(group, 8), :], picked.at[pl.ds(slot, 8), :], pick_sem
            ).start()
        return carry

    lax.fori_loop(0, count, fetch, 0, unroll=8)
    for at, value in enumerate(placement(index, starts_ref, rows)):
        meta_ref[at] = value.astype(jnp.int32)
    choices = []
    for shot, begin in ((index, here), (following, after)):
        place = column_of(seed_rows_ref[pl.ds(shot, 1), :]) + (begin - base)
        valid = (place >= 0) & (place < rows)
        target = lax.broadcasted_iota(jnp.int32, (count, 1), 0) * 8 + place % 8
        lane = lax.broadcasted_iota(jnp.int32, (count, 8 * count), 1)
        choices.append(jnp.where(valid & (lane == target), 1.0, 0.0).astype(BF16))
    pltpu.make_async_copy(tokens_ref.at[pl.ds(0, 16 * count), :], picked, pick_sem).wait()
    own, tail = (
        jnp.dot(
            choose,
            picked[pl.ds(which * 8 * count, 8 * count), :],
            preferred_element_type=F32,
        )
        for which, choose in enumerate(choices)
    )
    ahead = jnp.where(second, after <= base + rows, here > base)
    first = jnp.where(ahead, jnp.where(second, tail, 0.0), own)
    first_ref[...] = first.astype(BF16)
    own_ref[...] = own.astype(BF16)
    shared = later > base + 2 * rows
    give = jnp.where(second, 0.0, tail)
    give_ref[pl.ds(0, count), :] = jnp.where(shared, give, 0.0).astype(BF16)
    give_ref[pl.ds(count, count), :] = give.astype(BF16)
    strip.wait()


def load_kernel(tokens_ref, after_ref, out_ref, sems):
    pieces = sems.shape[0]
    piece = tokens_ref.shape[0] // pieces
    copies = [
        pltpu.make_async_copy(
            tokens_ref.at[pl.ds(i * piece, piece), :],
            out_ref.at[pl.ds(i * piece, piece), :],
            sems.at[i],
        )
        for i in range(pieces)
    ]
    for copy in copies:
        copy.start()
    for copy in copies:
        copy.wait()


def total_mass(block):
    return jnp.sum(block.astype(F32), axis=1, keepdims=True)


def pool_kernel(first, ends, devices, place_ref, meta_ref, *refs):
    at_end = (place_ref[0] == 0) | (place_ref[0] == devices - 1)

    @pl.when(at_end == ends)
    def _():
        pool_body(first, place_ref, meta_ref, *refs)


def pool_body(
    first,
    place_ref,
    meta_ref,
    tokens_ref,
    edge_ref,
    x_ref,
    recv_ref,
    mass_ref,
    y_ref,
    order_ref,
    send_out,
    x_out,
    mass_out,
    y_out,
    centroids,
    sums,
    masses,
):
    rows, width = tokens_ref.shape
    count = y_ref.shape[0]
    reach = edge_ref.shape[0]
    index = place_ref[0]
    base = index * rows
    edge_base = jnp.where(index % 2 == 1, base - reach, base + rows)
    x_range = (meta_ref[1], meta_ref[2])
    y_range = (meta_ref[3], meta_ref[4])
    scale = math.log2(math.e) / math.sqrt(width)

    occupied = x_range[0] < x_range[1]
    if first:
        joined = x_ref[...] + recv_ref[...]
        centroids[pl.ds(0, count), :] = jnp.where(occupied, joined, jnp.zeros_like(joined))
        centroids[pl.ds(count, count), :] = y_ref[...]
    else:
        mass = mass_ref[:, :1] + total_mass(recv_ref[:, width:])
        joined = x_ref[...] + recv_ref[:, :width].astype(F32)
        joined = jnp.where(occupied, joined * (1.0 / mass), 0.0)
        centroids[pl.ds(0, count), :] = joined.astype(BF16)
        centroids[pl.ds(count, count), :] = y_ref[...].astype(BF16)
    sums[...] = jnp.zeros_like(sums)
    masses[...] = jnp.zeros_like(masses)

    tiles = [(tokens_ref, i * TILE, base + i * TILE) for i in range(rows // TILE)]
    tiles += [(edge_ref, i * TILE, edge_base + i * TILE) for i in range(reach // TILE)]

    def scores_of(tile):
        ref, row, _ = tile
        return lax.dot_general(
            centroids[...],
            ref[pl.ds(row, TILE), :],
            (((1,), (1,)), ((), ())),
            preferred_element_type=F32,
        )

    def weights_of(tile, scores):
        place = tile[2] + lax.broadcasted_iota(jnp.int32, (1, TILE), 1)
        in_x = (place >= x_range[0]) & (place < x_range[1])
        in_y = (place >= y_range[0]) & (place < y_range[1])
        mine = jnp.where(in_y, scores[count:], scores[:count])
        top = jnp.max(mine, axis=0, keepdims=True)
        powers = jnp.exp2((mine - top) * scale)
        inverse = 1.0 / jnp.sum(powers, axis=0, keepdims=True)
        weights = jnp.concatenate(
            [powers * jnp.where(in_x, inverse, 0.0), powers * jnp.where(in_y, inverse, 0.0)], axis=0
        )
        part = weights[:, :LANES]
        for i in range(1, TILE // LANES):
            part = part + weights[:, i * LANES : (i + 1) * LANES]
        masses[...] += part
        return weights.astype(BF16)

    scores = scores_of(tiles[0])
    for at, tile in enumerate(tiles):
        upcoming = scores_of(tiles[at + 1]) if at + 1 < len(tiles) else None
        weights = weights_of(tile, scores)
        sums[...] += jnp.dot(
            weights, tile[0][pl.ds(tile[1], TILE), :], preferred_element_type=F32
        )
        scores = upcoming

    mass = jnp.sum(masses[...], axis=1, keepdims=True)
    x_mass = mass[:count]
    x_sums = sums[pl.ds(0, count), :]
    x_out[...] = x_sums
    mass_out[...] = jnp.broadcast_to(x_mass, mass_out.shape)
    y_out[...] = sums[pl.ds(count, count), :] * (1.0 / mass[count:])
    send_out[:, :width] = x_sums.astype(BF16)
    high = x_mass.astype(BF16).astype(F32)
    middle = (x_mass - high).astype(BF16).astype(F32)
    low = x_mass - high - middle
    lane = lax.broadcasted_iota(jnp.int32, (count, LANES), 1)
    block = jnp.where(
        lane == 0, high, jnp.where(lane == 1, middle, jnp.where(lane == 2, low, 0.0))
    )
    send_out[:, width:] = block.astype(BF16)


def norm_kernel(
    devices, place_ref, meta_ref, x_ref, recv_ref, mass_ref, y_ref, y_end_ref, gain_ref, out_ref
):
    width = x_ref.shape[1]
    split = meta_ref[0] != 0
    at_end = (place_ref[0] == 0) | (place_ref[0] == devices - 1)
    mass = mass_ref[:, :1] + total_mass(recv_ref[:, width:])
    joined = (x_ref[...] + recv_ref[:, :width].astype(F32)) * (1.0 / mass)
    own = jnp.where(at_end, y_end_ref[...], y_ref[...])
    centroid = jnp.where(split, own, joined)
    spread = jnp.sqrt(jnp.mean(centroid * centroid, axis=-1, keepdims=True) + 1e-06)
    out_ref[...] = (centroid * (1.0 / spread) * gain_ref[...]).astype(BF16)


def on_device(tokens, shot_starts, seed_offsets, norm_gain, proj_weight):
    rows, width = tokens.shape
    count = seed_offsets.shape[1]
    reach = 3 * rows // 8
    devices = lax.axis_size(AXES)
    place = lax.axis_index(AXES).astype(jnp.int32).reshape(1)
    across = [(i, i + 1) for i in range(1, devices - 1, 2)]
    across += [(target, source) for source, target in across]
    across += [(0, devices - 1), (devices - 1, 0)]
    pair = [(0, 1), (1, 0)]

    def shape(*dims, dtype=BF16):
        return jax.ShapeDtypeStruct(dims, dtype)

    far_tokens = pltpu.with_memory_space_constraint(tokens, pltpu.HBM)
    first, own, give, edge, meta = pl.pallas_call(
        seed_kernel,
        out_shape=(
            shape(count, width),
            shape(count, width),
            shape(2 * count, width),
            shape(reach, width),
            shape(8, dtype=jnp.int32),
        ),
        in_specs=[SMEM_SPEC, HBM_SPEC, HBM_SPEC, HBM_SPEC],
        out_specs=[VMEM_SPEC, VMEM_SPEC, VMEM_SPEC, VMEM_SPEC, SMEM_SPEC],
        scratch_shapes=[
            pltpu.SMEM(shot_starts.shape, jnp.int32),
            pltpu.SMEM(seed_offsets.shape, jnp.int32),
            pltpu.VMEM(seed_offsets.shape, jnp.int32),
            pltpu.VMEM((16 * count, width), BF16),
            pltpu.SemaphoreType.DMA((3,)),
            pltpu.SemaphoreType.DMA(()),
            pltpu.SemaphoreType.DMA(()),
        ],
        compiler_params=pltpu.CompilerParams(vmem_limit_bytes=16 << 20),
        name="seeds",
    )(
        place,
        pltpu.with_memory_space_constraint(shot_starts, pltpu.HBM),
        pltpu.with_memory_space_constraint(seed_offsets, pltpu.HBM),
        far_tokens,
    )
    given = lax.ppermute(give, "feat", pair)
    edge, given = lax.optimization_barrier((edge, given))
    edge = lax.ppermute(edge, "feat", pair)
    x = first + given[:count]
    y = own + given[count:]
    received = lax.ppermute(x, AXES, across)
    near_tokens = pl.pallas_call(
        load_kernel,
        out_shape=shape(rows, width),
        in_specs=[HBM_SPEC, VMEM_SPEC],
        out_specs=VMEM_SPEC,
        scratch_shapes=[pltpu.SemaphoreType.DMA((4,))],
        compiler_params=pltpu.CompilerParams(vmem_limit_bytes=16 << 20),
        name="load",
    )(far_tokens, x)
    mass = jnp.zeros((count, LANES), F32)

    def pool(iteration, ends, *state):
        return pl.pallas_call(
            functools.partial(pool_kernel, iteration == 0, ends, devices),
            out_shape=(
                shape(count, width + LANES),
                shape(count, width, dtype=F32),
                shape(count, LANES, dtype=F32),
                shape(count, width, dtype=F32),
            ),
            in_specs=[SMEM_SPEC] * 2 + [VMEM_SPEC] * 7,
            out_specs=[VMEM_SPEC] * 4,
            scratch_shapes=[
                pltpu.VMEM((2 * count, width), BF16),
                pltpu.VMEM((2 * count, width), F32),
                pltpu.VMEM((2 * count, LANES), F32),
            ],
            compiler_params=pltpu.CompilerParams(vmem_limit_bytes=16 << 20),
            name="ends" if ends else "pool",
        )(place, meta, near_tokens, edge, *state)

    y_end = y
    for iteration in range(ITERS):
        before = (x, received, mass)
        send, x, mass, y = pool(iteration, False, *before, y, y_end)
        received = lax.ppermute(send, AXES, across)
        y_end = pool(iteration, True, *before, y_end, mass)[3]
    normed = pl.pallas_call(
        functools.partial(norm_kernel, devices),
        out_shape=shape(count, width),
        in_specs=[SMEM_SPEC] * 2 + [VMEM_SPEC] * 6,
        out_specs=VMEM_SPEC,
        compiler_params=pltpu.CompilerParams(vmem_limit_bytes=8 << 20),
        name="norm",
    )(place, meta, x, received, mass, y, y_end, norm_gain[None, :])
    projected = jnp.dot(
        lax.all_gather(normed, "feat", axis=0, tiled=True),
        proj_weight,
        preferred_element_type=F32,
    )
    return projected.astype(BF16)


def solution(mesh):
    in_specs = (P(AXES, None), P(), P(), P(), P(None, "feat"))
    out_specs = P("seq", "feat")
    return jax.shard_map(
        on_device, mesh=mesh, in_specs=in_specs, out_specs=out_specs, check_vma=False
    )
```

```python
import functools
import math

import jax
import jax.numpy as jnp
from jax import lax
from jax.experimental import pallas as pl
from jax.experimental.pallas import tpu as pltpu
from jax.sharding import PartitionSpec as P

ITERS = 3
AXES = ("seq", "feat")
LANES = 128
TILE = 512
F32 = jnp.float32
BF16 = jnp.bfloat16
VMEM_SPEC = pl.BlockSpec(memory_space=pltpu.VMEM)
HBM_SPEC = pl.BlockSpec(memory_space=pltpu.HBM)
X_LOW, X_HIGH, Y_LOW, Y_HIGH, EDGE, SPLIT, OCCUPIED, UNUSED = range(8)


def start_of(starts_ref, shot, shots, total):
    first = starts_ref[jnp.minimum(shot, shots - 1)]
    return jnp.where(shot >= shots, total, first)


def column_of(row):
    n = row.shape[1]
    diagonal = lax.broadcasted_iota(jnp.int32, (n, n), 0) == lax.broadcasted_iota(
        jnp.int32, (n, n), 1
    )
    spread = jnp.where(diagonal, jnp.broadcast_to(row, (n, n)), 0)
    return jnp.sum(spread, axis=1, keepdims=True)


def seed_kernel(
    reach,
    starts_hbm,
    seeds_hbm,
    tokens_ref,
    first_ref,
    own_ref,
    tail_ref,
    share_ref,
    meta_ref,
    starts_ref,
    seeds_ref,
    seed_rows_ref,
    picked,
    index_sems,
    pick_sem,
):
    rows, width = tokens_ref.shape
    shots, count = seeds_ref.shape
    total = shots * rows
    index = lax.axis_index(AXES)
    second = index % 2 == 1
    base = index * rows
    indices = [
        pltpu.make_async_copy(starts_hbm, starts_ref, index_sems.at[0]),
        pltpu.make_async_copy(seeds_hbm, seeds_ref, index_sems.at[1]),
        pltpu.make_async_copy(seeds_hbm, seed_rows_ref, index_sems.at[2]),
    ]
    for copy in indices:
        copy.start()
    for copy in indices:
        copy.wait()
    following = jnp.minimum(index + 1, shots - 1)
    here = start_of(starts_ref, index, shots, total)
    after = start_of(starts_ref, index + 1, shots, total)

    def fetch(k, carry):
        for which, (shot, begin) in enumerate(((index, here), (following, after))):
            place = begin + seeds_ref[shot, k] - base
            slot = pl.multiple_of((which * count + k) * 8, 8)
            here_too = (place >= 0) & (place < rows)
            group = pl.multiple_of(jnp.where(here_too, (place // 8) * 8, slot), 8)
            pltpu.make_async_copy(
                tokens_ref.at[pl.ds(group, 8), :], picked.at[pl.ds(slot, 8), :], pick_sem
            ).start()
        return carry

    lax.fori_loop(0, count, fetch, 0, unroll=8)

    low = jnp.where(second, here - base, 0)
    high = jnp.where(second, rows, after - base)
    cut = jnp.where(second, after - base, here - base)
    split = jnp.where(second, after <= base + rows, here > base) | (index == 0)
    x_low = jnp.where(split & second, cut, low)
    x_high = jnp.where(split & ~second, cut, high)
    y_low = jnp.where(split, jnp.where(second, low, cut), high)
    y_high = jnp.where(split, jnp.where(second, cut, high), high)
    table = {
        X_LOW: x_low,
        X_HIGH: x_high,
        Y_LOW: y_low,
        Y_HIGH: y_high,
        EDGE: jnp.where(second, -reach, rows),
        SPLIT: split.astype(jnp.int32),
        OCCUPIED: (x_low < x_high).astype(jnp.int32),
        UNUSED: 0,
    }
    for row, value in table.items():
        meta_ref[pl.ds(row, 1), :] = jnp.full((1, width), value, jnp.int32)
    lends = jnp.where(second, 1.0, 0.0)
    row = lax.broadcasted_iota(jnp.int32, share_ref.shape, 0)
    share_ref[...] = jnp.where(row == 0, jnp.where(split, 0.0, lends), lends).astype(BF16)

    choices = []
    for shot, begin in ((index, here), (following, after)):
        place = column_of(seed_rows_ref[pl.ds(shot, 1), :]) + (begin - base)
        valid = (place >= 0) & (place < rows)
        target = lax.broadcasted_iota(jnp.int32, (count, 1), 0) * 8 + place % 8
        lane = lax.broadcasted_iota(jnp.int32, (count, 8 * count), 1)
        choices.append(jnp.where(valid & (lane == target), 1.0, 0.0).astype(BF16))
    pltpu.make_async_copy(tokens_ref.at[pl.ds(0, 16 * count), :], picked, pick_sem).wait()
    own, tail = (
        jnp.dot(
            choose,
            picked[pl.ds(which * 8 * count, 8 * count), :],
            preferred_element_type=F32,
        )
        for which, choose in enumerate(choices)
    )
    first_ref[...] = jnp.where(split, jnp.where(second, tail, 0.0), own).astype(BF16)
    own_ref[...] = own.astype(BF16)
    tail_ref[...] = tail.astype(BF16)


def copy_pieces(tokens_ref, low, out_ref, sems):
    pieces = sems.shape[0]
    piece = out_ref.shape[0] // pieces
    copies = [
        pltpu.make_async_copy(
            tokens_ref.at[pl.ds(pl.multiple_of(low + i * piece, 8), piece), :],
            out_ref.at[pl.ds(i * piece, piece), :],
            sems.at[i],
        )
        for i in range(pieces)
    ]
    for copy in copies:
        copy.start()
    for copy in copies:
        copy.wait()


def strip_kernel(tokens_ref, order_ref, out_ref, sems):
    second = lax.axis_index(AXES) % 2 == 1
    low = jnp.where(second, 0, tokens_ref.shape[0] - out_ref.shape[0])
    copy_pieces(tokens_ref, low, out_ref, sems)


def load_kernel(tokens_ref, order_ref, out_ref, sems):
    copy_pieces(tokens_ref, 0, out_ref, sems)


def at_end(devices):
    index = lax.axis_index(AXES)
    return (index == 0) | (index == devices - 1)


def lane_sum(block):
    return jnp.sum(block.astype(F32), axis=1, keepdims=True)


def pool_kernel(first, ends, devices, *refs):
    @pl.when(at_end(devices) == ends)
    def _():
        pool_body(first, ends, *refs)


def pool_body(first, ends, meta_ref, tokens_ref, edge_ref, *refs):
    if first:
        (x_ref, recv_ref, y_ref, _), refs = refs[:4], refs[4:]
        count, width = y_ref.shape
    else:
        (old_ref, old_mass_ref, recv_ref, _), refs = refs[:4], refs[4:]
        count, width = recv_ref.shape[0], old_ref.shape[1]
    sums, masses, *send_out, centroids = refs
    rows = tokens_ref.shape[0]
    reach = edge_ref.shape[0]
    scale = math.log2(math.e) / math.sqrt(width)
    x_rows, y_rows = pl.ds(0, count), pl.ds(count, count)

    occupied = meta_ref[pl.ds(OCCUPIED, 1), :] != 0
    if first:
        joined = x_ref[...] + recv_ref[...]
        centroids[x_rows, :] = jnp.where(occupied, joined, jnp.zeros_like(joined))
        centroids[y_rows, :] = y_ref[...]
    else:
        mass = lane_sum(old_mass_ref[x_rows, :]) + lane_sum(recv_ref[:, width:])
        joined = (old_ref[x_rows, :] + recv_ref[:, :width].astype(F32)) * (1.0 / mass)
        centroids[x_rows, :] = jnp.where(occupied, joined, 0.0).astype(BF16)
        mass = lane_sum(old_mass_ref[y_rows, :])
        centroids[y_rows, :] = (old_ref[y_rows, :] * (1.0 / mass)).astype(BF16)

    tiles = [(tokens_ref, i * TILE) for i in range(rows // TILE)]
    tiles += [(edge_ref, i * TILE) for i in range(reach // TILE)]

    def scores_of(tile):
        ref, row = tile
        return lax.dot_general(
            centroids[...],
            ref[pl.ds(row, TILE), :],
            (((1,), (1,)), ((), ())),
            preferred_element_type=F32,
        )

    def weights_of(tile, scores):
        ref, row = tile
        place = row + lax.broadcasted_iota(jnp.int32, (1, TILE), 1)
        if ref is edge_ref:
            place = place + meta_ref[pl.ds(EDGE, 1), :TILE]
        bound = [meta_ref[pl.ds(i, 1), :TILE] for i in (X_LOW, X_HIGH, Y_LOW, Y_HIGH)]
        in_x = (place >= bound[0]) & (place < bound[1])
        in_y = (place >= bound[2]) & (place < bound[3])
        mine = jnp.where(in_y, scores[count:], scores[:count])
        top = jnp.max(mine, axis=0, keepdims=True)
        powers = jnp.exp2((mine - top) * scale)
        inverse = 1.0 / jnp.sum(powers, axis=0, keepdims=True)
        return jnp.concatenate(
            [powers * jnp.where(in_x, inverse, 0.0), powers * jnp.where(in_y, inverse, 0.0)], axis=0
        )

    scores = scores_of(tiles[0])
    for at, tile in enumerate(tiles):
        upcoming = scores_of(tiles[at + 1]) if at + 1 < len(tiles) else None
        weights = weights_of(tile, scores)
        part = weights[:, :LANES]
        for i in range(1, TILE // LANES):
            part = part + weights[:, i * LANES : (i + 1) * LANES]
        added = jnp.dot(
            weights.astype(BF16), tile[0][pl.ds(tile[1], TILE), :], preferred_element_type=F32
        )
        if at == 0:
            masses[...] = part
            sums[...] = added
        else:
            masses[...] += part
            sums[...] += added
        scores = upcoming

    if ends:
        return
    (send_out,) = send_out
    mass = lane_sum(masses[x_rows, :])
    send_out[:, :width] = sums[x_rows, :].astype(BF16)
    high = mass.astype(BF16).astype(F32)
    middle = (mass - high).astype(BF16).astype(F32)
    low = mass - high - middle
    lane = lax.broadcasted_iota(jnp.int32, (count, LANES), 1)
    block = jnp.where(
        lane == 0, high, jnp.where(lane == 1, middle, jnp.where(lane == 2, low, 0.0))
    )
    send_out[:, width:] = block.astype(BF16)


def norm_kernel(devices, meta_ref, gain_ref, recv_ref, *refs):
    out_ref = refs[-1]
    count, width = out_ref.shape
    x_rows, y_rows = pl.ds(0, count), pl.ds(count, count)

    def finish(centroid):
        spread = jnp.sqrt(jnp.mean(centroid * centroid, axis=-1, keepdims=True) + 1e-06)
        out_ref[...] = (centroid * (1.0 / spread) * gain_ref[...]).astype(BF16)

    @pl.when(at_end(devices))
    def _():
        sums, masses = refs[2:4]
        finish(sums[y_rows, :] * (1.0 / lane_sum(masses[y_rows, :])))

    @pl.when(~at_end(devices))
    def _():
        sums, masses = refs[:2]
        mass = lane_sum(masses[x_rows, :]) + lane_sum(recv_ref[:, width:])
        joined = (sums[x_rows, :] + recv_ref[:, :width].astype(F32)) * (1.0 / mass)
        own = sums[y_rows, :] * (1.0 / lane_sum(masses[y_rows, :]))
        finish(jnp.where(meta_ref[pl.ds(SPLIT, 1), :] != 0, own, joined))


def on_device(tokens, shot_starts, seed_offsets, norm_gain, proj_weight):
    rows, width = tokens.shape
    count = seed_offsets.shape[1]
    reach = 3 * rows // 8
    devices = lax.axis_size(AXES)
    across = [(i, i + 1) for i in range(1, devices - 1, 2)]
    across += [(target, source) for source, target in across]
    across += [(0, devices - 1), (devices - 1, 0)]
    pair = [(0, 1), (1, 0)]

    def shape(*dims, dtype=BF16):
        return jax.ShapeDtypeStruct(dims, dtype)

    def in_hbm(array):
        return pltpu.with_memory_space_constraint(array, pltpu.HBM)

    far_tokens = in_hbm(tokens)
    first, own, tail, share, meta = pl.pallas_call(
        functools.partial(seed_kernel, reach),
        out_shape=(
            shape(count, width),
            shape(count, width),
            shape(count, width),
            shape(2, width),
            shape(8, width, dtype=jnp.int32),
        ),
        in_specs=[HBM_SPEC] * 3,
        out_specs=[VMEM_SPEC] * 5,
        scratch_shapes=[
            pltpu.SMEM(shot_starts.shape, jnp.int32),
            pltpu.SMEM(seed_offsets.shape, jnp.int32),
            pltpu.VMEM(seed_offsets.shape, jnp.int32),
            pltpu.VMEM((16 * count, width), BF16),
            pltpu.SemaphoreType.DMA((3,)),
            pltpu.SemaphoreType.DMA(()),
        ],
        compiler_params=pltpu.CompilerParams(vmem_limit_bytes=16 << 20),
        name="seeds",
    )(in_hbm(shot_starts), in_hbm(seed_offsets), far_tokens)
    given = lax.ppermute(tail, "feat", pair)

    def fetch(kernel, size, after, name):
        return pl.pallas_call(
            kernel,
            out_shape=shape(size, width),
            in_specs=[HBM_SPEC, VMEM_SPEC],
            out_specs=VMEM_SPEC,
            scratch_shapes=[pltpu.SemaphoreType.DMA((4,))],
            compiler_params=pltpu.CompilerParams(vmem_limit_bytes=16 << 20),
            name=name,
        )(far_tokens, after)

    edge = fetch(strip_kernel, reach, tail, "strip")
    edge, given = lax.optimization_barrier((edge, given))
    edge = lax.ppermute(edge, "feat", pair)
    x = first + given * share[:1]
    y = own + given * share[1:]
    received = lax.ppermute(x, AXES, across)
    near_tokens = fetch(load_kernel, rows, x, "load")

    def pool(first, ends, *state):
        outs = (shape(2 * count, width, dtype=F32), shape(2 * count, LANES, dtype=F32))
        outs += () if ends else (shape(count, width + LANES),)
        return pl.pallas_call(
            functools.partial(pool_kernel, first, ends, devices),
            out_shape=outs,
            in_specs=[VMEM_SPEC] * 7,
            out_specs=[VMEM_SPEC] * len(outs),
            scratch_shapes=[pltpu.VMEM((2 * count, width), BF16)],
            compiler_params=pltpu.CompilerParams(vmem_limit_bytes=16 << 20),
            name="ends" if ends else "pool",
        )(meta, near_tokens, edge, *state)

    sums, masses, send = pool(True, False, x, received, y, y)
    start = received
    received = lax.ppermute(send, AXES, across)
    end_sums, end_masses = pool(True, True, x, start, y, masses)
    for _ in range(ITERS - 1):
        before = received
        sums, masses, send = pool(False, False, sums, masses, before, end_masses)
        received = lax.ppermute(send, AXES, across)
        end_sums, end_masses = pool(False, True, end_sums, end_masses, before, masses)
    normed = pl.pallas_call(
        functools.partial(norm_kernel, devices),
        out_shape=shape(count, width),
        in_specs=[VMEM_SPEC] * 7,
        out_specs=VMEM_SPEC,
        compiler_params=pltpu.CompilerParams(vmem_limit_bytes=8 << 20),
        name="norm",
    )(meta, norm_gain[None, :], received, sums, masses, end_sums, end_masses)
    both = lax.all_gather(normed, "feat", axis=0, tiled=True)
    return jnp.dot(both, proj_weight, preferred_element_type=F32).astype(BF16)


def solution(mesh):
    in_specs = (P(AXES, None), P(), P(), P(), P(None, "feat"))
    out_specs = P("seq", "feat")
    return jax.shard_map(
        on_device, mesh=mesh, in_specs=in_specs, out_specs=out_specs, check_vma=False
    )
```

```python
import functools
import math

import jax
import jax.numpy as jnp
from jax import lax
from jax.experimental import pallas as pl
from jax.experimental.pallas import tpu as pltpu
from jax.sharding import PartitionSpec as P

ITERS = 3
AXES = ("seq", "feat")
LANES = 128
TILE = 512
F32 = jnp.float32
BF16 = jnp.bfloat16
VMEM_SPEC = pl.BlockSpec(memory_space=pltpu.VMEM)
HBM_SPEC = pl.BlockSpec(memory_space=pltpu.HBM)
X_LOW, X_HIGH, Y_LOW, Y_HIGH, EDGE, SPLIT, OCCUPIED, UNUSED = range(8)


def start_of(starts_ref, shot, shots, total):
    first = starts_ref[jnp.minimum(shot, shots - 1)]
    return jnp.where(shot >= shots, total, first)


def column_of(row):
    n = row.shape[1]
    diagonal = lax.broadcasted_iota(jnp.int32, (n, n), 0) == lax.broadcasted_iota(
        jnp.int32, (n, n), 1
    )
    spread = jnp.where(diagonal, jnp.broadcast_to(row, (n, n)), 0)
    return jnp.sum(spread, axis=1, keepdims=True)


def seed_kernel(
    reach,
    starts_hbm,
    seeds_hbm,
    tokens_ref,
    first_ref,
    own_ref,
    tail_ref,
    share_ref,
    meta_ref,
    starts_ref,
    seeds_ref,
    seed_rows_ref,
    picked,
    index_sems,
    pick_sem,
):
    rows, width = tokens_ref.shape
    shots, count = seeds_ref.shape
    total = shots * rows
    index = lax.axis_index(AXES)
    second = index % 2 == 1
    base = index * rows
    indices = [
        pltpu.make_async_copy(starts_hbm, starts_ref, index_sems.at[0]),
        pltpu.make_async_copy(seeds_hbm, seeds_ref, index_sems.at[1]),
        pltpu.make_async_copy(seeds_hbm, seed_rows_ref, index_sems.at[2]),
    ]
    for copy in indices:
        copy.start()
    for copy in indices:
        copy.wait()
    following = jnp.minimum(index + 1, shots - 1)
    here = start_of(starts_ref, index, shots, total)
    after = start_of(starts_ref, index + 1, shots, total)

    def fetch(k, carry):
        for which, (shot, begin) in enumerate(((index, here), (following, after))):
            place = begin + seeds_ref[shot, k] - base
            slot = pl.multiple_of((which * count + k) * 8, 8)
            here_too = (place >= 0) & (place < rows)
            group = pl.multiple_of(jnp.where(here_too, (place // 8) * 8, slot), 8)
            pltpu.make_async_copy(
                tokens_ref.at[pl.ds(group, 8), :], picked.at[pl.ds(slot, 8), :], pick_sem
            ).start()
        return carry

    lax.fori_loop(0, count, fetch, 0, unroll=8)

    low = jnp.where(second, here - base, 0)
    high = jnp.where(second, rows, after - base)
    cut = jnp.where(second, after - base, here - base)
    split = jnp.where(second, after <= base + rows, here > base) | (index == 0)
    x_low = jnp.where(split & second, cut, low)
    x_high = jnp.where(split & ~second, cut, high)
    y_low = jnp.where(split, jnp.where(second, low, cut), high)
    y_high = jnp.where(split, jnp.where(second, cut, high), high)
    table = {
        X_LOW: x_low,
        X_HIGH: x_high,
        Y_LOW: y_low,
        Y_HIGH: y_high,
        EDGE: jnp.where(second, -reach, rows),
        SPLIT: split.astype(jnp.int32),
        OCCUPIED: (x_low < x_high).astype(jnp.int32),
        UNUSED: 0,
    }
    for row, value in table.items():
        meta_ref[pl.ds(row, 1), :] = jnp.full((1, width), value, jnp.int32)
    lends = jnp.where(second, 1.0, 0.0)
    row = lax.broadcasted_iota(jnp.int32, share_ref.shape, 0)
    share_ref[...] = jnp.where(row == 0, jnp.where(split, 0.0, lends), lends).astype(BF16)

    choices = []
    for shot, begin in ((index, here), (following, after)):
        place = column_of(seed_rows_ref[pl.ds(shot, 1), :]) + (begin - base)
        valid = (place >= 0) & (place < rows)
        target = lax.broadcasted_iota(jnp.int32, (count, 1), 0) * 8 + place % 8
        lane = lax.broadcasted_iota(jnp.int32, (count, 8 * count), 1)
        choices.append(jnp.where(valid & (lane == target), 1.0, 0.0).astype(BF16))
    pltpu.make_async_copy(tokens_ref.at[pl.ds(0, 16 * count), :], picked, pick_sem).wait()
    own, tail = (
        jnp.dot(
            choose,
            picked[pl.ds(which * 8 * count, 8 * count), :],
            preferred_element_type=F32,
        )
        for which, choose in enumerate(choices)
    )
    first_ref[...] = jnp.where(split, jnp.where(second, tail, 0.0), own).astype(BF16)
    own_ref[...] = own.astype(BF16)
    tail_ref[...] = tail.astype(BF16)


def copy_pieces(tokens_ref, low, out_ref, sems):
    pieces = sems.shape[0]
    piece = out_ref.shape[0] // pieces
    copies = [
        pltpu.make_async_copy(
            tokens_ref.at[pl.ds(pl.multiple_of(low + i * piece, 8), piece), :],
            out_ref.at[pl.ds(i * piece, piece), :],
            sems.at[i],
        )
        for i in range(pieces)
    ]
    for copy in copies:
        copy.start()
    for copy in copies:
        copy.wait()


def strip_kernel(tokens_ref, order_ref, out_ref, sems):
    second = lax.axis_index(AXES) % 2 == 1
    low = jnp.where(second, 0, tokens_ref.shape[0] - out_ref.shape[0])
    copy_pieces(tokens_ref, low, out_ref, sems)


def load_kernel(tokens_ref, order_ref, out_ref, sems):
    copy_pieces(tokens_ref, 0, out_ref, sems)


def at_end(devices):
    index = lax.axis_index(AXES)
    return (index == 0) | (index == devices - 1)


def lane_sum(block):
    return jnp.sum(block.astype(F32), axis=1, keepdims=True)


def pool_kernel(first, ends, devices, *refs):
    @pl.when(at_end(devices) == ends)
    def _():
        pool_body(first, ends, *refs)


def pool_body(first, ends, meta_ref, tokens_ref, edge_ref, *refs):
    if first:
        (x_ref, recv_ref, y_ref, _), refs = refs[:4], refs[4:]
        count, width = y_ref.shape
    else:
        (old_ref, old_mass_ref, recv_ref, _), refs = refs[:4], refs[4:]
        count, width = recv_ref.shape[0], old_ref.shape[1]
    sums, masses, *send_out, centroids = refs
    rows = tokens_ref.shape[0]
    reach = edge_ref.shape[0]
    scale = math.log2(math.e) / math.sqrt(width)
    x_rows, y_rows = pl.ds(0, count), pl.ds(count, count)

    occupied = meta_ref[pl.ds(OCCUPIED, 1), :] != 0
    if first:
        joined = x_ref[...] + recv_ref[...]
        centroids[x_rows, :] = jnp.where(occupied, joined, jnp.zeros_like(joined))
        centroids[y_rows, :] = y_ref[...]
    else:
        mass = lane_sum(old_mass_ref[x_rows, :]) + lane_sum(recv_ref[:, width:])
        joined = (old_ref[x_rows, :] + recv_ref[:, :width].astype(F32)) * (1.0 / mass)
        centroids[x_rows, :] = jnp.where(occupied, joined, 0.0).astype(BF16)
        mass = lane_sum(old_mass_ref[y_rows, :])
        centroids[y_rows, :] = (old_ref[y_rows, :] * (1.0 / mass)).astype(BF16)

    tiles = [(tokens_ref, i * TILE) for i in range(rows // TILE)]
    tiles += [(edge_ref, i * TILE) for i in range(reach // TILE)]

    def scores_of(tile):
        ref, row = tile
        return lax.dot_general(
            centroids[...],
            ref[pl.ds(row, TILE), :],
            (((1,), (1,)), ((), ())),
            preferred_element_type=F32,
        )

    def weights_of(tile, scores):
        ref, row = tile
        place = row + lax.broadcasted_iota(jnp.int32, (1, TILE), 1)
        if ref is edge_ref:
            place = place + meta_ref[pl.ds(EDGE, 1), :TILE]
        bound = [meta_ref[pl.ds(i, 1), :TILE] for i in (X_LOW, X_HIGH, Y_LOW, Y_HIGH)]
        in_x = (place >= bound[0]) & (place < bound[1])
        in_y = (place >= bound[2]) & (place < bound[3])
        mine = jnp.where(in_y, scores[count:], scores[:count])
        top = jnp.max(mine, axis=0, keepdims=True)
        powers = jnp.exp2((mine - top) * scale)
        inverse = 1.0 / jnp.sum(powers, axis=0, keepdims=True)
        return jnp.concatenate(
            [powers * jnp.where(in_x, inverse, 0.0), powers * jnp.where(in_y, inverse, 0.0)], axis=0
        )

    scores = scores_of(tiles[0])
    for at, tile in enumerate(tiles):
        upcoming = scores_of(tiles[at + 1]) if at + 1 < len(tiles) else None
        weights = weights_of(tile, scores)
        part = weights[:, :LANES]
        for i in range(1, TILE // LANES):
            part = part + weights[:, i * LANES : (i + 1) * LANES]
        added = jnp.dot(
            weights.astype(BF16), tile[0][pl.ds(tile[1], TILE), :], preferred_element_type=F32
        )
        if at == 0:
            masses[...] = part
            sums[...] = added
        else:
            masses[...] += part
            sums[...] += added
        scores = upcoming

    if ends:
        return
    (send_out,) = send_out
    mass = lane_sum(masses[x_rows, :])
    send_out[:, :width] = sums[x_rows, :].astype(BF16)
    high = mass.astype(BF16).astype(F32)
    middle = (mass - high).astype(BF16).astype(F32)
    low = mass - high - middle
    lane = lax.broadcasted_iota(jnp.int32, (count, LANES), 1)
    block = jnp.where(
        lane == 0, high, jnp.where(lane == 1, middle, jnp.where(lane == 2, low, 0.0))
    )
    send_out[:, width:] = block.astype(BF16)


def norm_kernel(devices, meta_ref, gain_ref, recv_ref, *refs):
    out_ref = refs[-1]
    count, width = out_ref.shape
    x_rows, y_rows = pl.ds(0, count), pl.ds(count, count)

    def finish(centroid):
        spread = jnp.sqrt(jnp.mean(centroid * centroid, axis=-1, keepdims=True) + 1e-06)
        out_ref[...] = (centroid * (1.0 / spread) * gain_ref[...]).astype(BF16)

    @pl.when(at_end(devices))
    def _():
        sums, masses = refs[2:4]
        finish(sums[y_rows, :] * (1.0 / lane_sum(masses[y_rows, :])))

    @pl.when(~at_end(devices))
    def _():
        sums, masses = refs[:2]
        mass = lane_sum(masses[x_rows, :]) + lane_sum(recv_ref[:, width:])
        joined = (sums[x_rows, :] + recv_ref[:, :width].astype(F32)) * (1.0 / mass)
        own = sums[y_rows, :] * (1.0 / lane_sum(masses[y_rows, :]))
        finish(jnp.where(meta_ref[pl.ds(SPLIT, 1), :] != 0, own, joined))


def join_kernel(normed_ref, other_ref, out_ref):
    count = normed_ref.shape[0]
    for half in range(2):

        @pl.when(lax.axis_index("feat") == half)
        def _():
            out_ref[pl.ds(half * count, count), :] = normed_ref[...]
            out_ref[pl.ds((1 - half) * count, count), :] = other_ref[...]


def on_device(tokens, shot_starts, seed_offsets, norm_gain, proj_weight):
    rows, width = tokens.shape
    count = seed_offsets.shape[1]
    reach = 3 * rows // 8
    devices = lax.axis_size(AXES)
    across = [(i, i + 1) for i in range(1, devices - 1, 2)]
    across += [(target, source) for source, target in across]
    across += [(0, devices - 1), (devices - 1, 0)]
    pair = [(0, 1), (1, 0)]

    def shape(*dims, dtype=BF16):
        return jax.ShapeDtypeStruct(dims, dtype)

    def in_hbm(array):
        return pltpu.with_memory_space_constraint(array, pltpu.HBM)

    far_tokens = in_hbm(tokens)
    first, own, tail, share, meta = pl.pallas_call(
        functools.partial(seed_kernel, reach),
        out_shape=(
            shape(count, width),
            shape(count, width),
            shape(count, width),
            shape(2, width),
            shape(8, width, dtype=jnp.int32),
        ),
        in_specs=[HBM_SPEC] * 3,
        out_specs=[VMEM_SPEC] * 5,
        scratch_shapes=[
            pltpu.SMEM(shot_starts.shape, jnp.int32),
            pltpu.SMEM(seed_offsets.shape, jnp.int32),
            pltpu.VMEM(seed_offsets.shape, jnp.int32),
            pltpu.VMEM((16 * count, width), BF16),
            pltpu.SemaphoreType.DMA((3,)),
            pltpu.SemaphoreType.DMA(()),
        ],
        compiler_params=pltpu.CompilerParams(vmem_limit_bytes=16 << 20),
        name="seeds",
    )(in_hbm(shot_starts), in_hbm(seed_offsets), far_tokens)
    given = lax.ppermute(tail, "feat", pair)

    def fetch(kernel, size, after, name):
        return pl.pallas_call(
            kernel,
            out_shape=shape(size, width),
            in_specs=[HBM_SPEC, VMEM_SPEC],
            out_specs=VMEM_SPEC,
            scratch_shapes=[pltpu.SemaphoreType.DMA((4,))],
            compiler_params=pltpu.CompilerParams(vmem_limit_bytes=16 << 20),
            name=name,
        )(far_tokens, after)

    edge = fetch(strip_kernel, reach, tail, "strip")
    edge, given = lax.optimization_barrier((edge, given))
    edge = lax.ppermute(edge, "feat", pair)
    x = first + given * share[:1]
    y = own + given * share[1:]
    received = lax.ppermute(x, AXES, across)
    near_tokens = fetch(load_kernel, rows, x, "load")

    def pool(first, ends, *state):
        outs = (shape(2 * count, width, dtype=F32), shape(2 * count, LANES, dtype=F32))
        outs += () if ends else (shape(count, width + LANES),)
        return pl.pallas_call(
            functools.partial(pool_kernel, first, ends, devices),
            out_shape=outs,
            in_specs=[VMEM_SPEC] * 7,
            out_specs=[VMEM_SPEC] * len(outs),
            scratch_shapes=[pltpu.VMEM((2 * count, width), BF16)],
            compiler_params=pltpu.CompilerParams(vmem_limit_bytes=16 << 20),
            name="ends" if ends else "pool",
        )(meta, near_tokens, edge, *state)

    sums, masses, send = pool(True, False, x, received, y, y)
    start = received
    received = lax.ppermute(send, AXES, across)
    end_sums, end_masses = pool(True, True, x, start, y, masses)
    for _ in range(ITERS - 1):
        before = received
        sums, masses, send = pool(False, False, sums, masses, before, end_masses)
        received = lax.ppermute(send, AXES, across)
        end_sums, end_masses = pool(False, True, end_sums, end_masses, before, masses)
    normed = pl.pallas_call(
        functools.partial(norm_kernel, devices),
        out_shape=shape(count, width),
        in_specs=[VMEM_SPEC] * 7,
        out_specs=VMEM_SPEC,
        compiler_params=pltpu.CompilerParams(vmem_limit_bytes=8 << 20),
        name="norm",
    )(meta, norm_gain[None, :], received, sums, masses, end_sums, end_masses)
    both = pl.pallas_call(
        join_kernel,
        out_shape=shape(2 * count, width),
        in_specs=[VMEM_SPEC] * 2,
        out_specs=VMEM_SPEC,
        compiler_params=pltpu.CompilerParams(vmem_limit_bytes=8 << 20),
        name="join",
    )(normed, lax.ppermute(normed, "feat", pair))
    return jnp.dot(both, proj_weight, preferred_element_type=F32).astype(BF16)


def solution(mesh):
    in_specs = (P(AXES, None), P(), P(), P(), P(None, "feat"))
    out_specs = P("seq", "feat")
    return jax.shard_map(
        on_device, mesh=mesh, in_specs=in_specs, out_specs=out_specs, check_vma=False
    )
```

```python
import functools
import math

import jax
import jax.numpy as jnp
from jax import lax
from jax.experimental import pallas as pl
from jax.experimental.pallas import tpu as pltpu
from jax.sharding import PartitionSpec as P

ITERS = 3
AXES = ("seq", "feat")
LANES = 128
TILE = 512
F32 = jnp.float32
BF16 = jnp.bfloat16
VMEM_SPEC = pl.BlockSpec(memory_space=pltpu.VMEM)
HBM_SPEC = pl.BlockSpec(memory_space=pltpu.HBM)
X_LOW, X_HIGH, Y_LOW, Y_HIGH, EDGE, SPLIT, OCCUPIED, UNUSED = range(8)


def start_of(starts_ref, shot, shots, total):
    first = starts_ref[jnp.minimum(shot, shots - 1)]
    return jnp.where(shot >= shots, total, first)


def column_of(row):
    n = row.shape[1]
    diagonal = lax.broadcasted_iota(jnp.int32, (n, n), 0) == lax.broadcasted_iota(
        jnp.int32, (n, n), 1
    )
    spread = jnp.where(diagonal, jnp.broadcast_to(row, (n, n)), 0)
    return jnp.sum(spread, axis=1, keepdims=True)


def seed_kernel(
    reach,
    starts_hbm,
    seeds_hbm,
    tokens_ref,
    first_ref,
    own_ref,
    tail_ref,
    share_ref,
    meta_ref,
    edge_ref,
    starts_ref,
    seeds_ref,
    seed_rows_ref,
    picked,
    index_sems,
    pick_sem,
    edge_sem,
):
    rows, width = tokens_ref.shape
    shots, count = seeds_ref.shape
    total = shots * rows
    index = lax.axis_index(AXES)
    second = index % 2 == 1
    base = index * rows
    indices = [
        pltpu.make_async_copy(starts_hbm, starts_ref, index_sems.at[0]),
        pltpu.make_async_copy(seeds_hbm, seeds_ref, index_sems.at[1]),
        pltpu.make_async_copy(seeds_hbm, seed_rows_ref, index_sems.at[2]),
    ]
    for copy in indices:
        copy.start()
    strip_low = pl.multiple_of(jnp.where(second, 0, rows - reach), 8)
    strip = pltpu.make_async_copy(
        tokens_ref.at[pl.ds(strip_low, edge_ref.shape[0]), :], edge_ref, edge_sem
    )
    strip.start()
    for copy in indices:
        copy.wait()
    following = jnp.minimum(index + 1, shots - 1)
    here = start_of(starts_ref, index, shots, total)
    after = start_of(starts_ref, index + 1, shots, total)

    def fetch(k, carry):
        for which, (shot, begin) in enumerate(((index, here), (following, after))):
            place = begin + seeds_ref[shot, k] - base
            slot = pl.multiple_of((which * count + k) * 8, 8)
            here_too = (place >= 0) & (place < rows)
            group = pl.multiple_of(jnp.where(here_too, (place // 8) * 8, slot), 8)
            pltpu.make_async_copy(
                tokens_ref.at[pl.ds(group, 8), :], picked.at[pl.ds(slot, 8), :], pick_sem
            ).start()
        return carry

    lax.fori_loop(0, count, fetch, 0, unroll=8)

    low = jnp.where(second, here - base, 0)
    high = jnp.where(second, rows, after - base)
    cut = jnp.where(second, after - base, here - base)
    split = jnp.where(second, after <= base + rows, here > base) | (index == 0)
    x_low = jnp.where(split & second, cut, low)
    x_high = jnp.where(split & ~second, cut, high)
    y_low = jnp.where(split, jnp.where(second, low, cut), high)
    y_high = jnp.where(split, jnp.where(second, cut, high), high)
    table = {
        X_LOW: x_low,
        X_HIGH: x_high,
        Y_LOW: y_low,
        Y_HIGH: y_high,
        EDGE: jnp.where(second, -reach, rows),
        SPLIT: split.astype(jnp.int32),
        OCCUPIED: (x_low < x_high).astype(jnp.int32),
        UNUSED: 0,
    }
    for row, value in table.items():
        meta_ref[pl.ds(row, 1), :] = jnp.full((1, width), value, jnp.int32)
    lends = jnp.where(second, 1.0, 0.0)
    row = lax.broadcasted_iota(jnp.int32, share_ref.shape, 0)
    share_ref[...] = jnp.where(row == 0, jnp.where(split, 0.0, lends), lends).astype(BF16)

    choices = []
    for shot, begin in ((index, here), (following, after)):
        place = column_of(seed_rows_ref[pl.ds(shot, 1), :]) + (begin - base)
        valid = (place >= 0) & (place < rows)
        target = lax.broadcasted_iota(jnp.int32, (count, 1), 0) * 8 + place % 8
        lane = lax.broadcasted_iota(jnp.int32, (count, 8 * count), 1)
        choices.append(jnp.where(valid & (lane == target), 1.0, 0.0).astype(BF16))
    pltpu.make_async_copy(tokens_ref.at[pl.ds(0, 16 * count), :], picked, pick_sem).wait()
    own, tail = (
        jnp.dot(
            choose,
            picked[pl.ds(which * 8 * count, 8 * count), :],
            preferred_element_type=F32,
        )
        for which, choose in enumerate(choices)
    )
    first_ref[...] = jnp.where(split, jnp.where(second, tail, 0.0), own).astype(BF16)
    own_ref[...] = own.astype(BF16)
    tail_ref[...] = tail.astype(BF16)
    strip.wait()


def copy_pieces(tokens_ref, low, out_ref, sems):
    pieces = sems.shape[0]
    piece = out_ref.shape[0] // pieces
    copies = [
        pltpu.make_async_copy(
            tokens_ref.at[pl.ds(pl.multiple_of(low + i * piece, 8), piece), :],
            out_ref.at[pl.ds(i * piece, piece), :],
            sems.at[i],
        )
        for i in range(pieces)
    ]
    for copy in copies:
        copy.start()
    for copy in copies:
        copy.wait()


def strip_kernel(reach, tokens_ref, order_ref, out_ref, sems):
    size = out_ref.shape[0]
    second = lax.axis_index(AXES) % 2 == 1
    low = jnp.where(second, reach - size, tokens_ref.shape[0] - size)
    copy_pieces(tokens_ref, low, out_ref, sems)


def load_kernel(tokens_ref, order_ref, out_ref, sems):
    copy_pieces(tokens_ref, 0, out_ref, sems)


def at_end(devices):
    index = lax.axis_index(AXES)
    return (index == 0) | (index == devices - 1)


def lane_sum(block):
    return jnp.sum(block.astype(F32), axis=1, keepdims=True)


def pool_kernel(first, ends, devices, *refs):
    @pl.when(at_end(devices) == ends)
    def _():
        pool_body(first, ends, *refs)


def pool_body(first, ends, meta_ref, tokens_ref, *refs):
    edge_refs, refs = refs[:2], refs[2:]
    if first:
        (x_ref, recv_ref, y_ref, _), refs = refs[:4], refs[4:]
        count, width = y_ref.shape
    else:
        (old_ref, old_mass_ref, recv_ref, _), refs = refs[:4], refs[4:]
        count, width = recv_ref.shape[0], old_ref.shape[1]
    sums, masses, *send_out, centroids = refs
    rows = tokens_ref.shape[0]
    scale = math.log2(math.e) / math.sqrt(width)
    x_rows, y_rows = pl.ds(0, count), pl.ds(count, count)

    occupied = meta_ref[pl.ds(OCCUPIED, 1), :] != 0
    if first:
        joined = x_ref[...] + recv_ref[...]
        centroids[x_rows, :] = jnp.where(occupied, joined, jnp.zeros_like(joined))
        centroids[y_rows, :] = y_ref[...]
    else:
        mass = lane_sum(old_mass_ref[x_rows, :]) + lane_sum(recv_ref[:, width:])
        joined = (old_ref[x_rows, :] + recv_ref[:, :width].astype(F32)) * (1.0 / mass)
        centroids[x_rows, :] = jnp.where(occupied, joined, 0.0).astype(BF16)
        mass = lane_sum(old_mass_ref[y_rows, :])
        centroids[y_rows, :] = (old_ref[y_rows, :] * (1.0 / mass)).astype(BF16)

    tiles = [(tokens_ref, i * TILE, i * TILE, False) for i in range(rows // TILE)]
    begin = 0
    for ref in edge_refs:
        tiles += [(ref, i * TILE, begin + i * TILE, True) for i in range(ref.shape[0] // TILE)]
        begin += ref.shape[0]

    def scores_of(tile):
        ref, row, _, _ = tile
        return lax.dot_general(
            centroids[...],
            ref[pl.ds(row, TILE), :],
            (((1,), (1,)), ((), ())),
            preferred_element_type=F32,
        )

    def weights_of(tile, scores):
        _, _, begin, on_edge = tile
        place = begin + lax.broadcasted_iota(jnp.int32, (1, TILE), 1)
        if on_edge:
            place = place + meta_ref[pl.ds(EDGE, 1), :TILE]
        bound = [meta_ref[pl.ds(i, 1), :TILE] for i in (X_LOW, X_HIGH, Y_LOW, Y_HIGH)]
        in_x = (place >= bound[0]) & (place < bound[1])
        in_y = (place >= bound[2]) & (place < bound[3])
        mine = jnp.where(in_y, scores[count:], scores[:count])
        top = jnp.max(mine, axis=0, keepdims=True)
        powers = jnp.exp2((mine - top) * scale)
        inverse = 1.0 / jnp.sum(powers, axis=0, keepdims=True)
        return jnp.concatenate(
            [powers * jnp.where(in_x, inverse, 0.0), powers * jnp.where(in_y, inverse, 0.0)], axis=0
        )

    scores = scores_of(tiles[0])
    for at, tile in enumerate(tiles):
        upcoming = scores_of(tiles[at + 1]) if at + 1 < len(tiles) else None
        weights = weights_of(tile, scores)
        part = weights[:, :LANES]
        for i in range(1, TILE // LANES):
            part = part + weights[:, i * LANES : (i + 1) * LANES]
        added = jnp.dot(
            weights.astype(BF16), tile[0][pl.ds(tile[1], TILE), :], preferred_element_type=F32
        )
        if at == 0:
            masses[...] = part
            sums[...] = added
        else:
            masses[...] += part
            sums[...] += added
        scores = upcoming

    if ends:
        return
    (send_out,) = send_out
    mass = lane_sum(masses[x_rows, :])
    send_out[:, :width] = sums[x_rows, :].astype(BF16)
    high = mass.astype(BF16).astype(F32)
    middle = (mass - high).astype(BF16).astype(F32)
    low = mass - high - middle
    lane = lax.broadcasted_iota(jnp.int32, (count, LANES), 1)
    block = jnp.where(
        lane == 0, high, jnp.where(lane == 1, middle, jnp.where(lane == 2, low, 0.0))
    )
    send_out[:, width:] = block.astype(BF16)


def norm_kernel(devices, meta_ref, gain_ref, recv_ref, *refs):
    out_ref = refs[-1]
    count, width = out_ref.shape
    x_rows, y_rows = pl.ds(0, count), pl.ds(count, count)

    def finish(centroid):
        spread = jnp.sqrt(jnp.mean(centroid * centroid, axis=-1, keepdims=True) + 1e-06)
        out_ref[...] = (centroid * (1.0 / spread) * gain_ref[...]).astype(BF16)

    @pl.when(at_end(devices))
    def _():
        sums, masses = refs[2:4]
        finish(sums[y_rows, :] * (1.0 / lane_sum(masses[y_rows, :])))

    @pl.when(~at_end(devices))
    def _():
        sums, masses = refs[:2]
        mass = lane_sum(masses[x_rows, :]) + lane_sum(recv_ref[:, width:])
        joined = (sums[x_rows, :] + recv_ref[:, :width].astype(F32)) * (1.0 / mass)
        own = sums[y_rows, :] * (1.0 / lane_sum(masses[y_rows, :]))
        finish(jnp.where(meta_ref[pl.ds(SPLIT, 1), :] != 0, own, joined))


def join_kernel(normed_ref, other_ref, out_ref):
    count = normed_ref.shape[0]
    for half in range(2):

        @pl.when(lax.axis_index("feat") == half)
        def _():
            out_ref[pl.ds(half * count, count), :] = normed_ref[...]
            out_ref[pl.ds((1 - half) * count, count), :] = other_ref[...]


def on_device(tokens, shot_starts, seed_offsets, norm_gain, proj_weight):
    rows, width = tokens.shape
    count = seed_offsets.shape[1]
    reach = 3 * rows // 8
    devices = lax.axis_size(AXES)
    across = [(i, i + 1) for i in range(1, devices - 1, 2)]
    across += [(target, source) for source, target in across]
    across += [(0, devices - 1), (devices - 1, 0)]
    pair = [(0, 1), (1, 0)]

    def shape(*dims, dtype=BF16):
        return jax.ShapeDtypeStruct(dims, dtype)

    def in_hbm(array):
        return pltpu.with_memory_space_constraint(array, pltpu.HBM)

    far_tokens = in_hbm(tokens)
    first, own, tail, share, meta, edge = pl.pallas_call(
        functools.partial(seed_kernel, reach),
        out_shape=(
            shape(count, width),
            shape(count, width),
            shape(count, width),
            shape(2, width),
            shape(8, width, dtype=jnp.int32),
            shape(reach - TILE, width),
        ),
        in_specs=[HBM_SPEC] * 3,
        out_specs=[VMEM_SPEC] * 6,
        scratch_shapes=[
            pltpu.SMEM(shot_starts.shape, jnp.int32),
            pltpu.SMEM(seed_offsets.shape, jnp.int32),
            pltpu.VMEM(seed_offsets.shape, jnp.int32),
            pltpu.VMEM((16 * count, width), BF16),
            pltpu.SemaphoreType.DMA((3,)),
            pltpu.SemaphoreType.DMA(()),
            pltpu.SemaphoreType.DMA(()),
        ],
        compiler_params=pltpu.CompilerParams(vmem_limit_bytes=16 << 20),
        name="seeds",
    )(in_hbm(shot_starts), in_hbm(seed_offsets), far_tokens)
    given = lax.ppermute(tail, "feat", pair)

    def fetch(kernel, size, after, name):
        return pl.pallas_call(
            kernel,
            out_shape=shape(size, width),
            in_specs=[HBM_SPEC, VMEM_SPEC],
            out_specs=VMEM_SPEC,
            scratch_shapes=[pltpu.SemaphoreType.DMA((4,))],
            compiler_params=pltpu.CompilerParams(vmem_limit_bytes=16 << 20),
            name=name,
        )(far_tokens, after)

    edge_last = fetch(functools.partial(strip_kernel, reach), TILE, tail, "strip")
    edge, edge_last = lax.optimization_barrier((edge, edge_last))
    edge = lax.ppermute(edge, "feat", pair)
    x = first + given * share[:1]
    y = own + given * share[1:]
    edge_last, _ = lax.optimization_barrier((edge_last, x))
    edge_last = lax.ppermute(edge_last, "feat", pair)
    received = lax.ppermute(x, AXES, across)
    near_tokens = fetch(load_kernel, rows, x, "load")

    def pool(first, ends, *state):
        outs = (shape(2 * count, width, dtype=F32), shape(2 * count, LANES, dtype=F32))
        outs += () if ends else (shape(count, width + LANES),)
        return pl.pallas_call(
            functools.partial(pool_kernel, first, ends, devices),
            out_shape=outs,
            in_specs=[VMEM_SPEC] * 8,
            out_specs=[VMEM_SPEC] * len(outs),
            scratch_shapes=[pltpu.VMEM((2 * count, width), BF16)],
            compiler_params=pltpu.CompilerParams(vmem_limit_bytes=16 << 20),
            name="ends" if ends else "pool",
        )(meta, near_tokens, edge, edge_last, *state)

    sums, masses, send = pool(True, False, x, received, y, y)
    start = received
    received = lax.ppermute(send, AXES, across)
    end_sums, end_masses = pool(True, True, x, start, y, masses)
    for _ in range(ITERS - 1):
        before = received
        sums, masses, send = pool(False, False, sums, masses, before, end_masses)
        received = lax.ppermute(send, AXES, across)
        end_sums, end_masses = pool(False, True, end_sums, end_masses, before, masses)
    normed = pl.pallas_call(
        functools.partial(norm_kernel, devices),
        out_shape=shape(count, width),
        in_specs=[VMEM_SPEC] * 7,
        out_specs=VMEM_SPEC,
        compiler_params=pltpu.CompilerParams(vmem_limit_bytes=8 << 20),
        name="norm",
    )(meta, norm_gain[None, :], received, sums, masses, end_sums, end_masses)
    both = pl.pallas_call(
        join_kernel,
        out_shape=shape(2 * count, width),
        in_specs=[VMEM_SPEC] * 2,
        out_specs=VMEM_SPEC,
        compiler_params=pltpu.CompilerParams(vmem_limit_bytes=8 << 20),
        name="join",
    )(normed, lax.ppermute(normed, "feat", pair))
    return jnp.dot(both, proj_weight, preferred_element_type=F32).astype(BF16)


def solution(mesh):
    in_specs = (P(AXES, None), P(), P(), P(), P(None, "feat"))
    out_specs = P("seq", "feat")
    return jax.shard_map(
        on_device, mesh=mesh, in_specs=in_specs, out_specs=out_specs, check_vma=False
    )
```

```python
import functools
import math

import jax
import jax.numpy as jnp
from jax import lax
from jax.experimental import pallas as pl
from jax.experimental.pallas import tpu as pltpu
from jax.sharding import PartitionSpec as P

ITERS = 3
AXES = ("seq", "feat")
LANES = 128
TILE = 512
F32 = jnp.float32
BF16 = jnp.bfloat16
VMEM_SPEC = pl.BlockSpec(memory_space=pltpu.VMEM)
HBM_SPEC = pl.BlockSpec(memory_space=pltpu.HBM)
X_LOW, X_HIGH, Y_LOW, Y_HIGH, EDGE, SPLIT, OCCUPIED, UNUSED = range(8)


def start_of(starts_ref, shot, shots, total):
    first = starts_ref[jnp.minimum(shot, shots - 1)]
    return jnp.where(shot >= shots, total, first)


def column_of(row):
    n = row.shape[1]
    diagonal = lax.broadcasted_iota(jnp.int32, (n, n), 0) == lax.broadcasted_iota(
        jnp.int32, (n, n), 1
    )
    spread = jnp.where(diagonal, jnp.broadcast_to(row, (n, n)), 0)
    return jnp.sum(spread, axis=1, keepdims=True)


def seed_kernel(
    reach,
    starts_hbm,
    seeds_hbm,
    tokens_ref,
    first_ref,
    own_ref,
    tail_ref,
    share_ref,
    meta_ref,
    edge_ref,
    starts_ref,
    seeds_ref,
    seed_rows_ref,
    picked,
    index_sems,
    pick_sem,
    edge_sem,
):
    rows, width = tokens_ref.shape
    shots, count = seeds_ref.shape
    total = shots * rows
    index = lax.axis_index(AXES)
    second = index % 2 == 1
    base = index * rows
    indices = [
        pltpu.make_async_copy(starts_hbm, starts_ref, index_sems.at[0]),
        pltpu.make_async_copy(seeds_hbm, seeds_ref, index_sems.at[1]),
        pltpu.make_async_copy(seeds_hbm, seed_rows_ref, index_sems.at[2]),
    ]
    for copy in indices:
        copy.start()
    strip_low = pl.multiple_of(jnp.where(second, 0, rows - reach), 8)
    strip = pltpu.make_async_copy(
        tokens_ref.at[pl.ds(strip_low, edge_ref.shape[0]), :], edge_ref, edge_sem
    )
    strip.start()
    for copy in indices:
        copy.wait()
    following = jnp.minimum(index + 1, shots - 1)
    here = start_of(starts_ref, index, shots, total)
    after = start_of(starts_ref, index + 1, shots, total)

    def fetch(k, carry):
        for which, (shot, begin) in enumerate(((index, here), (following, after))):
            place = begin + seeds_ref[shot, k] - base
            slot = pl.multiple_of((which * count + k) * 8, 8)
            here_too = (place >= 0) & (place < rows)
            group = pl.multiple_of(jnp.where(here_too, (place // 8) * 8, slot), 8)
            pltpu.make_async_copy(
                tokens_ref.at[pl.ds(group, 8), :], picked.at[pl.ds(slot, 8), :], pick_sem
            ).start()
        return carry

    lax.fori_loop(0, count, fetch, 0, unroll=8)

    low = jnp.where(second, here - base, 0)
    high = jnp.where(second, rows, after - base)
    cut = jnp.where(second, after - base, here - base)
    split = jnp.where(second, after <= base + rows, here > base) | (index == 0)
    x_low = jnp.where(split & second, cut, low)
    x_high = jnp.where(split & ~second, cut, high)
    y_low = jnp.where(split, jnp.where(second, low, cut), high)
    y_high = jnp.where(split, jnp.where(second, cut, high), high)
    table = {
        X_LOW: x_low,
        X_HIGH: x_high,
        Y_LOW: y_low,
        Y_HIGH: y_high,
        EDGE: jnp.where(second, -reach, rows),
        SPLIT: split.astype(jnp.int32),
        OCCUPIED: (x_low < x_high).astype(jnp.int32),
        UNUSED: 0,
    }
    for row, value in table.items():
        meta_ref[pl.ds(row, 1), :] = jnp.full((1, width), value, jnp.int32)
    lends = jnp.where(second, 1.0, 0.0)
    row = lax.broadcasted_iota(jnp.int32, share_ref.shape, 0)
    share_ref[...] = jnp.where(row == 0, jnp.where(split, 0.0, lends), lends).astype(BF16)

    choices = []
    for shot, begin in ((index, here), (following, after)):
        place = column_of(seed_rows_ref[pl.ds(shot, 1), :]) + (begin - base)
        valid = (place >= 0) & (place < rows)
        target = lax.broadcasted_iota(jnp.int32, (count, 1), 0) * 8 + place % 8
        lane = lax.broadcasted_iota(jnp.int32, (count, 8 * count), 1)
        choices.append(jnp.where(valid & (lane == target), 1.0, 0.0).astype(BF16))
    pltpu.make_async_copy(tokens_ref.at[pl.ds(0, 16 * count), :], picked, pick_sem).wait()
    own, tail = (
        jnp.dot(
            choose,
            picked[pl.ds(which * 8 * count, 8 * count), :],
            preferred_element_type=F32,
        )
        for which, choose in enumerate(choices)
    )
    first_ref[...] = jnp.where(split, jnp.where(second, tail, 0.0), own).astype(BF16)
    own_ref[...] = own.astype(BF16)
    tail_ref[...] = tail.astype(BF16)
    strip.wait()


def copy_pieces(tokens_ref, low, out_ref, sems):
    pieces = sems.shape[0]
    piece = out_ref.shape[0] // pieces
    copies = [
        pltpu.make_async_copy(
            tokens_ref.at[pl.ds(pl.multiple_of(low + i * piece, 8), piece), :],
            out_ref.at[pl.ds(i * piece, piece), :],
            sems.at[i],
        )
        for i in range(pieces)
    ]
    for copy in copies:
        copy.start()
    for copy in copies:
        copy.wait()


def strip_kernel(reach, tokens_ref, order_ref, out_ref, sems):
    size = out_ref.shape[0]
    second = lax.axis_index(AXES) % 2 == 1
    low = jnp.where(second, reach - size, tokens_ref.shape[0] - size)
    copy_pieces(tokens_ref, low, out_ref, sems)


def load_kernel(tokens_ref, order_ref, out_ref, sems):
    copy_pieces(tokens_ref, 0, out_ref, sems)


def at_end(devices):
    index = lax.axis_index(AXES)
    return (index == 0) | (index == devices - 1)


def lane_sum(block):
    return jnp.sum(block.astype(F32), axis=1, keepdims=True)


def pool_kernel(first, ends, devices, *refs):
    @pl.when(at_end(devices) == ends)
    def _():
        pool_body(first, ends, *refs)


def pool_body(first, ends, meta_ref, tokens_ref, *refs):
    edge_refs, refs = refs[:2], refs[2:]
    if first:
        (x_ref, recv_ref, y_ref, _), refs = refs[:4], refs[4:]
        count, width = y_ref.shape
    else:
        (old_ref, old_mass_ref, recv_ref, _), refs = refs[:4], refs[4:]
        count, width = recv_ref.shape[0], old_ref.shape[1]
    sums, masses, *send_out, centroids = refs
    rows = tokens_ref.shape[0]
    scale = math.log2(math.e) / math.sqrt(width)
    x_rows, y_rows = pl.ds(0, count), pl.ds(count, count)

    occupied = meta_ref[pl.ds(OCCUPIED, 1), :] != 0
    if first:
        joined = x_ref[...] + recv_ref[...]
        centroids[x_rows, :] = jnp.where(occupied, joined, jnp.zeros_like(joined))
        centroids[y_rows, :] = y_ref[...]
    else:
        mass = lane_sum(old_mass_ref[x_rows, :]) + lane_sum(recv_ref[:, width:])
        joined = (old_ref[x_rows, :] + recv_ref[:, :width].astype(F32)) * (1.0 / mass)
        centroids[x_rows, :] = jnp.where(occupied, joined, 0.0).astype(BF16)
        mass = lane_sum(old_mass_ref[y_rows, :])
        centroids[y_rows, :] = (old_ref[y_rows, :] * (1.0 / mass)).astype(BF16)

    tiles = [(tokens_ref, i * TILE, i * TILE, False) for i in range(rows // TILE)]
    begin = 0
    for ref in edge_refs:
        tiles += [(ref, i * TILE, begin + i * TILE, True) for i in range(ref.shape[0] // TILE)]
        begin += ref.shape[0]

    def scores_of(tile):
        ref, row, _, _ = tile
        return lax.dot_general(
            centroids[...],
            ref[pl.ds(row, TILE), :],
            (((1,), (1,)), ((), ())),
            preferred_element_type=F32,
        )

    def weights_of(tile, scores):
        _, _, begin, on_edge = tile
        place = begin + lax.broadcasted_iota(jnp.int32, (1, TILE), 1)
        if on_edge:
            place = place + meta_ref[pl.ds(EDGE, 1), :TILE]
        bound = [meta_ref[pl.ds(i, 1), :TILE] for i in (X_LOW, X_HIGH, Y_LOW, Y_HIGH)]
        in_x = (place >= bound[0]) & (place < bound[1])
        in_y = (place >= bound[2]) & (place < bound[3])
        mine = jnp.where(in_y, scores[count:], scores[:count])
        top = jnp.max(mine, axis=0, keepdims=True)
        powers = jnp.exp2((mine - top) * scale)
        inverse = 1.0 / jnp.sum(powers, axis=0, keepdims=True)
        return jnp.concatenate(
            [powers * jnp.where(in_x, inverse, 0.0), powers * jnp.where(in_y, inverse, 0.0)], axis=0
        )

    scores = scores_of(tiles[0])
    for at, tile in enumerate(tiles):
        upcoming = scores_of(tiles[at + 1]) if at + 1 < len(tiles) else None
        weights = weights_of(tile, scores)
        part = weights[:, :LANES]
        for i in range(1, TILE // LANES):
            part = part + weights[:, i * LANES : (i + 1) * LANES]
        added = jnp.dot(
            weights.astype(BF16), tile[0][pl.ds(tile[1], TILE), :], preferred_element_type=F32
        )
        if at == 0:
            masses[...] = part
            sums[...] = added
        else:
            masses[...] += part
            sums[...] += added
        scores = upcoming

    if ends:
        return
    (send_out,) = send_out
    mass = lane_sum(masses[x_rows, :])
    send_out[:, :width] = sums[x_rows, :].astype(BF16)
    high = mass.astype(BF16).astype(F32)
    middle = (mass - high).astype(BF16).astype(F32)
    low = mass - high - middle
    lane = lax.broadcasted_iota(jnp.int32, (count, LANES), 1)
    block = jnp.where(
        lane == 0, high, jnp.where(lane == 1, middle, jnp.where(lane == 2, low, 0.0))
    )
    send_out[:, width:] = block.astype(BF16)


def norm_kernel(devices, meta_ref, gain_ref, recv_ref, *refs):
    out_ref = refs[-1]
    count, width = out_ref.shape
    x_rows, y_rows = pl.ds(0, count), pl.ds(count, count)

    def finish(centroid):
        spread = jnp.sqrt(jnp.mean(centroid * centroid, axis=-1, keepdims=True) + 1e-06)
        out_ref[...] = (centroid * (1.0 / spread) * gain_ref[...]).astype(BF16)

    @pl.when(at_end(devices))
    def _():
        sums, masses = refs[2:4]
        finish(sums[y_rows, :] * (1.0 / lane_sum(masses[y_rows, :])))

    @pl.when(~at_end(devices))
    def _():
        sums, masses = refs[:2]
        mass = lane_sum(masses[x_rows, :]) + lane_sum(recv_ref[:, width:])
        joined = (sums[x_rows, :] + recv_ref[:, :width].astype(F32)) * (1.0 / mass)
        own = sums[y_rows, :] * (1.0 / lane_sum(masses[y_rows, :]))
        finish(jnp.where(meta_ref[pl.ds(SPLIT, 1), :] != 0, own, joined))


def join_kernel(normed_ref, other_ref, out_ref):
    count = normed_ref.shape[0]
    for half in range(2):

        @pl.when(lax.axis_index("feat") == half)
        def _():
            out_ref[pl.ds(half * count, count), :] = normed_ref[...]
            out_ref[pl.ds((1 - half) * count, count), :] = other_ref[...]


def on_device(tokens, shot_starts, seed_offsets, norm_gain, proj_weight):
    rows, width = tokens.shape
    count = seed_offsets.shape[1]
    reach = 3 * rows // 8
    devices = lax.axis_size(AXES)
    across = [(i, i + 1) for i in range(1, devices - 1, 2)]
    across += [(target, source) for source, target in across]
    across += [(0, devices - 1), (devices - 1, 0)]
    pair = [(0, 1), (1, 0)]

    def shape(*dims, dtype=BF16):
        return jax.ShapeDtypeStruct(dims, dtype)

    def in_hbm(array):
        return pltpu.with_memory_space_constraint(array, pltpu.HBM)

    far_tokens = in_hbm(tokens)
    first, own, tail, share, meta, edge = pl.pallas_call(
        functools.partial(seed_kernel, reach),
        out_shape=(
            shape(count, width),
            shape(count, width),
            shape(count, width),
            shape(2, width),
            shape(8, width, dtype=jnp.int32),
            shape(reach - TILE, width),
        ),
        in_specs=[HBM_SPEC] * 3,
        out_specs=[VMEM_SPEC] * 6,
        scratch_shapes=[
            pltpu.SMEM(shot_starts.shape, jnp.int32),
            pltpu.SMEM(seed_offsets.shape, jnp.int32),
            pltpu.VMEM(seed_offsets.shape, jnp.int32),
            pltpu.VMEM((16 * count, width), BF16),
            pltpu.SemaphoreType.DMA((3,)),
            pltpu.SemaphoreType.DMA(()),
            pltpu.SemaphoreType.DMA(()),
        ],
        compiler_params=pltpu.CompilerParams(vmem_limit_bytes=16 << 20),
        name="seeds",
    )(in_hbm(shot_starts), in_hbm(seed_offsets), far_tokens)
    given = lax.ppermute(tail, "feat", pair)

    def fetch(kernel, size, after, name):
        return pl.pallas_call(
            kernel,
            out_shape=shape(size, width),
            in_specs=[HBM_SPEC, VMEM_SPEC],
            out_specs=VMEM_SPEC,
            scratch_shapes=[pltpu.SemaphoreType.DMA((4,))],
            compiler_params=pltpu.CompilerParams(vmem_limit_bytes=16 << 20),
            name=name,
        )(far_tokens, after)

    edge_last = fetch(functools.partial(strip_kernel, reach), TILE, tail, "strip")
    edge, edge_last, given = lax.optimization_barrier((edge, edge_last, given))
    edge = lax.ppermute(edge, "feat", pair)
    x = first + given * share[:1]
    y = own + given * share[1:]
    edge_last, _ = lax.optimization_barrier((edge_last, x))
    edge_last = lax.ppermute(edge_last, "feat", pair)
    received = lax.ppermute(x, AXES, across)
    near_tokens = fetch(load_kernel, rows, x, "load")

    def pool(first, ends, *state):
        outs = (shape(2 * count, width, dtype=F32), shape(2 * count, LANES, dtype=F32))
        outs += () if ends else (shape(count, width + LANES),)
        return pl.pallas_call(
            functools.partial(pool_kernel, first, ends, devices),
            out_shape=outs,
            in_specs=[VMEM_SPEC] * 8,
            out_specs=[VMEM_SPEC] * len(outs),
            scratch_shapes=[pltpu.VMEM((2 * count, width), BF16)],
            compiler_params=pltpu.CompilerParams(vmem_limit_bytes=16 << 20),
            name="ends" if ends else "pool",
        )(meta, near_tokens, edge, edge_last, *state)

    sums, masses, send = pool(True, False, x, received, y, y)
    start = received
    received = lax.ppermute(send, AXES, across)
    end_sums, end_masses = pool(True, True, x, start, y, masses)
    for _ in range(ITERS - 1):
        before = received
        sums, masses, send = pool(False, False, sums, masses, before, end_masses)
        received = lax.ppermute(send, AXES, across)
        end_sums, end_masses = pool(False, True, end_sums, end_masses, before, masses)
    normed = pl.pallas_call(
        functools.partial(norm_kernel, devices),
        out_shape=shape(count, width),
        in_specs=[VMEM_SPEC] * 7,
        out_specs=VMEM_SPEC,
        compiler_params=pltpu.CompilerParams(vmem_limit_bytes=8 << 20),
        name="norm",
    )(meta, norm_gain[None, :], received, sums, masses, end_sums, end_masses)
    both = pl.pallas_call(
        join_kernel,
        out_shape=shape(2 * count, width),
        in_specs=[VMEM_SPEC] * 2,
        out_specs=VMEM_SPEC,
        compiler_params=pltpu.CompilerParams(vmem_limit_bytes=8 << 20),
        name="join",
    )(normed, lax.ppermute(normed, "feat", pair))
    return jnp.dot(both, proj_weight, preferred_element_type=F32).astype(BF16)


def solution(mesh):
    in_specs = (P(AXES, None), P(), P(), P(), P(None, "feat"))
    out_specs = P("seq", "feat")
    return jax.shard_map(
        on_device, mesh=mesh, in_specs=in_specs, out_specs=out_specs, check_vma=False
    )
```

```python
import functools
import math

import jax
import jax.numpy as jnp
from jax import lax
from jax.experimental import pallas as pl
from jax.experimental.pallas import tpu as pltpu
from jax.sharding import PartitionSpec as P

ITERS = 3
AXES = ("seq", "feat")
LANES = 128
TILE = 512
F32 = jnp.float32
BF16 = jnp.bfloat16
VMEM_SPEC = pl.BlockSpec(memory_space=pltpu.VMEM)
HBM_SPEC = pl.BlockSpec(memory_space=pltpu.HBM)
X_LOW, X_HIGH, Y_LOW, Y_HIGH, EDGE, SPLIT, OCCUPIED, UNUSED = range(8)


def start_of(starts_ref, shot, shots, total):
    first = starts_ref[jnp.minimum(shot, shots - 1)]
    return jnp.where(shot >= shots, total, first)


def column_of(row):
    n = row.shape[1]
    diagonal = lax.broadcasted_iota(jnp.int32, (n, n), 0) == lax.broadcasted_iota(
        jnp.int32, (n, n), 1
    )
    spread = jnp.where(diagonal, jnp.broadcast_to(row, (n, n)), 0)
    return jnp.sum(spread, axis=1, keepdims=True)


def seed_kernel(
    starts_hbm,
    seeds_hbm,
    tokens_ref,
    first_ref,
    own_ref,
    tail_ref,
    share_ref,
    meta_ref,
    edge_ref,
    starts_ref,
    seeds_ref,
    seed_rows_ref,
    picked,
    index_sems,
    pick_sem,
    edge_sems,
):
    rows, width = tokens_ref.shape
    reach = edge_ref.shape[0]
    shots, count = seeds_ref.shape
    total = shots * rows
    index = lax.axis_index(AXES)
    second = index % 2 == 1
    base = index * rows
    indices = [
        pltpu.make_async_copy(starts_hbm, starts_ref, index_sems.at[0]),
        pltpu.make_async_copy(seeds_hbm, seeds_ref, index_sems.at[1]),
        pltpu.make_async_copy(seeds_hbm, seed_rows_ref, index_sems.at[2]),
    ]
    for copy in indices:
        copy.start()
    strip_low = jnp.where(second, 0, rows - reach)
    strip = [
        pltpu.make_async_copy(
            tokens_ref.at[pl.ds(pl.multiple_of(strip_low + begin, 8), size), :],
            edge_ref.at[pl.ds(begin, size), :],
            edge_sems.at[at],
        )
        for at, (begin, size) in enumerate(((0, reach - TILE), (reach - TILE, TILE)))
    ]
    strip[0].start()
    for copy in indices:
        copy.wait()
    following = jnp.minimum(index + 1, shots - 1)
    here = start_of(starts_ref, index, shots, total)
    after = start_of(starts_ref, index + 1, shots, total)

    def fetch(k, carry):
        for which, (shot, begin) in enumerate(((index, here), (following, after))):
            place = begin + seeds_ref[shot, k] - base
            slot = pl.multiple_of((which * count + k) * 8, 8)
            here_too = (place >= 0) & (place < rows)
            group = pl.multiple_of(jnp.where(here_too, (place // 8) * 8, slot), 8)
            pltpu.make_async_copy(
                tokens_ref.at[pl.ds(group, 8), :], picked.at[pl.ds(slot, 8), :], pick_sem
            ).start()
        return carry

    lax.fori_loop(0, count, fetch, 0, unroll=8)
    strip[1].start()

    low = jnp.where(second, here - base, 0)
    high = jnp.where(second, rows, after - base)
    cut = jnp.where(second, after - base, here - base)
    split = jnp.where(second, after <= base + rows, here > base) | (index == 0)
    x_low = jnp.where(split & second, cut, low)
    x_high = jnp.where(split & ~second, cut, high)
    y_low = jnp.where(split, jnp.where(second, low, cut), high)
    y_high = jnp.where(split, jnp.where(second, cut, high), high)
    table = {
        X_LOW: x_low,
        X_HIGH: x_high,
        Y_LOW: y_low,
        Y_HIGH: y_high,
        EDGE: jnp.where(second, -reach, rows),
        SPLIT: split.astype(jnp.int32),
        OCCUPIED: (x_low < x_high).astype(jnp.int32),
        UNUSED: 0,
    }
    for row, value in table.items():
        meta_ref[pl.ds(row, 1), :] = jnp.full((1, width), value, jnp.int32)
    lends = jnp.where(second, 1.0, 0.0)
    row = lax.broadcasted_iota(jnp.int32, share_ref.shape, 0)
    share_ref[...] = jnp.where(row == 0, jnp.where(split, 0.0, lends), lends).astype(BF16)

    choices = []
    for shot, begin in ((index, here), (following, after)):
        place = column_of(seed_rows_ref[pl.ds(shot, 1), :]) + (begin - base)
        valid = (place >= 0) & (place < rows)
        target = lax.broadcasted_iota(jnp.int32, (count, 1), 0) * 8 + place % 8
        lane = lax.broadcasted_iota(jnp.int32, (count, 8 * count), 1)
        choices.append(jnp.where(valid & (lane == target), 1.0, 0.0).astype(BF16))
    pltpu.make_async_copy(tokens_ref.at[pl.ds(0, 16 * count), :], picked, pick_sem).wait()
    own, tail = (
        jnp.dot(
            choose,
            picked[pl.ds(which * 8 * count, 8 * count), :],
            preferred_element_type=F32,
        )
        for which, choose in enumerate(choices)
    )
    first_ref[...] = jnp.where(split, jnp.where(second, tail, 0.0), own).astype(BF16)
    own_ref[...] = own.astype(BF16)
    tail_ref[...] = tail.astype(BF16)
    for copy in strip:
        copy.wait()


def copy_pieces(tokens_ref, low, out_ref, sems):
    pieces = sems.shape[0]
    piece = out_ref.shape[0] // pieces
    copies = [
        pltpu.make_async_copy(
            tokens_ref.at[pl.ds(pl.multiple_of(low + i * piece, 8), piece), :],
            out_ref.at[pl.ds(i * piece, piece), :],
            sems.at[i],
        )
        for i in range(pieces)
    ]
    for copy in copies:
        copy.start()
    for copy in copies:
        copy.wait()


def load_kernel(tokens_ref, order_ref, out_ref, sems):
    copy_pieces(tokens_ref, 0, out_ref, sems)


def at_end(devices):
    index = lax.axis_index(AXES)
    return (index == 0) | (index == devices - 1)


def lane_sum(block):
    return jnp.sum(block.astype(F32), axis=1, keepdims=True)


def pool_kernel(first, ends, devices, *refs):
    @pl.when(at_end(devices) == ends)
    def _():
        pool_body(first, ends, *refs)


def pool_body(first, ends, meta_ref, tokens_ref, edge_ref, *refs):
    if first:
        (x_ref, recv_ref, y_ref, _), refs = refs[:4], refs[4:]
        count, width = y_ref.shape
    else:
        (old_ref, old_mass_ref, recv_ref, _), refs = refs[:4], refs[4:]
        count, width = recv_ref.shape[0], old_ref.shape[1]
    sums, masses, *send_out, centroids = refs
    rows = tokens_ref.shape[0]
    reach = edge_ref.shape[0]
    scale = math.log2(math.e) / math.sqrt(width)
    x_rows, y_rows = pl.ds(0, count), pl.ds(count, count)

    occupied = meta_ref[pl.ds(OCCUPIED, 1), :] != 0
    if first:
        joined = x_ref[...] + recv_ref[...]
        centroids[x_rows, :] = jnp.where(occupied, joined, jnp.zeros_like(joined))
        centroids[y_rows, :] = y_ref[...]
    else:
        mass = lane_sum(old_mass_ref[x_rows, :]) + lane_sum(recv_ref[:, width:])
        joined = (old_ref[x_rows, :] + recv_ref[:, :width].astype(F32)) * (1.0 / mass)
        centroids[x_rows, :] = jnp.where(occupied, joined, 0.0).astype(BF16)
        mass = lane_sum(old_mass_ref[y_rows, :])
        centroids[y_rows, :] = (old_ref[y_rows, :] * (1.0 / mass)).astype(BF16)

    tiles = [(tokens_ref, i * TILE) for i in range(rows // TILE)]
    tiles += [(edge_ref, i * TILE) for i in range(reach // TILE)]

    def scores_of(tile):
        ref, row = tile
        return lax.dot_general(
            centroids[...],
            ref[pl.ds(row, TILE), :],
            (((1,), (1,)), ((), ())),
            preferred_element_type=F32,
        )

    def weights_of(tile, scores):
        ref, row = tile
        place = row + lax.broadcasted_iota(jnp.int32, (1, TILE), 1)
        if ref is edge_ref:
            place = place + meta_ref[pl.ds(EDGE, 1), :TILE]
        bound = [meta_ref[pl.ds(i, 1), :TILE] for i in (X_LOW, X_HIGH, Y_LOW, Y_HIGH)]
        in_x = (place >= bound[0]) & (place < bound[1])
        in_y = (place >= bound[2]) & (place < bound[3])
        mine = jnp.where(in_y, scores[count:], scores[:count])
        top = jnp.max(mine, axis=0, keepdims=True)
        powers = jnp.exp2((mine - top) * scale)
        inverse = 1.0 / jnp.sum(powers, axis=0, keepdims=True)
        return jnp.concatenate(
            [powers * jnp.where(in_x, inverse, 0.0), powers * jnp.where(in_y, inverse, 0.0)], axis=0
        )

    scores = scores_of(tiles[0])
    for at, tile in enumerate(tiles):
        upcoming = scores_of(tiles[at + 1]) if at + 1 < len(tiles) else None
        weights = weights_of(tile, scores)
        part = weights[:, :LANES]
        for i in range(1, TILE // LANES):
            part = part + weights[:, i * LANES : (i + 1) * LANES]
        added = jnp.dot(
            weights.astype(BF16), tile[0][pl.ds(tile[1], TILE), :], preferred_element_type=F32
        )
        if at == 0:
            masses[...] = part
            sums[...] = added
        else:
            masses[...] += part
            sums[...] += added
        scores = upcoming

    if ends:
        return
    (send_out,) = send_out
    mass = lane_sum(masses[x_rows, :])
    send_out[:, :width] = sums[x_rows, :].astype(BF16)
    high = mass.astype(BF16).astype(F32)
    middle = (mass - high).astype(BF16).astype(F32)
    low = mass - high - middle
    lane = lax.broadcasted_iota(jnp.int32, (count, LANES), 1)
    block = jnp.where(
        lane == 0, high, jnp.where(lane == 1, middle, jnp.where(lane == 2, low, 0.0))
    )
    send_out[:, width:] = block.astype(BF16)


def norm_kernel(devices, meta_ref, gain_ref, recv_ref, *refs):
    out_ref = refs[-1]
    count, width = out_ref.shape
    x_rows, y_rows = pl.ds(0, count), pl.ds(count, count)

    def finish(centroid):
        spread = jnp.sqrt(jnp.mean(centroid * centroid, axis=-1, keepdims=True) + 1e-06)
        out_ref[...] = (centroid * (1.0 / spread) * gain_ref[...]).astype(BF16)

    @pl.when(at_end(devices))
    def _():
        sums, masses = refs[2:4]
        finish(sums[y_rows, :] * (1.0 / lane_sum(masses[y_rows, :])))

    @pl.when(~at_end(devices))
    def _():
        sums, masses = refs[:2]
        mass = lane_sum(masses[x_rows, :]) + lane_sum(recv_ref[:, width:])
        joined = (sums[x_rows, :] + recv_ref[:, :width].astype(F32)) * (1.0 / mass)
        own = sums[y_rows, :] * (1.0 / lane_sum(masses[y_rows, :]))
        finish(jnp.where(meta_ref[pl.ds(SPLIT, 1), :] != 0, own, joined))


def join_kernel(normed_ref, other_ref, out_ref):
    count = normed_ref.shape[0]
    for half in range(2):

        @pl.when(lax.axis_index("feat") == half)
        def _():
            out_ref[pl.ds(half * count, count), :] = normed_ref[...]
            out_ref[pl.ds((1 - half) * count, count), :] = other_ref[...]


def on_device(tokens, shot_starts, seed_offsets, norm_gain, proj_weight):
    rows, width = tokens.shape
    count = seed_offsets.shape[1]
    reach = 3 * rows // 8
    devices = lax.axis_size(AXES)
    across = [(i, i + 1) for i in range(1, devices - 1, 2)]
    across += [(target, source) for source, target in across]
    across += [(0, devices - 1), (devices - 1, 0)]
    pair = [(0, 1), (1, 0)]

    def shape(*dims, dtype=BF16):
        return jax.ShapeDtypeStruct(dims, dtype)

    def in_hbm(array):
        return pltpu.with_memory_space_constraint(array, pltpu.HBM)

    far_tokens = in_hbm(tokens)
    first, own, tail, share, meta, edge = pl.pallas_call(
        seed_kernel,
        out_shape=(
            shape(count, width),
            shape(count, width),
            shape(count, width),
            shape(2, width),
            shape(8, width, dtype=jnp.int32),
            shape(reach, width),
        ),
        in_specs=[HBM_SPEC] * 3,
        out_specs=[VMEM_SPEC] * 6,
        scratch_shapes=[
            pltpu.SMEM(shot_starts.shape, jnp.int32),
            pltpu.SMEM(seed_offsets.shape, jnp.int32),
            pltpu.VMEM(seed_offsets.shape, jnp.int32),
            pltpu.VMEM((16 * count, width), BF16),
            pltpu.SemaphoreType.DMA((3,)),
            pltpu.SemaphoreType.DMA(()),
            pltpu.SemaphoreType.DMA((2,)),
        ],
        compiler_params=pltpu.CompilerParams(vmem_limit_bytes=16 << 20),
        name="seeds",
    )(in_hbm(shot_starts), in_hbm(seed_offsets), far_tokens)
    given = lax.ppermute(tail, "feat", pair)

    def fetch(kernel, size, after, name):
        return pl.pallas_call(
            kernel,
            out_shape=shape(size, width),
            in_specs=[HBM_SPEC, VMEM_SPEC],
            out_specs=VMEM_SPEC,
            scratch_shapes=[pltpu.SemaphoreType.DMA((4,))],
            compiler_params=pltpu.CompilerParams(vmem_limit_bytes=16 << 20),
            name=name,
        )(far_tokens, after)

    edge, given = lax.optimization_barrier((edge, given))
    edge = lax.ppermute(edge, "feat", pair)
    x = first + given * share[:1]
    y = own + given * share[1:]
    received = lax.ppermute(x, AXES, across)
    near_tokens = fetch(load_kernel, rows, x, "load")

    def pool(first, ends, *state):
        outs = (shape(2 * count, width, dtype=F32), shape(2 * count, LANES, dtype=F32))
        outs += () if ends else (shape(count, width + LANES),)
        return pl.pallas_call(
            functools.partial(pool_kernel, first, ends, devices),
            out_shape=outs,
            in_specs=[VMEM_SPEC] * 7,
            out_specs=[VMEM_SPEC] * len(outs),
            scratch_shapes=[pltpu.VMEM((2 * count, width), BF16)],
            compiler_params=pltpu.CompilerParams(vmem_limit_bytes=16 << 20),
            name="ends" if ends else "pool",
        )(meta, near_tokens, edge, *state)

    sums, masses, send = pool(True, False, x, received, y, y)
    start = received
    received = lax.ppermute(send, AXES, across)
    end_sums, end_masses = pool(True, True, x, start, y, masses)
    for _ in range(ITERS - 1):
        before = received
        sums, masses, send = pool(False, False, sums, masses, before, end_masses)
        received = lax.ppermute(send, AXES, across)
        end_sums, end_masses = pool(False, True, end_sums, end_masses, before, masses)
    normed = pl.pallas_call(
        functools.partial(norm_kernel, devices),
        out_shape=shape(count, width),
        in_specs=[VMEM_SPEC] * 7,
        out_specs=VMEM_SPEC,
        compiler_params=pltpu.CompilerParams(vmem_limit_bytes=8 << 20),
        name="norm",
    )(meta, norm_gain[None, :], received, sums, masses, end_sums, end_masses)
    both = pl.pallas_call(
        join_kernel,
        out_shape=shape(2 * count, width),
        in_specs=[VMEM_SPEC] * 2,
        out_specs=VMEM_SPEC,
        compiler_params=pltpu.CompilerParams(vmem_limit_bytes=8 << 20),
        name="join",
    )(normed, lax.ppermute(normed, "feat", pair))
    return jnp.dot(both, proj_weight, preferred_element_type=F32).astype(BF16)


def solution(mesh):
    in_specs = (P(AXES, None), P(), P(), P(), P(None, "feat"))
    out_specs = P("seq", "feat")
    return jax.shard_map(
        on_device, mesh=mesh, in_specs=in_specs, out_specs=out_specs, check_vma=False
    )
```

```python
import functools
import math

import jax
import jax.numpy as jnp
from jax import lax
from jax.experimental import pallas as pl
from jax.experimental.pallas import tpu as pltpu
from jax.sharding import PartitionSpec as P

ITERS = 3
AXES = ("seq", "feat")
LANES = 128
TILE = 512
F32 = jnp.float32
BF16 = jnp.bfloat16
VMEM_SPEC = pl.BlockSpec(memory_space=pltpu.VMEM)
HBM_SPEC = pl.BlockSpec(memory_space=pltpu.HBM)
X_LOW, X_HIGH, Y_LOW, Y_HIGH, EDGE, SPLIT, OCCUPIED, UNUSED = range(8)


def start_of(starts_ref, shot, shots, total):
    first = starts_ref[jnp.minimum(shot, shots - 1)]
    return jnp.where(shot >= shots, total, first)


def column_of(row):
    n = row.shape[1]
    diagonal = lax.broadcasted_iota(jnp.int32, (n, n), 0) == lax.broadcasted_iota(
        jnp.int32, (n, n), 1
    )
    spread = jnp.where(diagonal, jnp.broadcast_to(row, (n, n)), 0)
    return jnp.sum(spread, axis=1, keepdims=True)


def seed_kernel(
    starts_hbm,
    seeds_hbm,
    tokens_ref,
    first_ref,
    own_ref,
    tail_ref,
    share_ref,
    meta_ref,
    edge_ref,
    starts_ref,
    seeds_ref,
    seed_rows_ref,
    picked,
    index_sems,
    pick_sem,
    edge_sems,
):
    rows, width = tokens_ref.shape
    reach = edge_ref.shape[0]
    shots, count = seeds_ref.shape
    total = shots * rows
    index = lax.axis_index(AXES)
    second = index % 2 == 1
    base = index * rows
    indices = [
        pltpu.make_async_copy(starts_hbm, starts_ref, index_sems.at[0]),
        pltpu.make_async_copy(seeds_hbm, seeds_ref, index_sems.at[1]),
        pltpu.make_async_copy(seeds_hbm, seed_rows_ref, index_sems.at[2]),
    ]
    for copy in indices:
        copy.start()
    strip_low = jnp.where(second, 0, rows - reach)
    strip = [
        pltpu.make_async_copy(
            tokens_ref.at[pl.ds(pl.multiple_of(strip_low + begin, 8), size), :],
            edge_ref.at[pl.ds(begin, size), :],
            edge_sems.at[at],
        )
        for at, (begin, size) in enumerate(((0, reach - TILE), (reach - TILE, TILE)))
    ]
    strip[0].start()
    for copy in indices:
        copy.wait()
    following = jnp.minimum(index + 1, shots - 1)
    here = start_of(starts_ref, index, shots, total)
    after = start_of(starts_ref, index + 1, shots, total)

    def fetch(k, carry):
        for which, (shot, begin) in enumerate(((index, here), (following, after))):
            place = begin + seeds_ref[shot, k] - base
            slot = pl.multiple_of((which * count + k) * 8, 8)
            here_too = (place >= 0) & (place < rows)
            group = pl.multiple_of(jnp.where(here_too, (place // 8) * 8, slot), 8)
            pltpu.make_async_copy(
                tokens_ref.at[pl.ds(group, 8), :], picked.at[pl.ds(slot, 8), :], pick_sem
            ).start()
        return carry

    lax.fori_loop(0, count, fetch, 0, unroll=8)
    strip[1].start()

    low = jnp.where(second, here - base, 0)
    high = jnp.where(second, rows, after - base)
    cut = jnp.where(second, after - base, here - base)
    split = jnp.where(second, after <= base + rows, here > base) | (index == 0)
    x_low = jnp.where(split & second, cut, low)
    x_high = jnp.where(split & ~second, cut, high)
    y_low = jnp.where(split, jnp.where(second, low, cut), high)
    y_high = jnp.where(split, jnp.where(second, cut, high), high)
    table = {
        X_LOW: x_low,
        X_HIGH: x_high,
        Y_LOW: y_low,
        Y_HIGH: y_high,
        EDGE: jnp.where(second, -reach, rows),
        SPLIT: split.astype(jnp.int32),
        OCCUPIED: (x_low < x_high).astype(jnp.int32),
        UNUSED: 0,
    }
    for row, value in table.items():
        meta_ref[pl.ds(row, 1), :] = jnp.full((1, width), value, jnp.int32)
    lends = jnp.where(second, 1.0, 0.0)
    row = lax.broadcasted_iota(jnp.int32, share_ref.shape, 0)
    share_ref[...] = jnp.where(row == 0, jnp.where(split, 0.0, lends), lends).astype(BF16)

    choices = []
    for shot, begin in ((index, here), (following, after)):
        place = column_of(seed_rows_ref[pl.ds(shot, 1), :]) + (begin - base)
        valid = (place >= 0) & (place < rows)
        target = lax.broadcasted_iota(jnp.int32, (count, 1), 0) * 8 + place % 8
        lane = lax.broadcasted_iota(jnp.int32, (count, 8 * count), 1)
        choices.append(jnp.where(valid & (lane == target), 1.0, 0.0).astype(BF16))
    pltpu.make_async_copy(tokens_ref.at[pl.ds(0, 16 * count), :], picked, pick_sem).wait()
    own, tail = (
        jnp.dot(
            choose,
            picked[pl.ds(which * 8 * count, 8 * count), :],
            preferred_element_type=F32,
        )
        for which, choose in enumerate(choices)
    )
    first_ref[...] = jnp.where(split, jnp.where(second, tail, 0.0), own).astype(BF16)
    own_ref[...] = own.astype(BF16)
    tail_ref[...] = tail.astype(BF16)
    for copy in strip:
        copy.wait()


def copy_pieces(tokens_ref, low, out_ref, sems):
    pieces = sems.shape[0]
    piece = out_ref.shape[0] // pieces
    copies = [
        pltpu.make_async_copy(
            tokens_ref.at[pl.ds(pl.multiple_of(low + i * piece, 8), piece), :],
            out_ref.at[pl.ds(i * piece, piece), :],
            sems.at[i],
        )
        for i in range(pieces)
    ]
    for copy in copies:
        copy.start()
    for copy in copies:
        copy.wait()


def load_kernel(tokens_ref, order_ref, out_ref, sems):
    copy_pieces(tokens_ref, 0, out_ref, sems)


def at_end(devices):
    index = lax.axis_index(AXES)
    return (index == 0) | (index == devices - 1)


def lane_sum(block):
    return jnp.sum(block.astype(F32), axis=1, keepdims=True)


def on_diagonal(count):
    shape = (count, LANES)
    return lax.broadcasted_iota(jnp.int32, shape, 0) == lax.broadcasted_iota(jnp.int32, shape, 1)


def pack(sums, mass, out_ref):
    count, width = sums.shape
    blocks = width // LANES
    for at in range(blocks):
        block = sums[:, at * LANES : (at + 1) * LANES]
        out_ref[pl.ds(at * count, count), :] = block.astype(BF16)
    spread = jnp.sum(jnp.where(on_diagonal(count), mass, 0.0), axis=0, keepdims=True)
    high = spread.astype(BF16).astype(F32)
    middle = (spread - high).astype(BF16).astype(F32)
    low = spread - high - middle
    row = lax.broadcasted_iota(jnp.int32, (8, LANES), 0)
    terms = jnp.where(row == 0, high, jnp.where(row == 1, middle, jnp.where(row == 2, low, 0.0)))
    out_ref[pl.ds(blocks * count, 8), :] = terms.astype(BF16)


def unpack(packed_ref, count, width):
    blocks = width // LANES
    sums = jnp.concatenate(
        [packed_ref[pl.ds(at * count, count), :].astype(F32) for at in range(blocks)], axis=1
    )
    terms = packed_ref[pl.ds(blocks * count, 8), :].astype(F32)
    total = jnp.sum(terms, axis=0, keepdims=True)
    return sums, jnp.sum(jnp.where(on_diagonal(count), total, 0.0), axis=1, keepdims=True)


def pool_kernel(first, ends, devices, *refs):
    @pl.when(at_end(devices) == ends)
    def _():
        pool_body(first, ends, *refs)


def pool_body(first, ends, meta_ref, tokens_ref, edge_ref, *refs):
    if first:
        (x_ref, recv_ref, y_ref, _), refs = refs[:4], refs[4:]
        count, width = y_ref.shape
    else:
        (old_ref, old_mass_ref, recv_ref, _), refs = refs[:4], refs[4:]
        count, width = old_ref.shape[0] // 2, old_ref.shape[1]
    sums, masses, *send_out, centroids = refs
    rows = tokens_ref.shape[0]
    reach = edge_ref.shape[0]
    scale = math.log2(math.e) / math.sqrt(width)
    x_rows, y_rows = pl.ds(0, count), pl.ds(count, count)

    occupied = meta_ref[pl.ds(OCCUPIED, 1), :] != 0
    if first:
        joined = x_ref[...] + recv_ref[...]
        centroids[x_rows, :] = jnp.where(occupied, joined, jnp.zeros_like(joined))
        centroids[y_rows, :] = y_ref[...]
    else:
        other, other_mass = unpack(recv_ref, count, width)
        mass = lane_sum(old_mass_ref[x_rows, :]) + other_mass
        joined = (old_ref[x_rows, :] + other) * (1.0 / mass)
        centroids[x_rows, :] = jnp.where(occupied, joined, 0.0).astype(BF16)
        mass = lane_sum(old_mass_ref[y_rows, :])
        centroids[y_rows, :] = (old_ref[y_rows, :] * (1.0 / mass)).astype(BF16)

    tiles = [(tokens_ref, i * TILE) for i in range(rows // TILE)]
    tiles += [(edge_ref, i * TILE) for i in range(reach // TILE)]

    def scores_of(tile):
        ref, row = tile
        return lax.dot_general(
            centroids[...],
            ref[pl.ds(row, TILE), :],
            (((1,), (1,)), ((), ())),
            preferred_element_type=F32,
        )

    def weights_of(tile, scores):
        ref, row = tile
        place = row + lax.broadcasted_iota(jnp.int32, (1, TILE), 1)
        if ref is edge_ref:
            place = place + meta_ref[pl.ds(EDGE, 1), :TILE]
        bound = [meta_ref[pl.ds(i, 1), :TILE] for i in (X_LOW, X_HIGH, Y_LOW, Y_HIGH)]
        in_x = (place >= bound[0]) & (place < bound[1])
        in_y = (place >= bound[2]) & (place < bound[3])
        mine = jnp.where(in_y, scores[count:], scores[:count])
        top = jnp.max(mine, axis=0, keepdims=True)
        powers = jnp.exp2((mine - top) * scale)
        inverse = 1.0 / jnp.sum(powers, axis=0, keepdims=True)
        return jnp.concatenate(
            [powers * jnp.where(in_x, inverse, 0.0), powers * jnp.where(in_y, inverse, 0.0)], axis=0
        )

    scores = scores_of(tiles[0])
    for at, tile in enumerate(tiles):
        upcoming = scores_of(tiles[at + 1]) if at + 1 < len(tiles) else None
        weights = weights_of(tile, scores)
        part = weights[:, :LANES]
        for i in range(1, TILE // LANES):
            part = part + weights[:, i * LANES : (i + 1) * LANES]
        added = jnp.dot(
            weights.astype(BF16), tile[0][pl.ds(tile[1], TILE), :], preferred_element_type=F32
        )
        if at == 0:
            masses[...] = part
            sums[...] = added
        else:
            masses[...] += part
            sums[...] += added
        scores = upcoming

    if ends:
        return
    (send_out,) = send_out
    pack(sums[x_rows, :], lane_sum(masses[x_rows, :]), send_out)


def norm_kernel(devices, meta_ref, gain_ref, recv_ref, *refs):
    out_ref = refs[-1]
    count, width = out_ref.shape
    x_rows, y_rows = pl.ds(0, count), pl.ds(count, count)

    def finish(centroid):
        spread = jnp.sqrt(jnp.mean(centroid * centroid, axis=-1, keepdims=True) + 1e-06)
        out_ref[...] = (centroid * (1.0 / spread) * gain_ref[...]).astype(BF16)

    @pl.when(at_end(devices))
    def _():
        sums, masses = refs[2:4]
        finish(sums[y_rows, :] * (1.0 / lane_sum(masses[y_rows, :])))

    @pl.when(~at_end(devices))
    def _():
        sums, masses = refs[:2]
        other, other_mass = unpack(recv_ref, count, width)
        mass = lane_sum(masses[x_rows, :]) + other_mass
        joined = (sums[x_rows, :] + other) * (1.0 / mass)
        own = sums[y_rows, :] * (1.0 / lane_sum(masses[y_rows, :]))
        finish(jnp.where(meta_ref[pl.ds(SPLIT, 1), :] != 0, own, joined))


def join_kernel(normed_ref, other_ref, out_ref):
    count = normed_ref.shape[0]
    for half in range(2):

        @pl.when(lax.axis_index("feat") == half)
        def _():
            out_ref[pl.ds(half * count, count), :] = normed_ref[...]
            out_ref[pl.ds((1 - half) * count, count), :] = other_ref[...]


def on_device(tokens, shot_starts, seed_offsets, norm_gain, proj_weight):
    rows, width = tokens.shape
    count = seed_offsets.shape[1]
    reach = 3 * rows // 8
    devices = lax.axis_size(AXES)
    across = [(i, i + 1) for i in range(1, devices - 1, 2)]
    across += [(target, source) for source, target in across]
    across += [(0, devices - 1), (devices - 1, 0)]
    pair = [(0, 1), (1, 0)]

    def shape(*dims, dtype=BF16):
        return jax.ShapeDtypeStruct(dims, dtype)

    def in_hbm(array):
        return pltpu.with_memory_space_constraint(array, pltpu.HBM)

    far_tokens = in_hbm(tokens)
    first, own, tail, share, meta, edge = pl.pallas_call(
        seed_kernel,
        out_shape=(
            shape(count, width),
            shape(count, width),
            shape(count, width),
            shape(2, width),
            shape(8, width, dtype=jnp.int32),
            shape(reach, width),
        ),
        in_specs=[HBM_SPEC] * 3,
        out_specs=[VMEM_SPEC] * 6,
        scratch_shapes=[
            pltpu.SMEM(shot_starts.shape, jnp.int32),
            pltpu.SMEM(seed_offsets.shape, jnp.int32),
            pltpu.VMEM(seed_offsets.shape, jnp.int32),
            pltpu.VMEM((16 * count, width), BF16),
            pltpu.SemaphoreType.DMA((3,)),
            pltpu.SemaphoreType.DMA(()),
            pltpu.SemaphoreType.DMA((2,)),
        ],
        compiler_params=pltpu.CompilerParams(vmem_limit_bytes=16 << 20),
        name="seeds",
    )(in_hbm(shot_starts), in_hbm(seed_offsets), far_tokens)
    given = lax.ppermute(tail, "feat", pair)

    def fetch(kernel, size, after, name):
        return pl.pallas_call(
            kernel,
            out_shape=shape(size, width),
            in_specs=[HBM_SPEC, VMEM_SPEC],
            out_specs=VMEM_SPEC,
            scratch_shapes=[pltpu.SemaphoreType.DMA((4,))],
            compiler_params=pltpu.CompilerParams(vmem_limit_bytes=16 << 20),
            name=name,
        )(far_tokens, after)

    edge, given = lax.optimization_barrier((edge, given))
    edge = lax.ppermute(edge, "feat", pair)
    x = first + given * share[:1]
    y = own + given * share[1:]
    received = lax.ppermute(x, AXES, across)
    near_tokens = fetch(load_kernel, rows, x, "load")

    def pool(first, ends, *state):
        outs = (shape(2 * count, width, dtype=F32), shape(2 * count, LANES, dtype=F32))
        outs += () if ends else (shape(count * width // LANES + 8, LANES),)
        return pl.pallas_call(
            functools.partial(pool_kernel, first, ends, devices),
            out_shape=outs,
            in_specs=[VMEM_SPEC] * 7,
            out_specs=[VMEM_SPEC] * len(outs),
            scratch_shapes=[pltpu.VMEM((2 * count, width), BF16)],
            compiler_params=pltpu.CompilerParams(vmem_limit_bytes=16 << 20),
            name="ends" if ends else "pool",
        )(meta, near_tokens, edge, *state)

    sums, masses, send = pool(True, False, x, received, y, y)
    start = received
    received = lax.ppermute(send, AXES, across)
    end_sums, end_masses = pool(True, True, x, start, y, masses)
    for _ in range(ITERS - 1):
        before = received
        sums, masses, send = pool(False, False, sums, masses, before, end_masses)
        received = lax.ppermute(send, AXES, across)
        end_sums, end_masses = pool(False, True, end_sums, end_masses, before, masses)
    normed = pl.pallas_call(
        functools.partial(norm_kernel, devices),
        out_shape=shape(count, width),
        in_specs=[VMEM_SPEC] * 7,
        out_specs=VMEM_SPEC,
        compiler_params=pltpu.CompilerParams(vmem_limit_bytes=8 << 20),
        name="norm",
    )(meta, norm_gain[None, :], received, sums, masses, end_sums, end_masses)
    both = pl.pallas_call(
        join_kernel,
        out_shape=shape(2 * count, width),
        in_specs=[VMEM_SPEC] * 2,
        out_specs=VMEM_SPEC,
        compiler_params=pltpu.CompilerParams(vmem_limit_bytes=8 << 20),
        name="join",
    )(normed, lax.ppermute(normed, "feat", pair))
    return jnp.dot(both, proj_weight, preferred_element_type=F32).astype(BF16)


def solution(mesh):
    in_specs = (P(AXES, None), P(), P(), P(), P(None, "feat"))
    out_specs = P("seq", "feat")
    return jax.shard_map(
        on_device, mesh=mesh, in_specs=in_specs, out_specs=out_specs, check_vma=False
    )
```

```python
import functools
import math

import jax
import jax.numpy as jnp
from jax import lax
from jax.experimental import pallas as pl
from jax.experimental.pallas import tpu as pltpu
from jax.sharding import PartitionSpec as P

ITERS = 3
AXES = ("seq", "feat")
LANES = 128
TILE = 512
F32 = jnp.float32
BF16 = jnp.bfloat16
VMEM_SPEC = pl.BlockSpec(memory_space=pltpu.VMEM)
HBM_SPEC = pl.BlockSpec(memory_space=pltpu.HBM)
X_LOW, X_HIGH, Y_LOW, Y_HIGH, EDGE, SPLIT, OCCUPIED, UNUSED = range(8)


def start_of(starts_ref, shot, shots, total):
    first = starts_ref[jnp.minimum(shot, shots - 1)]
    return jnp.where(shot >= shots, total, first)


def column_of(row):
    n = row.shape[1]
    diagonal = lax.broadcasted_iota(jnp.int32, (n, n), 0) == lax.broadcasted_iota(
        jnp.int32, (n, n), 1
    )
    spread = jnp.where(diagonal, jnp.broadcast_to(row, (n, n)), 0)
    return jnp.sum(spread, axis=1, keepdims=True)


def seed_kernel(
    starts_hbm,
    seeds_hbm,
    tokens_ref,
    tail_ref,
    near_ref,
    choose_ref,
    share_ref,
    meta_ref,
    edge_ref,
    starts_ref,
    seeds_ref,
    seed_rows_ref,
    picked,
    index_sems,
    pick_sems,
    edge_sems,
):
    rows, width = tokens_ref.shape
    reach = edge_ref.shape[0]
    shots, count = seeds_ref.shape
    total = shots * rows
    index = lax.axis_index(AXES)
    second = index % 2 == 1
    base = index * rows
    indices = [
        pltpu.make_async_copy(starts_hbm, starts_ref, index_sems.at[0]),
        pltpu.make_async_copy(seeds_hbm, seeds_ref, index_sems.at[1]),
        pltpu.make_async_copy(seeds_hbm, seed_rows_ref, index_sems.at[2]),
    ]
    for copy in indices:
        copy.start()
    strip_low = jnp.where(second, 0, rows - reach)
    strip = [
        pltpu.make_async_copy(
            tokens_ref.at[pl.ds(pl.multiple_of(strip_low + begin, 8), size), :],
            edge_ref.at[pl.ds(begin, size), :],
            edge_sems.at[at],
        )
        for at, (begin, size) in enumerate(((0, reach - TILE), (reach - TILE, TILE)))
    ]
    strip[0].start()
    for copy in indices:
        copy.wait()
    following = jnp.minimum(index + 1, shots - 1)
    here = start_of(starts_ref, index, shots, total)
    after = start_of(starts_ref, index + 1, shots, total)

    sides = ((following, after, picked, pick_sems.at[0]), (index, here, near_ref, pick_sems.at[1]))
    for shot, begin, rows_ref, sem in sides:

        def fetch(k, carry, shot=shot, begin=begin, rows_ref=rows_ref, sem=sem):
            place = begin + seeds_ref[shot, k] - base
            slot = pl.multiple_of(k * 8, 8)
            here_too = (place >= 0) & (place < rows)
            group = pl.multiple_of(jnp.where(here_too, (place // 8) * 8, slot), 8)
            pltpu.make_async_copy(
                tokens_ref.at[pl.ds(group, 8), :], rows_ref.at[pl.ds(slot, 8), :], sem
            ).start()
            return carry

        lax.fori_loop(0, count, fetch, 0, unroll=8)
    strip[1].start()

    low = jnp.where(second, here - base, 0)
    high = jnp.where(second, rows, after - base)
    cut = jnp.where(second, after - base, here - base)
    split = jnp.where(second, after <= base + rows, here > base) | (index == 0)
    x_low = jnp.where(split & second, cut, low)
    x_high = jnp.where(split & ~second, cut, high)
    y_low = jnp.where(split, jnp.where(second, low, cut), high)
    y_high = jnp.where(split, jnp.where(second, cut, high), high)
    table = {
        X_LOW: x_low,
        X_HIGH: x_high,
        Y_LOW: y_low,
        Y_HIGH: y_high,
        EDGE: jnp.where(second, -reach, rows),
        SPLIT: split.astype(jnp.int32),
        OCCUPIED: (x_low < x_high).astype(jnp.int32),
        UNUSED: 0,
    }
    for row, value in table.items():
        meta_ref[pl.ds(row, 1), :] = jnp.full((1, width), value, jnp.int32)
    lends = jnp.where(second, 1.0, 0.0)
    row = lax.broadcasted_iota(jnp.int32, share_ref.shape, 0)
    share_ref[...] = jnp.where(row == 0, jnp.where(split, 0.0, lends), lends).astype(BF16)

    choices = []
    for shot, begin, _, _ in sides:
        place = column_of(seed_rows_ref[pl.ds(shot, 1), :]) + (begin - base)
        valid = (place >= 0) & (place < rows)
        target = lax.broadcasted_iota(jnp.int32, (count, 1), 0) * 8 + place % 8
        lane = lax.broadcasted_iota(jnp.int32, (count, 8 * count), 1)
        choices.append(jnp.where(valid & (lane == target), 1.0, 0.0).astype(BF16))
    choose_ref[...] = choices[1]
    waits = [
        pltpu.make_async_copy(tokens_ref.at[pl.ds(0, 8 * count), :], rows_ref, sem)
        for _, _, rows_ref, sem in sides
    ]
    waits[0].wait()
    tail_ref[...] = jnp.dot(choices[0], picked[...], preferred_element_type=F32).astype(BF16)
    waits[1].wait()
    for copy in strip:
        copy.wait()


def own_kernel(near_ref, choose_ref, tail_ref, meta_ref, first_ref, own_ref):
    own = jnp.dot(choose_ref[...], near_ref[...], preferred_element_type=F32)
    tail = tail_ref[...].astype(F32)
    second = lax.axis_index(AXES) % 2 == 1
    split = meta_ref[pl.ds(SPLIT, 1), :] != 0
    first_ref[...] = jnp.where(split, jnp.where(second, tail, 0.0), own).astype(BF16)
    own_ref[...] = own.astype(BF16)


def copy_pieces(tokens_ref, low, out_ref, sems):
    pieces = sems.shape[0]
    piece = out_ref.shape[0] // pieces
    copies = [
        pltpu.make_async_copy(
            tokens_ref.at[pl.ds(pl.multiple_of(low + i * piece, 8), piece), :],
            out_ref.at[pl.ds(i * piece, piece), :],
            sems.at[i],
        )
        for i in range(pieces)
    ]
    for copy in copies:
        copy.start()
    for copy in copies:
        copy.wait()


def load_kernel(tokens_ref, order_ref, out_ref, sems):
    copy_pieces(tokens_ref, 0, out_ref, sems)


def at_end(devices):
    index = lax.axis_index(AXES)
    return (index == 0) | (index == devices - 1)


def lane_sum(block):
    return jnp.sum(block.astype(F32), axis=1, keepdims=True)


def on_diagonal(count):
    shape = (count, LANES)
    return lax.broadcasted_iota(jnp.int32, shape, 0) == lax.broadcasted_iota(jnp.int32, shape, 1)


def pack(sums, mass, out_ref):
    count, width = sums.shape
    blocks = width // LANES
    for at in range(blocks):
        block = sums[:, at * LANES : (at + 1) * LANES]
        out_ref[pl.ds(at * count, count), :] = block.astype(BF16)
    spread = jnp.sum(jnp.where(on_diagonal(count), mass, 0.0), axis=0, keepdims=True)
    high = spread.astype(BF16).astype(F32)
    middle = (spread - high).astype(BF16).astype(F32)
    low = spread - high - middle
    row = lax.broadcasted_iota(jnp.int32, (8, LANES), 0)
    terms = jnp.where(row == 0, high, jnp.where(row == 1, middle, jnp.where(row == 2, low, 0.0)))
    out_ref[pl.ds(blocks * count, 8), :] = terms.astype(BF16)


def unpack(packed_ref, count, width):
    blocks = width // LANES
    sums = jnp.concatenate(
        [packed_ref[pl.ds(at * count, count), :].astype(F32) for at in range(blocks)], axis=1
    )
    terms = packed_ref[pl.ds(blocks * count, 8), :].astype(F32)
    total = jnp.sum(terms, axis=0, keepdims=True)
    return sums, jnp.sum(jnp.where(on_diagonal(count), total, 0.0), axis=1, keepdims=True)


def pool_kernel(first, ends, devices, *refs):
    @pl.when(at_end(devices) == ends)
    def _():
        pool_body(first, ends, *refs)


def pool_body(first, ends, meta_ref, tokens_ref, edge_ref, *refs):
    if first:
        (x_ref, recv_ref, y_ref, _), refs = refs[:4], refs[4:]
        count, width = y_ref.shape
    else:
        (old_ref, old_mass_ref, recv_ref, _), refs = refs[:4], refs[4:]
        count, width = old_ref.shape[0] // 2, old_ref.shape[1]
    sums, masses, *send_out, centroids = refs
    rows = tokens_ref.shape[0]
    reach = edge_ref.shape[0]
    scale = math.log2(math.e) / math.sqrt(width)
    x_rows, y_rows = pl.ds(0, count), pl.ds(count, count)

    occupied = meta_ref[pl.ds(OCCUPIED, 1), :] != 0
    if first:
        joined = x_ref[...] + recv_ref[...]
        centroids[x_rows, :] = jnp.where(occupied, joined, jnp.zeros_like(joined))
        centroids[y_rows, :] = y_ref[...]
    else:
        other, other_mass = unpack(recv_ref, count, width)
        mass = lane_sum(old_mass_ref[x_rows, :]) + other_mass
        joined = (old_ref[x_rows, :] + other) * (1.0 / mass)
        centroids[x_rows, :] = jnp.where(occupied, joined, 0.0).astype(BF16)
        mass = lane_sum(old_mass_ref[y_rows, :])
        centroids[y_rows, :] = (old_ref[y_rows, :] * (1.0 / mass)).astype(BF16)

    tiles = [(tokens_ref, i * TILE) for i in range(rows // TILE)]
    tiles += [(edge_ref, i * TILE) for i in range(reach // TILE)]

    def scores_of(tile):
        ref, row = tile
        return lax.dot_general(
            centroids[...],
            ref[pl.ds(row, TILE), :],
            (((1,), (1,)), ((), ())),
            preferred_element_type=F32,
        )

    def weights_of(tile, scores):
        ref, row = tile
        place = row + lax.broadcasted_iota(jnp.int32, (1, TILE), 1)
        if ref is edge_ref:
            place = place + meta_ref[pl.ds(EDGE, 1), :TILE]
        bound = [meta_ref[pl.ds(i, 1), :TILE] for i in (X_LOW, X_HIGH, Y_LOW, Y_HIGH)]
        in_x = (place >= bound[0]) & (place < bound[1])
        in_y = (place >= bound[2]) & (place < bound[3])
        mine = jnp.where(in_y, scores[count:], scores[:count])
        top = jnp.max(mine, axis=0, keepdims=True)
        powers = jnp.exp2((mine - top) * scale)
        inverse = 1.0 / jnp.sum(powers, axis=0, keepdims=True)
        return jnp.concatenate(
            [powers * jnp.where(in_x, inverse, 0.0), powers * jnp.where(in_y, inverse, 0.0)], axis=0
        )

    scores = scores_of(tiles[0])
    for at, tile in enumerate(tiles):
        upcoming = scores_of(tiles[at + 1]) if at + 1 < len(tiles) else None
        weights = weights_of(tile, scores)
        part = weights[:, :LANES]
        for i in range(1, TILE // LANES):
            part = part + weights[:, i * LANES : (i + 1) * LANES]
        added = jnp.dot(
            weights.astype(BF16), tile[0][pl.ds(tile[1], TILE), :], preferred_element_type=F32
        )
        if at == 0:
            masses[...] = part
            sums[...] = added
        else:
            masses[...] += part
            sums[...] += added
        scores = upcoming

    if ends:
        return
    (send_out,) = send_out
    pack(sums[x_rows, :], lane_sum(masses[x_rows, :]), send_out)


def norm_kernel(devices, meta_ref, gain_ref, recv_ref, *refs):
    out_ref = refs[-1]
    count, width = out_ref.shape
    x_rows, y_rows = pl.ds(0, count), pl.ds(count, count)

    def finish(centroid):
        spread = jnp.sqrt(jnp.mean(centroid * centroid, axis=-1, keepdims=True) + 1e-06)
        out_ref[...] = (centroid * (1.0 / spread) * gain_ref[...]).astype(BF16)

    @pl.when(at_end(devices))
    def _():
        sums, masses = refs[2:4]
        finish(sums[y_rows, :] * (1.0 / lane_sum(masses[y_rows, :])))

    @pl.when(~at_end(devices))
    def _():
        sums, masses = refs[:2]
        other, other_mass = unpack(recv_ref, count, width)
        mass = lane_sum(masses[x_rows, :]) + other_mass
        joined = (sums[x_rows, :] + other) * (1.0 / mass)
        own = sums[y_rows, :] * (1.0 / lane_sum(masses[y_rows, :]))
        finish(jnp.where(meta_ref[pl.ds(SPLIT, 1), :] != 0, own, joined))


def join_kernel(normed_ref, other_ref, out_ref):
    count = normed_ref.shape[0]
    for half in range(2):

        @pl.when(lax.axis_index("feat") == half)
        def _():
            out_ref[pl.ds(half * count, count), :] = normed_ref[...]
            out_ref[pl.ds((1 - half) * count, count), :] = other_ref[...]


def on_device(tokens, shot_starts, seed_offsets, norm_gain, proj_weight):
    rows, width = tokens.shape
    count = seed_offsets.shape[1]
    reach = 3 * rows // 8
    devices = lax.axis_size(AXES)
    across = [(i, i + 1) for i in range(1, devices - 1, 2)]
    across += [(target, source) for source, target in across]
    across += [(0, devices - 1), (devices - 1, 0)]
    pair = [(0, 1), (1, 0)]

    def shape(*dims, dtype=BF16):
        return jax.ShapeDtypeStruct(dims, dtype)

    def in_hbm(array):
        return pltpu.with_memory_space_constraint(array, pltpu.HBM)

    far_tokens = in_hbm(tokens)
    tail, near, choose, share, meta, edge = pl.pallas_call(
        seed_kernel,
        out_shape=(
            shape(count, width),
            shape(8 * count, width),
            shape(count, 8 * count),
            shape(2, width),
            shape(8, width, dtype=jnp.int32),
            shape(reach, width),
        ),
        in_specs=[HBM_SPEC] * 3,
        out_specs=[VMEM_SPEC] * 6,
        scratch_shapes=[
            pltpu.SMEM(shot_starts.shape, jnp.int32),
            pltpu.SMEM(seed_offsets.shape, jnp.int32),
            pltpu.VMEM(seed_offsets.shape, jnp.int32),
            pltpu.VMEM((8 * count, width), BF16),
            pltpu.SemaphoreType.DMA((3,)),
            pltpu.SemaphoreType.DMA((2,)),
            pltpu.SemaphoreType.DMA((2,)),
        ],
        compiler_params=pltpu.CompilerParams(vmem_limit_bytes=16 << 20),
        name="seeds",
    )(in_hbm(shot_starts), in_hbm(seed_offsets), far_tokens)
    given = lax.ppermute(tail, "feat", pair)
    first, own = pl.pallas_call(
        own_kernel,
        out_shape=(shape(count, width), shape(count, width)),
        in_specs=[VMEM_SPEC] * 4,
        out_specs=[VMEM_SPEC] * 2,
        compiler_params=pltpu.CompilerParams(vmem_limit_bytes=8 << 20),
        cost_estimate=pl.CostEstimate(
            flops=16 * count * count * width, bytes_accessed=24 * count * width, transcendentals=0
        ),
        name="own",
    )(near, choose, tail, meta)

    def fetch(kernel, size, after, name):
        return pl.pallas_call(
            kernel,
            out_shape=shape(size, width),
            in_specs=[HBM_SPEC, VMEM_SPEC],
            out_specs=VMEM_SPEC,
            scratch_shapes=[pltpu.SemaphoreType.DMA((4,))],
            compiler_params=pltpu.CompilerParams(vmem_limit_bytes=16 << 20),
            name=name,
        )(far_tokens, after)

    edge, given, first = lax.optimization_barrier((edge, given, first))
    edge = lax.ppermute(edge, "feat", pair)
    x = first + given * share[:1]
    y = own + given * share[1:]
    received = lax.ppermute(x, AXES, across)
    near_tokens = fetch(load_kernel, rows, x, "load")

    def pool(first, ends, *state):
        outs = (shape(2 * count, width, dtype=F32), shape(2 * count, LANES, dtype=F32))
        outs += () if ends else (shape(count * width // LANES + 8, LANES),)
        return pl.pallas_call(
            functools.partial(pool_kernel, first, ends, devices),
            out_shape=outs,
            in_specs=[VMEM_SPEC] * 7,
            out_specs=[VMEM_SPEC] * len(outs),
            scratch_shapes=[pltpu.VMEM((2 * count, width), BF16)],
            compiler_params=pltpu.CompilerParams(vmem_limit_bytes=16 << 20),
            name="ends" if ends else "pool",
        )(meta, near_tokens, edge, *state)

    sums, masses, send = pool(True, False, x, received, y, y)
    start = received
    received = lax.ppermute(send, AXES, across)
    end_sums, end_masses = pool(True, True, x, start, y, masses)
    for _ in range(ITERS - 1):
        before = received
        sums, masses, send = pool(False, False, sums, masses, before, end_masses)
        received = lax.ppermute(send, AXES, across)
        end_sums, end_masses = pool(False, True, end_sums, end_masses, before, masses)
    normed = pl.pallas_call(
        functools.partial(norm_kernel, devices),
        out_shape=shape(count, width),
        in_specs=[VMEM_SPEC] * 7,
        out_specs=VMEM_SPEC,
        compiler_params=pltpu.CompilerParams(vmem_limit_bytes=8 << 20),
        name="norm",
    )(meta, norm_gain[None, :], received, sums, masses, end_sums, end_masses)
    both = pl.pallas_call(
        join_kernel,
        out_shape=shape(2 * count, width),
        in_specs=[VMEM_SPEC] * 2,
        out_specs=VMEM_SPEC,
        compiler_params=pltpu.CompilerParams(vmem_limit_bytes=8 << 20),
        name="join",
    )(normed, lax.ppermute(normed, "feat", pair))
    return jnp.dot(both, proj_weight, preferred_element_type=F32).astype(BF16)


def solution(mesh):
    in_specs = (P(AXES, None), P(), P(), P(), P(None, "feat"))
    out_specs = P("seq", "feat")
    return jax.shard_map(
        on_device, mesh=mesh, in_specs=in_specs, out_specs=out_specs, check_vma=False
    )
```

```python
import functools
import math

import jax
import jax.numpy as jnp
from jax import lax
from jax.experimental import pallas as pl
from jax.experimental.pallas import tpu as pltpu
from jax.sharding import PartitionSpec as P

ITERS = 3
AXES = ("seq", "feat")
LANES = 128
TILE = 512
F32 = jnp.float32
BF16 = jnp.bfloat16
VMEM_SPEC = pl.BlockSpec(memory_space=pltpu.VMEM)
HBM_SPEC = pl.BlockSpec(memory_space=pltpu.HBM)
X_LOW, X_HIGH, Y_LOW, Y_HIGH, EDGE, SPLIT, OCCUPIED, UNUSED = range(8)


def start_of(starts_ref, shot, shots, total):
    first = starts_ref[jnp.minimum(shot, shots - 1)]
    return jnp.where(shot >= shots, total, first)


def column_of(row):
    n = row.shape[1]
    diagonal = lax.broadcasted_iota(jnp.int32, (n, n), 0) == lax.broadcasted_iota(
        jnp.int32, (n, n), 1
    )
    spread = jnp.where(diagonal, jnp.broadcast_to(row, (n, n)), 0)
    return jnp.sum(spread, axis=1, keepdims=True)


def seed_kernel(
    starts_hbm,
    seeds_hbm,
    tokens_ref,
    tail_ref,
    near_ref,
    choose_ref,
    share_ref,
    meta_ref,
    edge_ref,
    starts_ref,
    seeds_ref,
    seed_rows_ref,
    picked,
    index_sems,
    pick_sems,
    edge_sem,
):
    rows, width = tokens_ref.shape
    reach = edge_ref.shape[0]
    shots, count = seeds_ref.shape
    total = shots * rows
    index = lax.axis_index(AXES)
    second = index % 2 == 1
    base = index * rows
    indices = [
        pltpu.make_async_copy(starts_hbm, starts_ref, index_sems.at[0]),
        pltpu.make_async_copy(seeds_hbm, seeds_ref, index_sems.at[1]),
        pltpu.make_async_copy(seeds_hbm, seed_rows_ref, index_sems.at[2]),
    ]
    for copy in indices:
        copy.start()
    size = reach - TILE
    strip_low = pl.multiple_of(jnp.where(second, 0, rows - reach), 8)
    strip = pltpu.make_async_copy(
        tokens_ref.at[pl.ds(strip_low, size), :], edge_ref.at[pl.ds(0, size), :], edge_sem
    )
    strip.start()
    for copy in indices:
        copy.wait()
    following = jnp.minimum(index + 1, shots - 1)
    here = start_of(starts_ref, index, shots, total)
    after = start_of(starts_ref, index + 1, shots, total)

    sides = ((following, after, picked, pick_sems.at[0]), (index, here, near_ref, pick_sems.at[1]))
    for shot, begin, rows_ref, sem in sides:

        def fetch(k, carry, shot=shot, begin=begin, rows_ref=rows_ref, sem=sem):
            place = begin + seeds_ref[shot, k] - base
            slot = pl.multiple_of(k * 8, 8)
            here_too = (place >= 0) & (place < rows)
            group = pl.multiple_of(jnp.where(here_too, (place // 8) * 8, slot), 8)
            pltpu.make_async_copy(
                tokens_ref.at[pl.ds(group, 8), :], rows_ref.at[pl.ds(slot, 8), :], sem
            ).start()
            return carry

        lax.fori_loop(0, count, fetch, 0, unroll=8)

    low = jnp.where(second, here - base, 0)
    high = jnp.where(second, rows, after - base)
    cut = jnp.where(second, after - base, here - base)
    split = jnp.where(second, after <= base + rows, here > base) | (index == 0)
    x_low = jnp.where(split & second, cut, low)
    x_high = jnp.where(split & ~second, cut, high)
    y_low = jnp.where(split, jnp.where(second, low, cut), high)
    y_high = jnp.where(split, jnp.where(second, cut, high), high)
    table = {
        X_LOW: x_low,
        X_HIGH: x_high,
        Y_LOW: y_low,
        Y_HIGH: y_high,
        EDGE: jnp.where(second, -reach, rows),
        SPLIT: split.astype(jnp.int32),
        OCCUPIED: (x_low < x_high).astype(jnp.int32),
        UNUSED: 0,
    }
    for row, value in table.items():
        meta_ref[pl.ds(row, 1), :] = jnp.full((1, width), value, jnp.int32)
    lends = jnp.where(second, 1.0, 0.0)
    row = lax.broadcasted_iota(jnp.int32, share_ref.shape, 0)
    share_ref[...] = jnp.where(row == 0, jnp.where(split, 0.0, lends), lends).astype(BF16)

    choices = []
    for shot, begin, _, _ in sides:
        place = column_of(seed_rows_ref[pl.ds(shot, 1), :]) + (begin - base)
        valid = (place >= 0) & (place < rows)
        target = lax.broadcasted_iota(jnp.int32, (count, 1), 0) * 8 + place % 8
        lane = lax.broadcasted_iota(jnp.int32, (count, 8 * count), 1)
        choices.append(jnp.where(valid & (lane == target), 1.0, 0.0).astype(BF16))
    choose_ref[...] = choices[1]
    waits = [
        pltpu.make_async_copy(tokens_ref.at[pl.ds(0, 8 * count), :], rows_ref, sem)
        for _, _, rows_ref, sem in sides
    ]
    waits[0].wait()
    tail_ref[...] = jnp.dot(choices[0], picked[...], preferred_element_type=F32).astype(BF16)
    waits[1].wait()
    strip.wait()


def own_kernel(
    tokens_ref,
    edge_in_ref,
    near_ref,
    choose_ref,
    tail_ref,
    meta_ref,
    first_ref,
    own_ref,
    edge_ref,
    edge_sem,
):
    rows, reach = tokens_ref.shape[0], edge_ref.shape[0]
    begin = jnp.where(lax.axis_index(AXES) % 2 == 1, reach, rows) - TILE
    strip = pltpu.make_async_copy(
        tokens_ref.at[pl.ds(pl.multiple_of(begin, 8), TILE), :],
        edge_ref.at[pl.ds(reach - TILE, TILE), :],
        edge_sem,
    )
    strip.start()
    own = jnp.dot(choose_ref[...], near_ref[...], preferred_element_type=F32)
    tail = tail_ref[...].astype(F32)
    second = lax.axis_index(AXES) % 2 == 1
    split = meta_ref[pl.ds(SPLIT, 1), :] != 0
    first_ref[...] = jnp.where(split, jnp.where(second, tail, 0.0), own).astype(BF16)
    own_ref[...] = own.astype(BF16)
    strip.wait()


def copy_pieces(tokens_ref, low, out_ref, sems):
    pieces = sems.shape[0]
    piece = out_ref.shape[0] // pieces
    copies = [
        pltpu.make_async_copy(
            tokens_ref.at[pl.ds(pl.multiple_of(low + i * piece, 8), piece), :],
            out_ref.at[pl.ds(i * piece, piece), :],
            sems.at[i],
        )
        for i in range(pieces)
    ]
    for copy in copies:
        copy.start()
    for copy in copies:
        copy.wait()


def load_kernel(tokens_ref, order_ref, out_ref, sems):
    copy_pieces(tokens_ref, 0, out_ref, sems)


def at_end(devices):
    index = lax.axis_index(AXES)
    return (index == 0) | (index == devices - 1)


def lane_sum(block):
    return jnp.sum(block.astype(F32), axis=1, keepdims=True)


def on_diagonal(count):
    shape = (count, LANES)
    return lax.broadcasted_iota(jnp.int32, shape, 0) == lax.broadcasted_iota(jnp.int32, shape, 1)


def pack(sums, mass, out_ref):
    count, width = sums.shape
    blocks = width // LANES
    for at in range(blocks):
        block = sums[:, at * LANES : (at + 1) * LANES]
        out_ref[pl.ds(at * count, count), :] = block.astype(BF16)
    spread = jnp.sum(jnp.where(on_diagonal(count), mass, 0.0), axis=0, keepdims=True)
    high = spread.astype(BF16).astype(F32)
    middle = (spread - high).astype(BF16).astype(F32)
    low = spread - high - middle
    row = lax.broadcasted_iota(jnp.int32, (8, LANES), 0)
    terms = jnp.where(row == 0, high, jnp.where(row == 1, middle, jnp.where(row == 2, low, 0.0)))
    out_ref[pl.ds(blocks * count, 8), :] = terms.astype(BF16)


def unpack(packed_ref, count, width):
    blocks = width // LANES
    sums = jnp.concatenate(
        [packed_ref[pl.ds(at * count, count), :].astype(F32) for at in range(blocks)], axis=1
    )
    terms = packed_ref[pl.ds(blocks * count, 8), :].astype(F32)
    total = jnp.sum(terms, axis=0, keepdims=True)
    return sums, jnp.sum(jnp.where(on_diagonal(count), total, 0.0), axis=1, keepdims=True)


def pool_kernel(first, ends, devices, *refs):
    @pl.when(at_end(devices) == ends)
    def _():
        pool_body(first, ends, *refs)


def pool_body(first, ends, meta_ref, tokens_ref, edge_ref, *refs):
    if first:
        (x_ref, recv_ref, y_ref, _), refs = refs[:4], refs[4:]
        count, width = y_ref.shape
    else:
        (old_ref, old_mass_ref, recv_ref, _), refs = refs[:4], refs[4:]
        count, width = old_ref.shape[0] // 2, old_ref.shape[1]
    sums, masses, *send_out, centroids = refs
    rows = tokens_ref.shape[0]
    reach = edge_ref.shape[0]
    scale = math.log2(math.e) / math.sqrt(width)
    x_rows, y_rows = pl.ds(0, count), pl.ds(count, count)

    occupied = meta_ref[pl.ds(OCCUPIED, 1), :] != 0
    if first:
        joined = x_ref[...] + recv_ref[...]
        centroids[x_rows, :] = jnp.where(occupied, joined, jnp.zeros_like(joined))
        centroids[y_rows, :] = y_ref[...]
    else:
        other, other_mass = unpack(recv_ref, count, width)
        mass = lane_sum(old_mass_ref[x_rows, :]) + other_mass
        joined = (old_ref[x_rows, :] + other) * (1.0 / mass)
        centroids[x_rows, :] = jnp.where(occupied, joined, 0.0).astype(BF16)
        mass = lane_sum(old_mass_ref[y_rows, :])
        centroids[y_rows, :] = (old_ref[y_rows, :] * (1.0 / mass)).astype(BF16)

    tiles = [(tokens_ref, i * TILE) for i in range(rows // TILE)]
    tiles += [(edge_ref, i * TILE) for i in range(reach // TILE)]

    def scores_of(tile):
        ref, row = tile
        return lax.dot_general(
            centroids[...],
            ref[pl.ds(row, TILE), :],
            (((1,), (1,)), ((), ())),
            preferred_element_type=F32,
        )

    def weights_of(tile, scores):
        ref, row = tile
        place = row + lax.broadcasted_iota(jnp.int32, (1, TILE), 1)
        if ref is edge_ref:
            place = place + meta_ref[pl.ds(EDGE, 1), :TILE]
        bound = [meta_ref[pl.ds(i, 1), :TILE] for i in (X_LOW, X_HIGH, Y_LOW, Y_HIGH)]
        in_x = (place >= bound[0]) & (place < bound[1])
        in_y = (place >= bound[2]) & (place < bound[3])
        mine = jnp.where(in_y, scores[count:], scores[:count])
        top = jnp.max(mine, axis=0, keepdims=True)
        powers = jnp.exp2((mine - top) * scale)
        inverse = 1.0 / jnp.sum(powers, axis=0, keepdims=True)
        return jnp.concatenate(
            [powers * jnp.where(in_x, inverse, 0.0), powers * jnp.where(in_y, inverse, 0.0)], axis=0
        )

    scores = scores_of(tiles[0])
    for at, tile in enumerate(tiles):
        upcoming = scores_of(tiles[at + 1]) if at + 1 < len(tiles) else None
        weights = weights_of(tile, scores)
        part = weights[:, :LANES]
        for i in range(1, TILE // LANES):
            part = part + weights[:, i * LANES : (i + 1) * LANES]
        added = jnp.dot(
            weights.astype(BF16), tile[0][pl.ds(tile[1], TILE), :], preferred_element_type=F32
        )
        if at == 0:
            masses[...] = part
            sums[...] = added
        else:
            masses[...] += part
            sums[...] += added
        scores = upcoming

    if ends:
        return
    (send_out,) = send_out
    pack(sums[x_rows, :], lane_sum(masses[x_rows, :]), send_out)


def norm_kernel(devices, meta_ref, gain_ref, recv_ref, *refs):
    out_ref = refs[-1]
    count, width = out_ref.shape
    x_rows, y_rows = pl.ds(0, count), pl.ds(count, count)

    def finish(centroid):
        spread = jnp.sqrt(jnp.mean(centroid * centroid, axis=-1, keepdims=True) + 1e-06)
        out_ref[...] = (centroid * (1.0 / spread) * gain_ref[...]).astype(BF16)

    @pl.when(at_end(devices))
    def _():
        sums, masses = refs[2:4]
        finish(sums[y_rows, :] * (1.0 / lane_sum(masses[y_rows, :])))

    @pl.when(~at_end(devices))
    def _():
        sums, masses = refs[:2]
        other, other_mass = unpack(recv_ref, count, width)
        mass = lane_sum(masses[x_rows, :]) + other_mass
        joined = (sums[x_rows, :] + other) * (1.0 / mass)
        own = sums[y_rows, :] * (1.0 / lane_sum(masses[y_rows, :]))
        finish(jnp.where(meta_ref[pl.ds(SPLIT, 1), :] != 0, own, joined))


def join_kernel(normed_ref, other_ref, out_ref):
    count = normed_ref.shape[0]
    for half in range(2):

        @pl.when(lax.axis_index("feat") == half)
        def _():
            out_ref[pl.ds(half * count, count), :] = normed_ref[...]
            out_ref[pl.ds((1 - half) * count, count), :] = other_ref[...]


def on_device(tokens, shot_starts, seed_offsets, norm_gain, proj_weight):
    rows, width = tokens.shape
    count = seed_offsets.shape[1]
    reach = 3 * rows // 8
    devices = lax.axis_size(AXES)
    across = [(i, i + 1) for i in range(1, devices - 1, 2)]
    across += [(target, source) for source, target in across]
    across += [(0, devices - 1), (devices - 1, 0)]
    pair = [(0, 1), (1, 0)]

    def shape(*dims, dtype=BF16):
        return jax.ShapeDtypeStruct(dims, dtype)

    def in_hbm(array):
        return pltpu.with_memory_space_constraint(array, pltpu.HBM)

    far_tokens = in_hbm(tokens)
    tail, near, choose, share, meta, edge = pl.pallas_call(
        seed_kernel,
        out_shape=(
            shape(count, width),
            shape(8 * count, width),
            shape(count, 8 * count),
            shape(2, width),
            shape(8, width, dtype=jnp.int32),
            shape(reach, width),
        ),
        in_specs=[HBM_SPEC] * 3,
        out_specs=[VMEM_SPEC] * 6,
        scratch_shapes=[
            pltpu.SMEM(shot_starts.shape, jnp.int32),
            pltpu.SMEM(seed_offsets.shape, jnp.int32),
            pltpu.VMEM(seed_offsets.shape, jnp.int32),
            pltpu.VMEM((8 * count, width), BF16),
            pltpu.SemaphoreType.DMA((3,)),
            pltpu.SemaphoreType.DMA((2,)),
            pltpu.SemaphoreType.DMA(()),
        ],
        compiler_params=pltpu.CompilerParams(vmem_limit_bytes=16 << 20),
        name="seeds",
    )(in_hbm(shot_starts), in_hbm(seed_offsets), far_tokens)
    given = lax.ppermute(tail, "feat", pair)
    first, own, edge = pl.pallas_call(
        own_kernel,
        out_shape=(shape(count, width), shape(count, width), shape(reach, width)),
        in_specs=[HBM_SPEC] + [VMEM_SPEC] * 5,
        out_specs=[VMEM_SPEC] * 3,
        scratch_shapes=[pltpu.SemaphoreType.DMA(())],
        input_output_aliases={1: 2},
        compiler_params=pltpu.CompilerParams(vmem_limit_bytes=8 << 20),
        cost_estimate=pl.CostEstimate(
            flops=16 * count * count * width, bytes_accessed=24 * count * width, transcendentals=0
        ),
        name="own",
    )(far_tokens, edge, near, choose, tail, meta)

    def fetch(kernel, size, after, name):
        return pl.pallas_call(
            kernel,
            out_shape=shape(size, width),
            in_specs=[HBM_SPEC, VMEM_SPEC],
            out_specs=VMEM_SPEC,
            scratch_shapes=[pltpu.SemaphoreType.DMA((4,))],
            compiler_params=pltpu.CompilerParams(vmem_limit_bytes=16 << 20),
            name=name,
        )(far_tokens, after)

    edge, given, first = lax.optimization_barrier((edge, given, first))
    edge = lax.ppermute(edge, "feat", pair)
    x = first + given * share[:1]
    y = own + given * share[1:]
    received = lax.ppermute(x, AXES, across)
    near_tokens = fetch(load_kernel, rows, x, "load")

    def pool(first, ends, *state):
        outs = (shape(2 * count, width, dtype=F32), shape(2 * count, LANES, dtype=F32))
        outs += () if ends else (shape(count * width // LANES + 8, LANES),)
        return pl.pallas_call(
            functools.partial(pool_kernel, first, ends, devices),
            out_shape=outs,
            in_specs=[VMEM_SPEC] * 7,
            out_specs=[VMEM_SPEC] * len(outs),
            scratch_shapes=[pltpu.VMEM((2 * count, width), BF16)],
            compiler_params=pltpu.CompilerParams(vmem_limit_bytes=16 << 20),
            name="ends" if ends else "pool",
        )(meta, near_tokens, edge, *state)

    sums, masses, send = pool(True, False, x, received, y, y)
    start = received
    received = lax.ppermute(send, AXES, across)
    end_sums, end_masses = pool(True, True, x, start, y, masses)
    for _ in range(ITERS - 1):
        before = received
        sums, masses, send = pool(False, False, sums, masses, before, end_masses)
        received = lax.ppermute(send, AXES, across)
        end_sums, end_masses = pool(False, True, end_sums, end_masses, before, masses)
    normed = pl.pallas_call(
        functools.partial(norm_kernel, devices),
        out_shape=shape(count, width),
        in_specs=[VMEM_SPEC] * 7,
        out_specs=VMEM_SPEC,
        compiler_params=pltpu.CompilerParams(vmem_limit_bytes=8 << 20),
        name="norm",
    )(meta, norm_gain[None, :], received, sums, masses, end_sums, end_masses)
    both = pl.pallas_call(
        join_kernel,
        out_shape=shape(2 * count, width),
        in_specs=[VMEM_SPEC] * 2,
        out_specs=VMEM_SPEC,
        compiler_params=pltpu.CompilerParams(vmem_limit_bytes=8 << 20),
        name="join",
    )(normed, lax.ppermute(normed, "feat", pair))
    return jnp.dot(both, proj_weight, preferred_element_type=F32).astype(BF16)


def solution(mesh):
    in_specs = (P(AXES, None), P(), P(), P(), P(None, "feat"))
    out_specs = P("seq", "feat")
    return jax.shard_map(
        on_device, mesh=mesh, in_specs=in_specs, out_specs=out_specs, check_vma=False
    )
```

```python
import functools
import math

import jax
import jax.numpy as jnp
from jax import lax
from jax.experimental import pallas as pl
from jax.experimental.pallas import tpu as pltpu
from jax.sharding import PartitionSpec as P

ITERS = 3
AXES = ("seq", "feat")
LANES = 128
TILE = 512
LATE = TILE // 2
F32 = jnp.float32
BF16 = jnp.bfloat16
VMEM_SPEC = pl.BlockSpec(memory_space=pltpu.VMEM)
HBM_SPEC = pl.BlockSpec(memory_space=pltpu.HBM)
X_LOW, X_HIGH, Y_LOW, Y_HIGH, EDGE, SPLIT, OCCUPIED, UNUSED = range(8)


def start_of(starts_ref, shot, shots, total):
    first = starts_ref[jnp.minimum(shot, shots - 1)]
    return jnp.where(shot >= shots, total, first)


def column_of(row):
    n = row.shape[1]
    diagonal = lax.broadcasted_iota(jnp.int32, (n, n), 0) == lax.broadcasted_iota(
        jnp.int32, (n, n), 1
    )
    spread = jnp.where(diagonal, jnp.broadcast_to(row, (n, n)), 0)
    return jnp.sum(spread, axis=1, keepdims=True)


def seed_kernel(
    starts_hbm,
    seeds_hbm,
    tokens_ref,
    tail_ref,
    near_ref,
    choose_ref,
    share_ref,
    meta_ref,
    edge_ref,
    starts_ref,
    seeds_ref,
    seed_rows_ref,
    picked,
    index_sems,
    pick_sems,
    edge_sem,
):
    rows, width = tokens_ref.shape
    reach = edge_ref.shape[0]
    shots, count = seeds_ref.shape
    total = shots * rows
    index = lax.axis_index(AXES)
    second = index % 2 == 1
    base = index * rows
    indices = [
        pltpu.make_async_copy(starts_hbm, starts_ref, index_sems.at[0]),
        pltpu.make_async_copy(seeds_hbm, seeds_ref, index_sems.at[1]),
        pltpu.make_async_copy(seeds_hbm, seed_rows_ref, index_sems.at[2]),
    ]
    for copy in indices:
        copy.start()
    size = reach - LATE
    strip_low = pl.multiple_of(jnp.where(second, 0, rows - reach), 8)
    strip = pltpu.make_async_copy(
        tokens_ref.at[pl.ds(strip_low, size), :], edge_ref.at[pl.ds(0, size), :], edge_sem
    )
    strip.start()
    for copy in indices:
        copy.wait()
    following = jnp.minimum(index + 1, shots - 1)
    here = start_of(starts_ref, index, shots, total)
    after = start_of(starts_ref, index + 1, shots, total)

    sides = ((following, after, picked, pick_sems.at[0]), (index, here, near_ref, pick_sems.at[1]))
    for shot, begin, rows_ref, sem in sides:

        def fetch(k, carry, shot=shot, begin=begin, rows_ref=rows_ref, sem=sem):
            place = begin + seeds_ref[shot, k] - base
            slot = pl.multiple_of(k * 8, 8)
            here_too = (place >= 0) & (place < rows)
            group = pl.multiple_of(jnp.where(here_too, (place // 8) * 8, slot), 8)
            pltpu.make_async_copy(
                tokens_ref.at[pl.ds(group, 8), :], rows_ref.at[pl.ds(slot, 8), :], sem
            ).start()
            return carry

        lax.fori_loop(0, count, fetch, 0, unroll=8)

    low = jnp.where(second, here - base, 0)
    high = jnp.where(second, rows, after - base)
    cut = jnp.where(second, after - base, here - base)
    split = jnp.where(second, after <= base + rows, here > base) | (index == 0)
    x_low = jnp.where(split & second, cut, low)
    x_high = jnp.where(split & ~second, cut, high)
    y_low = jnp.where(split, jnp.where(second, low, cut), high)
    y_high = jnp.where(split, jnp.where(second, cut, high), high)
    table = {
        X_LOW: x_low,
        X_HIGH: x_high,
        Y_LOW: y_low,
        Y_HIGH: y_high,
        EDGE: jnp.where(second, -reach, rows),
        SPLIT: split.astype(jnp.int32),
        OCCUPIED: (x_low < x_high).astype(jnp.int32),
        UNUSED: 0,
    }
    for row, value in table.items():
        meta_ref[pl.ds(row, 1), :] = jnp.full((1, width), value, jnp.int32)
    lends = jnp.where(second, 1.0, 0.0)
    row = lax.broadcasted_iota(jnp.int32, share_ref.shape, 0)
    share_ref[...] = jnp.where(row == 0, jnp.where(split, 0.0, lends), lends).astype(BF16)

    choices = []
    for shot, begin, _, _ in sides:
        place = column_of(seed_rows_ref[pl.ds(shot, 1), :]) + (begin - base)
        valid = (place >= 0) & (place < rows)
        target = lax.broadcasted_iota(jnp.int32, (count, 1), 0) * 8 + place % 8
        lane = lax.broadcasted_iota(jnp.int32, (count, 8 * count), 1)
        choices.append(jnp.where(valid & (lane == target), 1.0, 0.0).astype(BF16))
    choose_ref[...] = choices[1]
    waits = [
        pltpu.make_async_copy(tokens_ref.at[pl.ds(0, 8 * count), :], rows_ref, sem)
        for _, _, rows_ref, sem in sides
    ]
    waits[0].wait()
    tail_ref[...] = jnp.dot(choices[0], picked[...], preferred_element_type=F32).astype(BF16)
    waits[1].wait()
    strip.wait()


def own_kernel(
    tokens_ref,
    edge_in_ref,
    near_ref,
    choose_ref,
    tail_ref,
    meta_ref,
    first_ref,
    own_ref,
    edge_ref,
    edge_sem,
):
    rows, reach = tokens_ref.shape[0], edge_ref.shape[0]
    begin = jnp.where(lax.axis_index(AXES) % 2 == 1, reach, rows) - LATE
    strip = pltpu.make_async_copy(
        tokens_ref.at[pl.ds(pl.multiple_of(begin, 8), LATE), :],
        edge_ref.at[pl.ds(reach - LATE, LATE), :],
        edge_sem,
    )
    strip.start()
    own = jnp.dot(choose_ref[...], near_ref[...], preferred_element_type=F32)
    tail = tail_ref[...].astype(F32)
    second = lax.axis_index(AXES) % 2 == 1
    split = meta_ref[pl.ds(SPLIT, 1), :] != 0
    first_ref[...] = jnp.where(split, jnp.where(second, tail, 0.0), own).astype(BF16)
    own_ref[...] = own.astype(BF16)
    strip.wait()


def copy_pieces(tokens_ref, low, out_ref, sems):
    pieces = sems.shape[0]
    piece = out_ref.shape[0] // pieces
    copies = [
        pltpu.make_async_copy(
            tokens_ref.at[pl.ds(pl.multiple_of(low + i * piece, 8), piece), :],
            out_ref.at[pl.ds(i * piece, piece), :],
            sems.at[i],
        )
        for i in range(pieces)
    ]
    for copy in copies:
        copy.start()
    for copy in copies:
        copy.wait()


def load_kernel(tokens_ref, order_ref, out_ref, sems):
    copy_pieces(tokens_ref, 0, out_ref, sems)


def at_end(devices):
    index = lax.axis_index(AXES)
    return (index == 0) | (index == devices - 1)


def lane_sum(block):
    return jnp.sum(block.astype(F32), axis=1, keepdims=True)


def on_diagonal(count):
    shape = (count, LANES)
    return lax.broadcasted_iota(jnp.int32, shape, 0) == lax.broadcasted_iota(jnp.int32, shape, 1)


def pack(sums, mass, out_ref):
    count, width = sums.shape
    blocks = width // LANES
    for at in range(blocks):
        block = sums[:, at * LANES : (at + 1) * LANES]
        out_ref[pl.ds(at * count, count), :] = block.astype(BF16)
    spread = jnp.sum(jnp.where(on_diagonal(count), mass, 0.0), axis=0, keepdims=True)
    high = spread.astype(BF16).astype(F32)
    middle = (spread - high).astype(BF16).astype(F32)
    low = spread - high - middle
    row = lax.broadcasted_iota(jnp.int32, (8, LANES), 0)
    terms = jnp.where(row == 0, high, jnp.where(row == 1, middle, jnp.where(row == 2, low, 0.0)))
    out_ref[pl.ds(blocks * count, 8), :] = terms.astype(BF16)


def unpack(packed_ref, count, width):
    blocks = width // LANES
    sums = jnp.concatenate(
        [packed_ref[pl.ds(at * count, count), :].astype(F32) for at in range(blocks)], axis=1
    )
    terms = packed_ref[pl.ds(blocks * count, 8), :].astype(F32)
    total = jnp.sum(terms, axis=0, keepdims=True)
    return sums, jnp.sum(jnp.where(on_diagonal(count), total, 0.0), axis=1, keepdims=True)


def pool_kernel(first, ends, devices, *refs):
    @pl.when(at_end(devices) == ends)
    def _():
        pool_body(first, ends, *refs)


def pool_body(first, ends, meta_ref, tokens_ref, edge_ref, *refs):
    if first:
        (x_ref, recv_ref, y_ref, _), refs = refs[:4], refs[4:]
        count, width = y_ref.shape
    else:
        (old_ref, old_mass_ref, recv_ref, _), refs = refs[:4], refs[4:]
        count, width = old_ref.shape[0] // 2, old_ref.shape[1]
    sums, masses, *send_out, centroids = refs
    rows = tokens_ref.shape[0]
    reach = edge_ref.shape[0]
    scale = math.log2(math.e) / math.sqrt(width)
    x_rows, y_rows = pl.ds(0, count), pl.ds(count, count)

    occupied = meta_ref[pl.ds(OCCUPIED, 1), :] != 0
    if first:
        joined = x_ref[...] + recv_ref[...]
        centroids[x_rows, :] = jnp.where(occupied, joined, jnp.zeros_like(joined))
        centroids[y_rows, :] = y_ref[...]
    else:
        other, other_mass = unpack(recv_ref, count, width)
        mass = lane_sum(old_mass_ref[x_rows, :]) + other_mass
        joined = (old_ref[x_rows, :] + other) * (1.0 / mass)
        centroids[x_rows, :] = jnp.where(occupied, joined, 0.0).astype(BF16)
        mass = lane_sum(old_mass_ref[y_rows, :])
        centroids[y_rows, :] = (old_ref[y_rows, :] * (1.0 / mass)).astype(BF16)

    tiles = [(tokens_ref, i * TILE) for i in range(rows // TILE)]
    tiles += [(edge_ref, i * TILE) for i in range(reach // TILE)]

    def scores_of(tile):
        ref, row = tile
        return lax.dot_general(
            centroids[...],
            ref[pl.ds(row, TILE), :],
            (((1,), (1,)), ((), ())),
            preferred_element_type=F32,
        )

    def weights_of(tile, scores):
        ref, row = tile
        place = row + lax.broadcasted_iota(jnp.int32, (1, TILE), 1)
        if ref is edge_ref:
            place = place + meta_ref[pl.ds(EDGE, 1), :TILE]
        bound = [meta_ref[pl.ds(i, 1), :TILE] for i in (X_LOW, X_HIGH, Y_LOW, Y_HIGH)]
        in_x = (place >= bound[0]) & (place < bound[1])
        in_y = (place >= bound[2]) & (place < bound[3])
        mine = jnp.where(in_y, scores[count:], scores[:count])
        top = jnp.max(mine, axis=0, keepdims=True)
        powers = jnp.exp2((mine - top) * scale)
        inverse = 1.0 / jnp.sum(powers, axis=0, keepdims=True)
        return jnp.concatenate(
            [powers * jnp.where(in_x, inverse, 0.0), powers * jnp.where(in_y, inverse, 0.0)], axis=0
        )

    scores = scores_of(tiles[0])
    for at, tile in enumerate(tiles):
        upcoming = scores_of(tiles[at + 1]) if at + 1 < len(tiles) else None
        weights = weights_of(tile, scores)
        part = weights[:, :LANES]
        for i in range(1, TILE // LANES):
            part = part + weights[:, i * LANES : (i + 1) * LANES]
        added = jnp.dot(
            weights.astype(BF16), tile[0][pl.ds(tile[1], TILE), :], preferred_element_type=F32
        )
        if at == 0:
            masses[...] = part
            sums[...] = added
        else:
            masses[...] += part
            sums[...] += added
        scores = upcoming

    if ends:
        return
    (send_out,) = send_out
    pack(sums[x_rows, :], lane_sum(masses[x_rows, :]), send_out)


def norm_kernel(devices, meta_ref, gain_ref, recv_ref, *refs):
    out_ref = refs[-1]
    count, width = out_ref.shape
    x_rows, y_rows = pl.ds(0, count), pl.ds(count, count)

    def finish(centroid):
        spread = jnp.sqrt(jnp.mean(centroid * centroid, axis=-1, keepdims=True) + 1e-06)
        out_ref[...] = (centroid * (1.0 / spread) * gain_ref[...]).astype(BF16)

    @pl.when(at_end(devices))
    def _():
        sums, masses = refs[2:4]
        finish(sums[y_rows, :] * (1.0 / lane_sum(masses[y_rows, :])))

    @pl.when(~at_end(devices))
    def _():
        sums, masses = refs[:2]
        other, other_mass = unpack(recv_ref, count, width)
        mass = lane_sum(masses[x_rows, :]) + other_mass
        joined = (sums[x_rows, :] + other) * (1.0 / mass)
        own = sums[y_rows, :] * (1.0 / lane_sum(masses[y_rows, :]))
        finish(jnp.where(meta_ref[pl.ds(SPLIT, 1), :] != 0, own, joined))


def join_kernel(normed_ref, other_ref, out_ref):
    count = normed_ref.shape[0]
    for half in range(2):

        @pl.when(lax.axis_index("feat") == half)
        def _():
            out_ref[pl.ds(half * count, count), :] = normed_ref[...]
            out_ref[pl.ds((1 - half) * count, count), :] = other_ref[...]


def on_device(tokens, shot_starts, seed_offsets, norm_gain, proj_weight):
    rows, width = tokens.shape
    count = seed_offsets.shape[1]
    reach = 3 * rows // 8
    devices = lax.axis_size(AXES)
    across = [(i, i + 1) for i in range(1, devices - 1, 2)]
    across += [(target, source) for source, target in across]
    across += [(0, devices - 1), (devices - 1, 0)]
    pair = [(0, 1), (1, 0)]

    def shape(*dims, dtype=BF16):
        return jax.ShapeDtypeStruct(dims, dtype)

    def in_hbm(array):
        return pltpu.with_memory_space_constraint(array, pltpu.HBM)

    far_tokens = in_hbm(tokens)
    tail, near, choose, share, meta, edge = pl.pallas_call(
        seed_kernel,
        out_shape=(
            shape(count, width),
            shape(8 * count, width),
            shape(count, 8 * count),
            shape(2, width),
            shape(8, width, dtype=jnp.int32),
            shape(reach, width),
        ),
        in_specs=[HBM_SPEC] * 3,
        out_specs=[VMEM_SPEC] * 6,
        scratch_shapes=[
            pltpu.SMEM(shot_starts.shape, jnp.int32),
            pltpu.SMEM(seed_offsets.shape, jnp.int32),
            pltpu.VMEM(seed_offsets.shape, jnp.int32),
            pltpu.VMEM((8 * count, width), BF16),
            pltpu.SemaphoreType.DMA((3,)),
            pltpu.SemaphoreType.DMA((2,)),
            pltpu.SemaphoreType.DMA(()),
        ],
        compiler_params=pltpu.CompilerParams(vmem_limit_bytes=16 << 20),
        name="seeds",
    )(in_hbm(shot_starts), in_hbm(seed_offsets), far_tokens)
    given = lax.ppermute(tail, "feat", pair)
    first, own, edge = pl.pallas_call(
        own_kernel,
        out_shape=(shape(count, width), shape(count, width), shape(reach, width)),
        in_specs=[HBM_SPEC] + [VMEM_SPEC] * 5,
        out_specs=[VMEM_SPEC] * 3,
        scratch_shapes=[pltpu.SemaphoreType.DMA(())],
        input_output_aliases={1: 2},
        compiler_params=pltpu.CompilerParams(vmem_limit_bytes=8 << 20),
        cost_estimate=pl.CostEstimate(
            flops=16 * count * count * width, bytes_accessed=24 * count * width, transcendentals=0
        ),
        name="own",
    )(far_tokens, edge, near, choose, tail, meta)

    def fetch(kernel, size, after, name):
        return pl.pallas_call(
            kernel,
            out_shape=shape(size, width),
            in_specs=[HBM_SPEC, VMEM_SPEC],
            out_specs=VMEM_SPEC,
            scratch_shapes=[pltpu.SemaphoreType.DMA((4,))],
            compiler_params=pltpu.CompilerParams(vmem_limit_bytes=16 << 20),
            name=name,
        )(far_tokens, after)

    edge, given, first = lax.optimization_barrier((edge, given, first))
    edge = lax.ppermute(edge, "feat", pair)
    x = first + given * share[:1]
    y = own + given * share[1:]
    received = lax.ppermute(x, AXES, across)
    near_tokens = fetch(load_kernel, rows, x, "load")

    def pool(first, ends, *state):
        outs = (shape(2 * count, width, dtype=F32), shape(2 * count, LANES, dtype=F32))
        outs += () if ends else (shape(count * width // LANES + 8, LANES),)
        return pl.pallas_call(
            functools.partial(pool_kernel, first, ends, devices),
            out_shape=outs,
            in_specs=[VMEM_SPEC] * 7,
            out_specs=[VMEM_SPEC] * len(outs),
            scratch_shapes=[pltpu.VMEM((2 * count, width), BF16)],
            compiler_params=pltpu.CompilerParams(vmem_limit_bytes=16 << 20),
            name="ends" if ends else "pool",
        )(meta, near_tokens, edge, *state)

    sums, masses, send = pool(True, False, x, received, y, y)
    start = received
    received = lax.ppermute(send, AXES, across)
    end_sums, end_masses = pool(True, True, x, start, y, masses)
    for _ in range(ITERS - 1):
        before = received
        sums, masses, send = pool(False, False, sums, masses, before, end_masses)
        received = lax.ppermute(send, AXES, across)
        end_sums, end_masses = pool(False, True, end_sums, end_masses, before, masses)
    normed = pl.pallas_call(
        functools.partial(norm_kernel, devices),
        out_shape=shape(count, width),
        in_specs=[VMEM_SPEC] * 7,
        out_specs=VMEM_SPEC,
        compiler_params=pltpu.CompilerParams(vmem_limit_bytes=8 << 20),
        name="norm",
    )(meta, norm_gain[None, :], received, sums, masses, end_sums, end_masses)
    both = pl.pallas_call(
        join_kernel,
        out_shape=shape(2 * count, width),
        in_specs=[VMEM_SPEC] * 2,
        out_specs=VMEM_SPEC,
        compiler_params=pltpu.CompilerParams(vmem_limit_bytes=8 << 20),
        name="join",
    )(normed, lax.ppermute(normed, "feat", pair))
    return jnp.dot(both, proj_weight, preferred_element_type=F32).astype(BF16)


def solution(mesh):
    in_specs = (P(AXES, None), P(), P(), P(), P(None, "feat"))
    out_specs = P("seq", "feat")
    return jax.shard_map(
        on_device, mesh=mesh, in_specs=in_specs, out_specs=out_specs, check_vma=False
    )
```

```python
import functools
import math

import jax
import jax.numpy as jnp
from jax import lax
from jax.experimental import pallas as pl
from jax.experimental.pallas import tpu as pltpu
from jax.sharding import PartitionSpec as P

ITERS = 3
AXES = ("seq", "feat")
LANES = 128
TILE = 512
LATE = TILE // 2
F32 = jnp.float32
BF16 = jnp.bfloat16
VMEM_SPEC = pl.BlockSpec(memory_space=pltpu.VMEM)
HBM_SPEC = pl.BlockSpec(memory_space=pltpu.HBM)
X_LOW, X_HIGH, Y_LOW, Y_HIGH, EDGE, SPLIT, OCCUPIED, UNUSED = range(8)


def start_of(starts_ref, shot, shots, total):
    first = starts_ref[jnp.minimum(shot, shots - 1)]
    return jnp.where(shot >= shots, total, first)


def column_of(row):
    n = row.shape[1]
    diagonal = lax.broadcasted_iota(jnp.int32, (n, n), 0) == lax.broadcasted_iota(
        jnp.int32, (n, n), 1
    )
    spread = jnp.where(diagonal, jnp.broadcast_to(row, (n, n)), 0)
    return jnp.sum(spread, axis=1, keepdims=True)


def seed_kernel(
    starts_hbm,
    seeds_hbm,
    tokens_ref,
    tail_ref,
    near_ref,
    choose_ref,
    share_ref,
    meta_ref,
    edge_ref,
    starts_ref,
    seeds_ref,
    seed_rows_ref,
    picked,
    index_sems,
    pick_sems,
    edge_sem,
):
    rows, width = tokens_ref.shape
    reach = edge_ref.shape[0]
    shots, count = seeds_ref.shape
    total = shots * rows
    index = lax.axis_index(AXES)
    second = index % 2 == 1
    base = index * rows
    indices = [
        pltpu.make_async_copy(starts_hbm, starts_ref, index_sems.at[0]),
        pltpu.make_async_copy(seeds_hbm, seeds_ref, index_sems.at[1]),
        pltpu.make_async_copy(seeds_hbm, seed_rows_ref, index_sems.at[2]),
    ]
    for copy in indices:
        copy.start()
    size = reach - LATE
    strip_low = pl.multiple_of(jnp.where(second, 0, rows - reach), 8)
    strip = pltpu.make_async_copy(
        tokens_ref.at[pl.ds(strip_low, size), :], edge_ref.at[pl.ds(0, size), :], edge_sem
    )
    strip.start()
    for copy in indices:
        copy.wait()
    following = jnp.minimum(index + 1, shots - 1)
    here = start_of(starts_ref, index, shots, total)
    after = start_of(starts_ref, index + 1, shots, total)

    sides = ((following, after, picked, pick_sems.at[0]), (index, here, near_ref, pick_sems.at[1]))
    for shot, begin, rows_ref, sem in sides:

        def fetch(k, carry, shot=shot, begin=begin, rows_ref=rows_ref, sem=sem):
            place = begin + seeds_ref[shot, k] - base
            slot = pl.multiple_of(k * 8, 8)
            here_too = (place >= 0) & (place < rows)
            group = pl.multiple_of(jnp.where(here_too, (place // 8) * 8, slot), 8)
            pltpu.make_async_copy(
                tokens_ref.at[pl.ds(group, 8), :], rows_ref.at[pl.ds(slot, 8), :], sem
            ).start()
            return carry

        lax.fori_loop(0, count, fetch, 0, unroll=32)

    low = jnp.where(second, here - base, 0)
    high = jnp.where(second, rows, after - base)
    cut = jnp.where(second, after - base, here - base)
    split = jnp.where(second, after <= base + rows, here > base) | (index == 0)
    x_low = jnp.where(split & second, cut, low)
    x_high = jnp.where(split & ~second, cut, high)
    y_low = jnp.where(split, jnp.where(second, low, cut), high)
    y_high = jnp.where(split, jnp.where(second, cut, high), high)
    table = {
        X_LOW: x_low,
        X_HIGH: x_high,
        Y_LOW: y_low,
        Y_HIGH: y_high,
        EDGE: jnp.where(second, -reach, rows),
        SPLIT: split.astype(jnp.int32),
        OCCUPIED: (x_low < x_high).astype(jnp.int32),
        UNUSED: 0,
    }
    for row, value in table.items():
        meta_ref[pl.ds(row, 1), :] = jnp.full((1, width), value, jnp.int32)
    lends = jnp.where(second, 1.0, 0.0)
    row = lax.broadcasted_iota(jnp.int32, share_ref.shape, 0)
    share_ref[...] = jnp.where(row == 0, jnp.where(split, 0.0, lends), lends).astype(BF16)

    choices = []
    for shot, begin, _, _ in sides:
        place = column_of(seed_rows_ref[pl.ds(shot, 1), :]) + (begin - base)
        valid = (place >= 0) & (place < rows)
        target = lax.broadcasted_iota(jnp.int32, (count, 1), 0) * 8 + place % 8
        lane = lax.broadcasted_iota(jnp.int32, (count, 8 * count), 1)
        choices.append(jnp.where(valid & (lane == target), 1.0, 0.0).astype(BF16))
    choose_ref[...] = choices[1]
    waits = [
        pltpu.make_async_copy(tokens_ref.at[pl.ds(0, 8 * count), :], rows_ref, sem)
        for _, _, rows_ref, sem in sides
    ]
    waits[0].wait()
    tail_ref[...] = jnp.dot(choices[0], picked[...], preferred_element_type=F32).astype(BF16)
    waits[1].wait()
    strip.wait()


def own_kernel(
    tokens_ref,
    edge_in_ref,
    near_ref,
    choose_ref,
    tail_ref,
    meta_ref,
    first_ref,
    own_ref,
    edge_ref,
    edge_sem,
):
    rows, reach = tokens_ref.shape[0], edge_ref.shape[0]
    begin = jnp.where(lax.axis_index(AXES) % 2 == 1, reach, rows) - LATE
    strip = pltpu.make_async_copy(
        tokens_ref.at[pl.ds(pl.multiple_of(begin, 8), LATE), :],
        edge_ref.at[pl.ds(reach - LATE, LATE), :],
        edge_sem,
    )
    strip.start()
    own = jnp.dot(choose_ref[...], near_ref[...], preferred_element_type=F32)
    tail = tail_ref[...].astype(F32)
    second = lax.axis_index(AXES) % 2 == 1
    split = meta_ref[pl.ds(SPLIT, 1), :] != 0
    first_ref[...] = jnp.where(split, jnp.where(second, tail, 0.0), own).astype(BF16)
    own_ref[...] = own.astype(BF16)
    strip.wait()


def copy_pieces(tokens_ref, low, out_ref, sems):
    pieces = sems.shape[0]
    piece = out_ref.shape[0] // pieces
    copies = [
        pltpu.make_async_copy(
            tokens_ref.at[pl.ds(pl.multiple_of(low + i * piece, 8), piece), :],
            out_ref.at[pl.ds(i * piece, piece), :],
            sems.at[i],
        )
        for i in range(pieces)
    ]
    for copy in copies:
        copy.start()
    for copy in copies:
        copy.wait()


def load_kernel(tokens_ref, order_ref, out_ref, sems):
    copy_pieces(tokens_ref, 0, out_ref, sems)


def at_end(devices):
    index = lax.axis_index(AXES)
    return (index == 0) | (index == devices - 1)


def lane_sum(block):
    return jnp.sum(block.astype(F32), axis=1, keepdims=True)


def on_diagonal(count):
    shape = (count, LANES)
    return lax.broadcasted_iota(jnp.int32, shape, 0) == lax.broadcasted_iota(jnp.int32, shape, 1)


def pack(sums, mass, out_ref):
    count, width = sums.shape
    blocks = width // LANES
    for at in range(blocks):
        block = sums[:, at * LANES : (at + 1) * LANES]
        out_ref[pl.ds(at * count, count), :] = block.astype(BF16)
    spread = jnp.sum(jnp.where(on_diagonal(count), mass, 0.0), axis=0, keepdims=True)
    high = spread.astype(BF16).astype(F32)
    middle = (spread - high).astype(BF16).astype(F32)
    low = spread - high - middle
    row = lax.broadcasted_iota(jnp.int32, (8, LANES), 0)
    terms = jnp.where(row == 0, high, jnp.where(row == 1, middle, jnp.where(row == 2, low, 0.0)))
    out_ref[pl.ds(blocks * count, 8), :] = terms.astype(BF16)


def unpack(packed_ref, count, width):
    blocks = width // LANES
    sums = jnp.concatenate(
        [packed_ref[pl.ds(at * count, count), :].astype(F32) for at in range(blocks)], axis=1
    )
    terms = packed_ref[pl.ds(blocks * count, 8), :].astype(F32)
    total = jnp.sum(terms, axis=0, keepdims=True)
    return sums, jnp.sum(jnp.where(on_diagonal(count), total, 0.0), axis=1, keepdims=True)


def pool_kernel(first, ends, devices, *refs):
    @pl.when(at_end(devices) == ends)
    def _():
        pool_body(first, ends, *refs)


def pool_body(first, ends, meta_ref, tokens_ref, edge_ref, *refs):
    if first:
        (x_ref, recv_ref, y_ref, _), refs = refs[:4], refs[4:]
        count, width = y_ref.shape
    else:
        (old_ref, old_mass_ref, recv_ref, _), refs = refs[:4], refs[4:]
        count, width = old_ref.shape[0] // 2, old_ref.shape[1]
    sums, masses, *send_out, centroids = refs
    rows = tokens_ref.shape[0]
    reach = edge_ref.shape[0]
    scale = math.log2(math.e) / math.sqrt(width)
    x_rows, y_rows = pl.ds(0, count), pl.ds(count, count)

    occupied = meta_ref[pl.ds(OCCUPIED, 1), :] != 0
    if first:
        joined = x_ref[...] + recv_ref[...]
        centroids[x_rows, :] = jnp.where(occupied, joined, jnp.zeros_like(joined))
        centroids[y_rows, :] = y_ref[...]
    else:
        other, other_mass = unpack(recv_ref, count, width)
        mass = lane_sum(old_mass_ref[x_rows, :]) + other_mass
        joined = (old_ref[x_rows, :] + other) * (1.0 / mass)
        centroids[x_rows, :] = jnp.where(occupied, joined, 0.0).astype(BF16)
        mass = lane_sum(old_mass_ref[y_rows, :])
        centroids[y_rows, :] = (old_ref[y_rows, :] * (1.0 / mass)).astype(BF16)

    tiles = [(tokens_ref, i * TILE) for i in range(rows // TILE)]
    tiles += [(edge_ref, i * TILE) for i in range(reach // TILE)]

    def scores_of(tile):
        ref, row = tile
        return lax.dot_general(
            centroids[...],
            ref[pl.ds(row, TILE), :],
            (((1,), (1,)), ((), ())),
            preferred_element_type=F32,
        )

    def weights_of(tile, scores):
        ref, row = tile
        place = row + lax.broadcasted_iota(jnp.int32, (1, TILE), 1)
        if ref is edge_ref:
            place = place + meta_ref[pl.ds(EDGE, 1), :TILE]
        bound = [meta_ref[pl.ds(i, 1), :TILE] for i in (X_LOW, X_HIGH, Y_LOW, Y_HIGH)]
        in_x = (place >= bound[0]) & (place < bound[1])
        in_y = (place >= bound[2]) & (place < bound[3])
        mine = jnp.where(in_y, scores[count:], scores[:count])
        top = jnp.max(mine, axis=0, keepdims=True)
        powers = jnp.exp2((mine - top) * scale)
        inverse = 1.0 / jnp.sum(powers, axis=0, keepdims=True)
        return jnp.concatenate(
            [powers * jnp.where(in_x, inverse, 0.0), powers * jnp.where(in_y, inverse, 0.0)], axis=0
        )

    scores = scores_of(tiles[0])
    for at, tile in enumerate(tiles):
        upcoming = scores_of(tiles[at + 1]) if at + 1 < len(tiles) else None
        weights = weights_of(tile, scores)
        part = weights[:, :LANES]
        for i in range(1, TILE // LANES):
            part = part + weights[:, i * LANES : (i + 1) * LANES]
        added = jnp.dot(
            weights.astype(BF16), tile[0][pl.ds(tile[1], TILE), :], preferred_element_type=F32
        )
        if at == 0:
            masses[...] = part
            sums[...] = added
        else:
            masses[...] += part
            sums[...] += added
        scores = upcoming

    if ends:
        return
    (send_out,) = send_out
    pack(sums[x_rows, :], lane_sum(masses[x_rows, :]), send_out)


def norm_kernel(devices, meta_ref, gain_ref, recv_ref, *refs):
    out_ref = refs[-1]
    count, width = out_ref.shape
    x_rows, y_rows = pl.ds(0, count), pl.ds(count, count)

    def finish(centroid):
        spread = jnp.sqrt(jnp.mean(centroid * centroid, axis=-1, keepdims=True) + 1e-06)
        out_ref[...] = (centroid * (1.0 / spread) * gain_ref[...]).astype(BF16)

    @pl.when(at_end(devices))
    def _():
        sums, masses = refs[2:4]
        finish(sums[y_rows, :] * (1.0 / lane_sum(masses[y_rows, :])))

    @pl.when(~at_end(devices))
    def _():
        sums, masses = refs[:2]
        other, other_mass = unpack(recv_ref, count, width)
        mass = lane_sum(masses[x_rows, :]) + other_mass
        joined = (sums[x_rows, :] + other) * (1.0 / mass)
        own = sums[y_rows, :] * (1.0 / lane_sum(masses[y_rows, :]))
        finish(jnp.where(meta_ref[pl.ds(SPLIT, 1), :] != 0, own, joined))


def join_kernel(normed_ref, other_ref, out_ref):
    count = normed_ref.shape[0]
    for half in range(2):

        @pl.when(lax.axis_index("feat") == half)
        def _():
            out_ref[pl.ds(half * count, count), :] = normed_ref[...]
            out_ref[pl.ds((1 - half) * count, count), :] = other_ref[...]


def on_device(tokens, shot_starts, seed_offsets, norm_gain, proj_weight):
    rows, width = tokens.shape
    count = seed_offsets.shape[1]
    reach = 3 * rows // 8
    devices = lax.axis_size(AXES)
    across = [(i, i + 1) for i in range(1, devices - 1, 2)]
    across += [(target, source) for source, target in across]
    across += [(0, devices - 1), (devices - 1, 0)]
    pair = [(0, 1), (1, 0)]

    def shape(*dims, dtype=BF16):
        return jax.ShapeDtypeStruct(dims, dtype)

    def in_hbm(array):
        return pltpu.with_memory_space_constraint(array, pltpu.HBM)

    far_tokens = in_hbm(tokens)
    tail, near, choose, share, meta, edge = pl.pallas_call(
        seed_kernel,
        out_shape=(
            shape(count, width),
            shape(8 * count, width),
            shape(count, 8 * count),
            shape(2, width),
            shape(8, width, dtype=jnp.int32),
            shape(reach, width),
        ),
        in_specs=[HBM_SPEC] * 3,
        out_specs=[VMEM_SPEC] * 6,
        scratch_shapes=[
            pltpu.SMEM(shot_starts.shape, jnp.int32),
            pltpu.SMEM(seed_offsets.shape, jnp.int32),
            pltpu.VMEM(seed_offsets.shape, jnp.int32),
            pltpu.VMEM((8 * count, width), BF16),
            pltpu.SemaphoreType.DMA((3,)),
            pltpu.SemaphoreType.DMA((2,)),
            pltpu.SemaphoreType.DMA(()),
        ],
        compiler_params=pltpu.CompilerParams(vmem_limit_bytes=16 << 20),
        name="seeds",
    )(in_hbm(shot_starts), in_hbm(seed_offsets), far_tokens)
    given = lax.ppermute(tail, "feat", pair)
    first, own, edge = pl.pallas_call(
        own_kernel,
        out_shape=(shape(count, width), shape(count, width), shape(reach, width)),
        in_specs=[HBM_SPEC] + [VMEM_SPEC] * 5,
        out_specs=[VMEM_SPEC] * 3,
        scratch_shapes=[pltpu.SemaphoreType.DMA(())],
        input_output_aliases={1: 2},
        compiler_params=pltpu.CompilerParams(vmem_limit_bytes=8 << 20),
        cost_estimate=pl.CostEstimate(
            flops=16 * count * count * width, bytes_accessed=24 * count * width, transcendentals=0
        ),
        name="own",
    )(far_tokens, edge, near, choose, tail, meta)

    def fetch(kernel, size, after, name):
        return pl.pallas_call(
            kernel,
            out_shape=shape(size, width),
            in_specs=[HBM_SPEC, VMEM_SPEC],
            out_specs=VMEM_SPEC,
            scratch_shapes=[pltpu.SemaphoreType.DMA((4,))],
            compiler_params=pltpu.CompilerParams(vmem_limit_bytes=16 << 20),
            name=name,
        )(far_tokens, after)

    edge, given, first = lax.optimization_barrier((edge, given, first))
    edge = lax.ppermute(edge, "feat", pair)
    x = first + given * share[:1]
    y = own + given * share[1:]
    received = lax.ppermute(x, AXES, across)
    near_tokens = fetch(load_kernel, rows, x, "load")

    def pool(first, ends, *state):
        outs = (shape(2 * count, width, dtype=F32), shape(2 * count, LANES, dtype=F32))
        outs += () if ends else (shape(count * width // LANES + 8, LANES),)
        return pl.pallas_call(
            functools.partial(pool_kernel, first, ends, devices),
            out_shape=outs,
            in_specs=[VMEM_SPEC] * 7,
            out_specs=[VMEM_SPEC] * len(outs),
            scratch_shapes=[pltpu.VMEM((2 * count, width), BF16)],
            compiler_params=pltpu.CompilerParams(vmem_limit_bytes=16 << 20),
            name="ends" if ends else "pool",
        )(meta, near_tokens, edge, *state)

    sums, masses, send = pool(True, False, x, received, y, y)
    start = received
    received = lax.ppermute(send, AXES, across)
    end_sums, end_masses = pool(True, True, x, start, y, masses)
    for _ in range(ITERS - 1):
        before = received
        sums, masses, send = pool(False, False, sums, masses, before, end_masses)
        received = lax.ppermute(send, AXES, across)
        end_sums, end_masses = pool(False, True, end_sums, end_masses, before, masses)
    normed = pl.pallas_call(
        functools.partial(norm_kernel, devices),
        out_shape=shape(count, width),
        in_specs=[VMEM_SPEC] * 7,
        out_specs=VMEM_SPEC,
        compiler_params=pltpu.CompilerParams(vmem_limit_bytes=8 << 20),
        name="norm",
    )(meta, norm_gain[None, :], received, sums, masses, end_sums, end_masses)
    both = pl.pallas_call(
        join_kernel,
        out_shape=shape(2 * count, width),
        in_specs=[VMEM_SPEC] * 2,
        out_specs=VMEM_SPEC,
        compiler_params=pltpu.CompilerParams(vmem_limit_bytes=8 << 20),
        name="join",
    )(normed, lax.ppermute(normed, "feat", pair))
    return jnp.dot(both, proj_weight, preferred_element_type=F32).astype(BF16)


def solution(mesh):
    in_specs = (P(AXES, None), P(), P(), P(), P(None, "feat"))
    out_specs = P("seq", "feat")
    return jax.shard_map(
        on_device, mesh=mesh, in_specs=in_specs, out_specs=out_specs, check_vma=False
    )
```
